32 devices in a mesh: wide: 8 (over z, x), narrow: 4 (over y, core).
Axes of the slice: x: 2, y: 2, z: 4, core: 2. Of those that a mesh axis runs over, the one named last changes fastest.
Arguments:
- star_pos: float32 [3, 2048], P(None, ('wide', 'narrow')), may hold values from -6 to 6
- star_vel: float32 [3, 2048], P(None, ('wide', 'narrow')), may hold values from -6 to 6
- star_mass: float32 [2048], P(('wide', 'narrow')), may hold values from 0.00048828125 to 0.0048828125
- star_acc: float32 [3, 2048], P(None, ('wide', 'narrow')), may hold values from -6 to 6
- star_jerk: float32 [3, 2048], P(None, ('wide', 'narrow')), may hold values from -120 to 120
- gal_pos: float32 [3, 16384], P(None, ('wide', 'narrow')), may hold values from -6 to 6
- gal_vel: float32 [3, 16384], P(None, ('wide', 'narrow')), may hold values from -6 to 6
- gal_mass: float32 [16384], P(('wide', 'narrow')), may hold values from 0.0009765625 to 0.009765625
- group_of: int32 [16384], P(('wide', 'narrow')), may hold values from 0 to 31, as said below
- let_send: int32 [32, 8, 1], P(('wide', 'narrow')), may hold values from -1 to 3, as said below
- star_leaf: int32 [128, 8], P(('wide', 'narrow')), may hold values from 0 to 7, as said below
Outputs:
- gal_vel_new: float32 [3, 16384], P(None, ('wide', 'narrow'))
- star_pos_new: float32 [3, 2048], P(None, ('wide', 'narrow'))
- star_vel_new: float32 [3, 2048], P(None, ('wide', 'narrow'))
The draws below stay inside these ranges and needn't reach their ends.
Inputs may be any that keep to these rules, and one draw needn't show every extreme that they name: `group_of`: within each leaf of 128 bodies every group number is held by exactly 4 bodies. `let_send`: entry [k, j, s] is a local leaf of device k sent to the device of wide index j with k's narrow index, or -1 for an empty slot; the leaves of one row are distinct; a device lists nothing for its own wide index; for some wide index j, every device whose wide index is not j lists a leaf for j, in every draw. `star_leaf`: the star blocks listed for one leaf are distinct.
All inputs are finite; a program needn't handle non-finite values.
Results may differ from the reference program's by a relative error of at most 0.0003.
Values sent between devices are 32-bit elements; how exact they have to be, the bound alone decides.
A program may use at most 64 MiB of HBM per device.

```python
import math
import jax
import jax.numpy as jnp
from jax import lax

LEAF = 128
GROUPS = 32
L_DEV = 4
S_DEV = 64
SLOTS = 1
KICK_BLOCKS = 8
NS = 2048
NLEAF = 128
NB = 16384
N_WIDE = 8
N_NARROW = 4
DEVICES = 32


def draw_group_of(key, part):
    keys = jax.random.split(key, NLEAF)
    base = jnp.arange(LEAF, dtype=jnp.int32) % GROUPS
    rows = jax.vmap(lambda row_key: jax.random.permutation(row_key, base))(keys)
    return rows.reshape(NB).astype(jnp.int32)


def draw_let_send(key, part):
    key_perm, key_busy, key_special, key_roll = jax.random.split(jax.random.fold_in(key, 11), 4)
    keys = jax.random.split(key_perm, DEVICES * N_WIDE)
    base = jnp.arange(L_DEV, dtype=jnp.int32)
    picks = jax.vmap(lambda row_key: jax.random.permutation(row_key, base)[:SLOTS])(keys)
    picks = picks.reshape(DEVICES, N_WIDE, SLOTS)
    busy = jax.random.randint(key_busy, (N_WIDE,), 1, 5)
    special = jax.random.randint(key_special, (), 0, N_WIDE)
    busy = jnp.where(jnp.arange(N_WIDE) == special, 4, busy)
    roll = jax.random.randint(key_roll, (DEVICES, N_WIDE, SLOTS), 0, 4)
    live = roll < busy[None, :, None]
    own = (jnp.arange(DEVICES) // N_NARROW)[:, None] == jnp.arange(N_WIDE)[None, :]
    live = jnp.logical_and(live, jnp.logical_not(own)[:, :, None])
    return jnp.where(live, picks, -1).astype(jnp.int32)


def draw_star_leaf(key, part):
    keys = jax.random.split(jax.random.fold_in(key, 23), NLEAF)
    base = jnp.arange(N_WIDE, dtype=jnp.int32)
    rows = jax.vmap(lambda row_key: jax.random.permutation(row_key, base)[:KICK_BLOCKS])(keys)
    return rows.astype(jnp.int32)


def shard_levels(stream_key, shape, cuts, least, top_value):
    level, own = 1.0, jax.random.fold_in(stream_key, 6)
    for position, blocks in cuts:
        steps = jnp.exp(jax.random.uniform(jax.random.fold_in(own, position), (blocks,), jnp.float32, least / len(cuts), top_value / len(cuts)))
        level = level * jnp.repeat(steps, shape[position] // blocks).reshape([-1 if axis == position else 1 for axis in range(len(shape))])
    return level


def bell_draw(rng, shape, width, bound, cuts=(), kind=jnp.bfloat16):
    loudness = shard_levels(rng, shape, cuts, -0.22, 0.18) if cuts else 1.0
    entries = jax.random.normal(rng, shape, jnp.float32) * width * loudness
    return jnp.minimum(jnp.maximum(entries, -bound), bound).astype(kind)


def setup_inputs(seed: int = 0) -> dict:
    streams_of = jax.random.split(jax.random.key(seed), 12)
    star_pos = bell_draw(streams_of[0], (3, NS), 1.0, 6.0, ((1, 32),), jnp.float32)
    star_vel = bell_draw(streams_of[1], (3, NS), 1.0, 6.0, ((1, 32),), jnp.float32)
    star_mass = jnp.clip(jnp.exp(math.log(0.0048828125) - 2.3025851 * jax.random.uniform(streams_of[2], (NS,), jnp.float32) ** shard_levels(streams_of[2], (NS,), ((0, 32),), -0.2, 0.2)), 0.00048828125, 0.0048828125)
    star_acc = bell_draw(streams_of[3], (3, NS), 1.0, 6.0, ((1, 32),), jnp.float32)
    star_jerk = bell_draw(streams_of[4], (3, NS), 20.0, 120.0, ((1, 32),), jnp.float32)
    gal_pos = bell_draw(streams_of[5], (3, NB), 1.0, 6.0, ((1, 32),), jnp.float32)
    gal_vel = bell_draw(streams_of[6], (3, NB), 1.0, 6.0, ((1, 32),), jnp.float32)
    gal_mass = jnp.clip(jnp.exp(math.log(0.009765625) - 2.3025851 * jax.random.uniform(streams_of[7], (NB,), jnp.float32) ** shard_levels(streams_of[7], (NB,), ((0, 32),), -0.2, 0.2)), 0.0009765625, 0.009765625)
    group_of = draw_group_of(jax.random.fold_in(streams_of[11], 71), 0)
    let_send = draw_let_send(jax.random.fold_in(streams_of[11], 71), 0)
    star_leaf = draw_star_leaf(jax.random.fold_in(streams_of[11], 71), 0)
    return {"star_pos": star_pos, "star_vel": star_vel, "star_mass": star_mass, "star_acc": star_acc, "star_jerk": star_jerk, "gal_pos": gal_pos, "gal_vel": gal_vel, "gal_mass": gal_mass, "group_of": group_of, "let_send": let_send, "star_leaf": star_leaf}


time_step = 0.25
soften_sq = 0.05

def by_blocks(kernel, arrays):
    total_rows = arrays[0].shape[1]
    block_rows = math.gcd(total_rows, 512)
    nblocks = total_rows // block_rows
    split = tuple((member.reshape(member.shape[0], nblocks, block_rows).transpose(1, 0, 2) for member in arrays))
    result = lax.map(kernel, split)
    return jax.tree.map(lambda piece: piece.transpose(1, 0, 2).reshape(piece.shape[1], total_rows), result)

def attract(tgt_pos, src_pos, src_mass):

    def kernel(pieces):
        here_pos = pieces[0]
        offset = src_pos[:, None, :] - here_pos[:, :, None]
        dist_sq = lax.optimization_barrier(jnp.sum(offset * offset, axis=0)) + soften_sq
        inverse = lax.rsqrt(dist_sq)
        weight = src_mass[None, :] * inverse * inverse * inverse
        return lax.optimization_barrier(jnp.sum(offset * weight[None], axis=2))
    return by_blocks(kernel, (tgt_pos,))

def hermite(tgt_pos, tgt_vel, src_pos, src_vel, src_mass):

    def kernel(pieces):
        here_pos, here_vel = pieces
        offset = src_pos[:, None, :] - here_pos[:, :, None]
        rel_vel = src_vel[:, None, :] - here_vel[:, :, None]
        dist_sq = lax.optimization_barrier(jnp.sum(offset * offset, axis=0)) + soften_sq
        inverse = lax.rsqrt(dist_sq)
        weight = src_mass[None, :] * inverse * inverse * inverse
        approach = 3.0 * lax.optimization_barrier(jnp.sum(offset * rel_vel, axis=0)) / dist_sq
        accel_sum = lax.optimization_barrier(jnp.sum(offset * weight[None], axis=2))
        jerk_sum = lax.optimization_barrier(jnp.sum((rel_vel - offset * approach[None]) * weight[None], axis=2))
        return (accel_sum, jerk_sum)
    return by_blocks(kernel, (tgt_pos, tgt_vel))

def reference(star_pos, star_vel, star_mass, star_acc, star_jerk, gal_pos, gal_vel, gal_mass, group_of, let_send, star_leaf):
    step_sq = time_step * time_step
    pred_pos = star_pos + time_step * star_vel + step_sq * 0.5 * star_acc + step_sq * time_step / 6.0 * star_jerk
    pred_vel = star_vel + time_step * star_acc + step_sq * 0.5 * star_jerk
    direct_acc, direct_jerk = hermite(pred_pos, pred_vel, pred_pos, pred_vel, star_mass)
    leaf_of = jnp.arange(NB, dtype=jnp.int32) // LEAF
    segment = leaf_of * GROUPS + group_of
    cell_mass = jax.ops.segment_sum(gal_mass, segment, num_segments=NLEAF * GROUPS)
    cell_mom = jax.vmap(lambda coord: jax.ops.segment_sum(coord * gal_mass, segment, num_segments=NLEAF * GROUPS))(gal_pos)
    cell_pos = cell_mom / cell_mass[None]
    local_size = L_DEV * LEAF
    group_range = jnp.arange(GROUPS, dtype=jnp.int32)
    star_range = jnp.arange(S_DEV, dtype=jnp.int32)

    def per_device(device):
        wide_idx = device // N_NARROW
        narrow_idx = device % N_NARROW
        sources = jnp.arange(N_WIDE, dtype=jnp.int32) * N_NARROW + narrow_idx
        slot_ids = let_send[sources, wide_idx]
        live = (slot_ids >= 0).astype(jnp.float32)
        leaf_idx = sources[:, None] * L_DEV + jnp.maximum(slot_ids, 0)
        cell_idx = (leaf_idx[:, :, None] * GROUPS + group_range[None, None, :]).reshape(-1)
        let_pos = cell_pos[:, cell_idx]
        let_mass = (cell_mass[cell_idx].reshape(N_WIDE, SLOTS, GROUPS) * live[:, :, None]).reshape(-1)
        own_cells = device * (L_DEV * GROUPS) + jnp.arange(L_DEV * GROUPS, dtype=jnp.int32)
        cells_pos = jnp.concatenate([cell_pos[:, own_cells], let_pos], axis=1)
        cells_mass = jnp.concatenate([cell_mass[own_cells], let_mass], axis=0)
        start = (device * local_size).astype(jnp.int32)
        bodies = lax.dynamic_slice_in_dim(gal_pos, start, local_size, 1)
        masses = lax.dynamic_slice_in_dim(gal_mass, start, local_size, 0)
        gal_acc = attract(bodies, bodies, masses) + attract(bodies, let_pos, let_mass)
        blocks = lax.dynamic_slice_in_dim(star_leaf, (device * L_DEV).astype(jnp.int32), L_DEV, 0)
        star_idx = (((blocks * N_NARROW + narrow_idx) * S_DEV)[:, :, None] + star_range[None, None, :]).reshape(L_DEV, KICK_BLOCKS * S_DEV)
        leaf_targets = bodies.reshape(3, L_DEV, LEAF)
        star_term = jax.vmap(lambda target, index: attract(target, pred_pos[:, index], star_mass[index]), in_axes=(1, 0), out_axes=1)(leaf_targets, star_idx)
        gal_acc = gal_acc + star_term.reshape(3, local_size)
        own_stars = lax.dynamic_slice_in_dim(pred_pos, (device * S_DEV).astype(jnp.int32), S_DEV, 1)
        star_cell = attract(own_stars, cells_pos, cells_mass)
        return (gal_acc, star_cell)
    gal_acc, cell_acc = lax.map(per_device, jnp.arange(DEVICES, dtype=jnp.int32))
    gal_acc = gal_acc.transpose(1, 0, 2).reshape(3, NB)
    cell_acc = cell_acc.transpose(1, 0, 2).reshape(3, NS)
    gal_vel_new = gal_vel + time_step * gal_acc
    new_acc = direct_acc + cell_acc
    star_vel_new = star_vel + time_step * 0.5 * (star_acc + new_acc) + step_sq / 12.0 * (star_jerk - direct_jerk)
    star_pos_new = star_pos + time_step * 0.5 * (star_vel + star_vel_new) + step_sq / 12.0 * (star_acc - new_acc)
    return (gal_vel_new, star_pos_new, star_vel_new)
```

```python
import functools

import jax
import jax.numpy as jnp
from jax import lax
from jax.experimental import pallas as pl
from jax.experimental.pallas import tpu as pltpu
from jax.sharding import PartitionSpec as P

GROUPS = 32
LANES = 128
ROWS = 8
BODY_UNROLL = 16
MESH = pl.DeviceIdType.MESH

time_step = 0.25
soften_sq = 0.05


def loop(count, step, init, most=4):
    unroll = next(u for u in range(min(most, count), 0, -1) if count % u == 0)
    return lax.fori_loop(0, count, step, init, unroll=unroll)


def spread(row):
    return jnp.broadcast_to(row, (ROWS, row.shape[1]))


def column(block, index):
    return jnp.broadcast_to(block[:, index : index + 1], (ROWS, LANES))


def pull(source, mass, target, total):
    dx, dy, dz = (s - t for s, t in zip(source, target))
    inverse = lax.rsqrt(dx * dx + dy * dy + dz * dz + soften_sq)
    weight = mass * inverse * inverse * inverse
    return (total[0] + dx * weight, total[1] + dy * weight, total[2] + dz * weight)


def kernel(
    n_wide,
    n_narrow,
    star_pos_hbm,
    star_vel_hbm,
    star_mass_hbm,
    star_acc_hbm,
    star_jerk_hbm,
    gal_pos_hbm,
    gal_vel_hbm,
    gal_mass_hbm,
    group_of_hbm,
    let_send_hbm,
    star_leaf_hbm,
    out,
    star_pos,
    star_vel,
    star_mass,
    star_acc,
    star_jerk,
    gal_pos,
    gal_vel,
    gal_mass,
    group_of,
    let_send,
    star_leaf,
    in_sem,
    states,
    cell_out,
    cell_in,
    cols,
    srow,
    aims,
    body_sum,
    star_sum,
    send_sem,
    near_sem,
    cell_send_sem,
    cell_recv_sem,
    pass_send_sem,
    pass_recv_sem,
    enter_sem,
):
    wide, narrow = lax.axis_index("wide"), lax.axis_index("narrow")
    stars = star_pos.shape[1]
    bodies = gal_pos.shape[1]
    leaves, kicks = star_leaf.shape
    slots = LANES // GROUPS
    step_sq = time_step * time_step
    tiles = bodies // LANES
    every = tuple(range(tiles))
    star_at = bodies
    cell_at = bodies + n_wide * stars

    fetches = [
        pltpu.make_async_copy(source, target, in_sem.at[i])
        for i, (source, target) in enumerate(
            (
                (star_pos_hbm, star_pos),
                (star_vel_hbm, star_vel),
                (star_mass_hbm, star_mass),
                (star_acc_hbm, star_acc),
                (star_jerk_hbm, star_jerk),
                (gal_pos_hbm, gal_pos),
                (gal_vel_hbm, gal_vel),
                (gal_mass_hbm, gal_mass),
                (group_of_hbm, group_of),
                (let_send_hbm, let_send),
                (star_leaf_hbm, star_leaf),
            )
        )
    ]
    for fetch in fetches:
        fetch.start()

    barrier = pltpu.get_barrier_semaphore()
    others = [lax.rem(narrow + m, n_narrow) for m in range(1, n_narrow)]

    def run(first, last, step):
        def body(i, carry):
            step(i)
            return carry

        lax.fori_loop(first, last, body, 0)

    def signal(sem, w, n):
        pl.semaphore_signal(sem, inc=1, device_id=(w, n), device_id_type=MESH)

    def signal_group(sem, w):
        for n in range(n_narrow):
            signal(sem, w, n)

    run(narrow + 1, n_narrow, lambda n: signal(barrier, wide, n))
    run(wide + 1, n_wide, lambda w: signal_group(barrier, w))

    lane = lax.broadcasted_iota(jnp.int32, (1, LANES), 1)
    lane4 = lax.broadcasted_iota(jnp.int32, (4, LANES), 1)
    lane8 = lax.broadcasted_iota(jnp.int32, (ROWS, LANES), 1)
    row8 = lax.broadcasted_iota(jnp.int32, (ROWS, LANES), 0)
    left = lane4 < stars

    for fetch in fetches[:5]:
        fetch.wait()

    spos, svel = star_pos[...], star_vel[...]
    sacc, sjerk = star_acc[...], star_jerk[...]
    pred_pos = (
        spos + time_step * svel + step_sq * 0.5 * sacc + step_sq * time_step / 6.0 * sjerk
    )
    pred_vel = svel + time_step * sacc + step_sq * 0.5 * sjerk
    pos4 = jnp.concatenate([pred_pos, star_mass[...]], axis=0)
    vel4 = jnp.concatenate([pred_vel, jnp.zeros((1, stars), jnp.float32)], axis=0)
    block = jnp.concatenate([pos4, vel4], axis=1)
    block = jnp.where(lax.rem(wide, 2) == 0, block, pltpu.roll(block, stars, 1))
    states[narrow, wide] = block

    smaller = wide * n_narrow + narrow

    @pl.when(smaller > 0)
    def _():
        pl.semaphore_wait(barrier, smaller)

    def send_state(w, n, sends, recvs):
        pltpu.make_async_remote_copy(
            src_ref=states.at[narrow, wide],
            dst_ref=states.at[narrow, wide],
            send_sem=sends,
            recv_sem=recvs.at[wide],
            device_id=(w, n),
            device_id_type=MESH,
        ).start()

    def send_group(w):
        send_state(w, narrow, send_sem, near_sem)
        for n in others:
            send_state(w, n, pass_send_sem, pass_recv_sem)

    def send_beside(n):
        send_state(wide, n, pass_send_sem, pass_recv_sem)

    def send_cells(w):
        pltpu.make_async_remote_copy(
            src_ref=cell_out.at[w],
            dst_ref=cell_in.at[wide],
            send_sem=cell_send_sem,
            recv_sem=cell_recv_sem.at[wide],
            device_id=(w, narrow),
            device_id_type=MESH,
        ).start()

    run(0, wide, send_group)
    run(0, narrow, send_beside)
    run(0, wide, lambda w: signal_group(enter_sem.at[wide], w))
    run(0, narrow, lambda n: signal(enter_sem.at[wide], wide, n))

    for fetch in fetches[5:]:
        fetch.wait()

    gpos, gmass = gal_pos[...], gal_mass[...]
    body_lane = lax.broadcasted_iota(jnp.int32, (1, bodies), 1)
    segment = group_of[...] + (body_lane // (bodies // leaves)) * GROUPS
    onehot = (
        lax.broadcasted_iota(jnp.int32, (LANES, bodies), 0)
        == jnp.broadcast_to(segment, (LANES, bodies))
    ).astype(jnp.float32)
    moments = jnp.concatenate(
        [gpos * gmass, gmass, jnp.zeros((4, bodies), jnp.float32)], axis=0
    )
    sums = lax.dot_general(
        moments,
        onehot,
        (((1,), (1,)), ((), ())),
        precision=lax.Precision.HIGHEST,
        preferred_element_type=jnp.float32,
    )
    cells = jnp.where(row8 < 3, sums / spread(sums[3:4]), sums)

    group = lane // GROUPS
    part = jnp.bitwise_and(group - lax.rem(wide, slots), slots - 1)
    square = (n_wide, n_wide)
    diagonal = lax.broadcasted_iota(jnp.int32, square, 0) == lax.broadcasted_iota(
        jnp.int32, square, 1
    )
    listed = jnp.broadcast_to(let_send[...].astype(jnp.float32), square)
    chosen = jnp.sum(jnp.where(diagonal, listed, 0.0), axis=1, keepdims=True)
    chosen = jnp.broadcast_to(chosen, (n_wide, LANES)).astype(jnp.int32)
    outgoing = jnp.zeros((n_wide, LANES), jnp.float32)
    pick = jnp.bitwise_and(group - chosen, slots - 1)
    for k in range(slots):
        turned = cells if k == 0 else pltpu.roll(cells, k * GROUPS, 1)
        base = jnp.zeros((1, LANES), jnp.float32)
        for c in range(4):
            base = jnp.where(part == c, turned[c : c + 1], base)
        outgoing = jnp.where(
            jnp.logical_and(pick == k, chosen >= 0),
            jnp.broadcast_to(base, (n_wide, LANES)),
            outgoing,
        )
    cell_out[:, 0, :] = outgoing
    cell_in[wide] = jnp.zeros((1, LANES), jnp.float32)
    run(0, wide, send_cells)

    both = jnp.concatenate([pos4, vel4], axis=0)
    targets = jnp.transpose(
        jnp.concatenate([both, jnp.zeros((ROWS, LANES - stars), jnp.float32)], axis=1)
    )
    body_rows = jnp.concatenate(
        [gpos, gmass, jnp.zeros((4, bodies), jnp.float32)], axis=0
    )
    for t in every:
        cols[t * LANES : (t + 1) * LANES, :] = jnp.transpose(
            body_rows[:, t * LANES : (t + 1) * LANES]
        )
    here = [
        [spread(gpos[c : c + 1, t * LANES : (t + 1) * LANES]) for c in range(3)]
        for t in every
    ]
    zero = jnp.zeros((ROWS, LANES), jnp.float32)

    def on_bodies(start, which, total):
        source = cols[pl.ds(pl.multiple_of(start, ROWS), ROWS), :]
        place = [column(source, c) for c in range(3)]
        mass = column(source, 3)
        return tuple(pull(place, mass, here[t], total[i]) for i, t in enumerate(which))

    def keep(total):
        for t in every:
            for c in range(3):
                body_sum[3 * t + c] = total[t][c]

    def kept():
        return tuple(tuple(body_sum[3 * t + c] for c in range(3)) for t in every)

    def sweep(start, count, total):
        return loop(
            count // ROWS,
            lambda g, acc: on_bodies(start + g * ROWS, every, acc),
            total,
            BODY_UNROLL,
        )

    def cells_on_stars(rows, t):
        place = [aims[t, c] for c in range(3)]
        return pull(rows[:3], rows[3], place, [star_sum[t, c] for c in range(3)])

    own = [spread(cells[c : c + 1, :]) for c in range(4)]
    star_groups = stars // ROWS
    for t in range(star_groups):
        mine = targets[t * ROWS : (t + 1) * ROWS, :]
        place = [column(mine, c) for c in range(3)]
        for c in range(3):
            aims[t, c] = place[c]
            aims[t, 3 + c] = column(mine, 4 + c)
            star_sum[t, 3 + c] = zero
        for c, value in enumerate(pull(own[:3], own[3], place, (zero,) * 3)):
            star_sum[t, c] = value

    keep(sweep(0, bodies, ((zero,) * 3,) * tiles))

    def answer(w):
        @pl.when(w == wide)
        def _():
            @pl.when(narrow < n_narrow - 1)
            def _():
                pl.semaphore_wait(enter_sem.at[wide], n_narrow - 1 - narrow)

            run(narrow + 1, n_narrow, send_beside)

        @pl.when(w > wide)
        def _():
            pl.semaphore_wait(enter_sem.at[w], n_narrow)
            send_group(w)
            send_cells(w)

    halves = n_wide // 2
    lower = wide < halves

    run(wide, n_wide, answer)

    def gather(n, even):
        even_block, odd_block = states[n, even], states[n, even + 1]
        rows = jnp.where(left, even_block, odd_block)
        speeds = pltpu.roll(jnp.where(left, odd_block, even_block), stars, 1)
        return rows, speeds

    def arrived(ref, sem, w):
        @pl.when(w != wide)
        def _():
            pltpu.make_async_copy(ref, ref, sem.at[w]).wait()

    def near_stars(even):
        for w in (even, even + 1):
            arrived(states.at[0, 0], near_sem, w)
        rows, _ = gather(narrow, even)
        rows = jnp.concatenate([rows, jnp.zeros((4, LANES), jnp.float32)], axis=0)
        start = pl.multiple_of(star_at + even * stars, LANES)
        cols[pl.ds(start, LANES), :] = jnp.transpose(rows)
        if kicks == n_wide:
            keep(sweep(start, LANES, kept()))

    def near_cells(e):
        for k in range(slots):
            arrived(cell_in.at[0], cell_recv_sem, e * slots + k)
        parts = []
        for c in range(4):
            row = jnp.zeros((1, LANES), jnp.float32)
            for k in range(slots):
                row = jnp.where(group == (c + k) % slots, cell_in[e * slots + k], row)
            parts.append(row if c == 0 else pltpu.roll(row, LANES - c * GROUPS, 1))
        rows = [spread(part) for part in parts]
        for t in range(star_groups):
            for c, value in enumerate(cells_on_stars(rows, t)):
                star_sum[t, c] = value
        parts.append(jnp.zeros((4, LANES), jnp.float32))
        start = pl.multiple_of(cell_at + e * LANES, LANES)
        cols[pl.ds(start, LANES), :] = jnp.transpose(jnp.concatenate(parts, axis=0))
        keep(sweep(start, LANES, kept()))

    def all_stars(even):
        for w in (even, even + 1):
            few = states.at[pl.ds(0, n_narrow - 1), 0]
            pltpu.make_async_copy(few, few, pass_recv_sem.at[w]).wait()
        for n in range(n_narrow):
            rows, speeds = gather(n, even)
            srow[n, 0:4, :] = rows
            srow[n, 4:8, :] = speeds
        sources = [
            [spread(srow[n, c : c + 1, :]) for c in range(7)] for n in range(n_narrow)
        ]
        for t in range(star_groups):
            place = [aims[t, c] for c in range(3)]
            speed = [aims[t, 3 + c] for c in range(3)]
            acc = [star_sum[t, c] for c in range(6)]
            for rows in sources:
                dx, dy, dz = (rows[c] - place[c] for c in range(3))
                ux, uy, uz = (rows[4 + c] - speed[c] for c in range(3))
                inverse = lax.rsqrt(dx * dx + dy * dy + dz * dz + soften_sq)
                square = inverse * inverse
                weight = rows[3] * inverse * square
                approach = 3.0 * (dx * ux + dy * uy + dz * uz) * square
                acc = [
                    acc[0] + dx * weight,
                    acc[1] + dy * weight,
                    acc[2] + dz * weight,
                    acc[3] + (ux - dx * approach) * weight,
                    acc[4] + (uy - dy * approach) * weight,
                    acc[5] + (uz - dz * approach) * weight,
                ]
            for c in range(6):
                star_sum[t, c] = acc[c]

    pairs_per_row = slots // 2

    def turn(p):
        q = jnp.where(lower, p, halves - 1 - p)
        near_stars(2 * q)

        @pl.when(lax.rem(p, pairs_per_row) == pairs_per_row - 1)
        def _():
            near_cells(q // pairs_per_row)

        all_stars(2 * q)

    run(0, halves, turn)

    total = kept()
    if kicks != n_wide:
        kicked = []
        for t in every:

            def one_block(k, acc):
                listed = star_leaf[t * leaves // tiles, k]
                start = star_at + listed * stars
                return loop(
                    stars // ROWS, lambda g, part: on_bodies(start + g * ROWS, (t,), part), acc
                )

            kicked.append(lax.fori_loop(0, kicks, one_block, (total[t],))[0])
        total = tuple(kicked)
    for t in every:
        for c in range(3):
            piece = jnp.sum(total[t][c], axis=0, keepdims=True)
            spot = (slice(c, c + 1), slice(t * LANES, (t + 1) * LANES))
            out[spot] = gal_vel[spot] + time_step * piece

    pieces = []
    for t in range(star_groups):
        piece = jnp.zeros((ROWS, LANES), jnp.float32)
        for c in range(6):
            piece = jnp.where(
                lane8 == c, jnp.sum(star_sum[t, c], axis=1, keepdims=True), piece
            )
        pieces.append(piece)
    result = jnp.transpose(jnp.concatenate(pieces, axis=0))
    new_acc, new_jerk = result[0:3], result[3:6]
    vel_new = (
        svel + time_step * 0.5 * (sacc + new_acc) + step_sq / 12.0 * (sjerk - new_jerk)
    )
    vel_at = bodies + LANES
    out[:, vel_at : vel_at + stars] = vel_new
    out[:, bodies : bodies + stars] = (
        spos + time_step * 0.5 * (svel + vel_new) + step_sq / 12.0 * (sacc - new_acc)
    )

    some = states.at[0, pl.ds(0, n_wide - 1)]
    few = cell_in.at[pl.ds(0, n_wide - 1)]
    rest = states.at[pl.ds(0, n_narrow - 1)]
    pltpu.make_async_copy(some, some, send_sem).wait()
    pltpu.make_async_copy(few, few, cell_send_sem).wait()
    pltpu.make_async_copy(rest, rest, pass_send_sem).wait()


def unpack(packed, gal_out, pos_out, vel_out):
    bodies, stars = gal_out.shape[1], pos_out.shape[1]
    gal_out[...] = packed[:, 0:bodies]
    pos_out[...] = packed[:, bodies : bodies + stars]
    vel_out[...] = packed[:, bodies + LANES : bodies + LANES + stars]


def body(
    n_wide,
    n_narrow,
    star_pos,
    star_vel,
    star_mass,
    star_acc,
    star_jerk,
    gal_pos,
    gal_vel,
    gal_mass,
    group_of,
    let_send,
    star_leaf,
):
    stars, bodies = star_pos.shape[1], gal_pos.shape[1]
    vmem = pl.BlockSpec(memory_space=pltpu.VMEM)
    f32 = jnp.float32
    i32 = jnp.int32
    hbm = pl.BlockSpec(memory_space=pltpu.HBM)
    packed = pl.pallas_call(
        functools.partial(kernel, n_wide, n_narrow),
        out_shape=jax.ShapeDtypeStruct((3, bodies + 2 * LANES), f32),
        in_specs=[hbm] * 11,
        out_specs=vmem,
        scratch_shapes=[
            pltpu.VMEM((3, stars), f32),
            pltpu.VMEM((3, stars), f32),
            pltpu.VMEM((1, stars), f32),
            pltpu.VMEM((3, stars), f32),
            pltpu.VMEM((3, stars), f32),
            pltpu.VMEM((3, bodies), f32),
            pltpu.VMEM((3, bodies), f32),
            pltpu.VMEM((1, bodies), f32),
            pltpu.VMEM((1, bodies), i32),
            pltpu.VMEM((1, n_wide), i32),
            pltpu.SMEM(star_leaf.shape, i32),
            pltpu.SemaphoreType.DMA((11,)),
            pltpu.VMEM((n_narrow, n_wide, 4, LANES), f32),
            pltpu.VMEM((n_wide, 1, LANES), f32),
            pltpu.VMEM((n_wide, 1, LANES), f32),
            pltpu.VMEM((bodies + n_wide * (stars + GROUPS), ROWS), f32),
            pltpu.VMEM((n_narrow, ROWS, LANES), f32),
            pltpu.VMEM((stars // ROWS, 6, ROWS, LANES), f32),
            pltpu.VMEM((3 * bodies // LANES, ROWS, LANES), f32),
            pltpu.VMEM((stars // ROWS, 6, ROWS, LANES), f32),
            pltpu.SemaphoreType.DMA,
            pltpu.SemaphoreType.DMA((n_wide,)),
            pltpu.SemaphoreType.DMA,
            pltpu.SemaphoreType.DMA((n_wide,)),
            pltpu.SemaphoreType.DMA,
            pltpu.SemaphoreType.DMA((n_wide,)),
            pltpu.SemaphoreType.REGULAR((n_wide,)),
        ],
        compiler_params=pltpu.CompilerParams(
            collective_id=0, has_side_effects=True, vmem_limit_bytes=24 << 20
        ),
    )(
        *(
            pltpu.with_memory_space_constraint(array, pltpu.HBM)
            for array in (
                star_pos,
                star_vel,
                star_mass.reshape(1, stars),
                star_acc,
                star_jerk,
                gal_pos,
                gal_vel,
                gal_mass.reshape(1, bodies),
                group_of.reshape(1, bodies),
                let_send.reshape(1, n_wide),
                star_leaf,
            )
        )
    )
    return pl.pallas_call(
        unpack,
        out_shape=(
            jax.ShapeDtypeStruct(gal_vel.shape, f32),
            jax.ShapeDtypeStruct(star_pos.shape, f32),
            jax.ShapeDtypeStruct(star_vel.shape, f32),
        ),
        in_specs=[vmem],
        out_specs=(vmem,) * 3,
        compiler_params=pltpu.CompilerParams(vmem_limit_bytes=1 << 20),
    )(packed)


def solution(mesh):
    both = ("wide", "narrow")
    columns, flat = P(None, both), P(both)
    return jax.shard_map(
        functools.partial(body, mesh.shape["wide"], mesh.shape["narrow"]),
        mesh=mesh,
        in_specs=(
            columns,
            columns,
            flat,
            columns,
            columns,
            columns,
            columns,
            flat,
            flat,
            P(both, None, None),
            P(both, None),
        ),
        out_specs=(columns, columns, columns),
        check_vma=False,
    )
```

```python
import functools

import jax
import jax.numpy as jnp
from jax import lax
from jax.experimental import pallas as pl
from jax.experimental.pallas import tpu as pltpu
from jax.sharding import PartitionSpec as P

GROUPS = 32
LANES = 128
ROWS = 8
BODY_UNROLL = 16
MESH = pl.DeviceIdType.MESH

time_step = 0.25
soften_sq = 0.05


def loop(count, step, init, most=4):
    unroll = next(u for u in range(min(most, count), 0, -1) if count % u == 0)
    return lax.fori_loop(0, count, step, init, unroll=unroll)


def spread(row):
    return jnp.broadcast_to(row, (ROWS, row.shape[1]))


def column(block, index):
    return jnp.broadcast_to(block[:, index : index + 1], (ROWS, LANES))


def pull(source, mass, target, total):
    dx, dy, dz = (s - t for s, t in zip(source, target))
    inverse = lax.rsqrt(dx * dx + dy * dy + dz * dz + soften_sq)
    weight = mass * inverse * inverse * inverse
    return (total[0] + dx * weight, total[1] + dy * weight, total[2] + dz * weight)


def kernel(
    n_wide,
    n_narrow,
    star_pos_hbm,
    star_vel_hbm,
    star_mass_hbm,
    star_acc_hbm,
    star_jerk_hbm,
    gal_pos_hbm,
    gal_vel_hbm,
    gal_mass_hbm,
    group_of_hbm,
    let_send_hbm,
    star_leaf_hbm,
    out,
    star_pos,
    star_vel,
    star_mass,
    star_acc,
    star_jerk,
    gal_pos,
    gal_vel,
    gal_mass,
    group_of,
    let_send,
    star_leaf,
    in_sem,
    states,
    cell_out,
    cell_in,
    cols,
    srow,
    aims,
    body_sum,
    star_sum,
    send_sem,
    near_sem,
    cell_send_sem,
    cell_recv_sem,
    pass_send_sem,
    pass_recv_sem,
    enter_sem,
):
    wide, narrow = lax.axis_index("wide"), lax.axis_index("narrow")
    stars = star_pos.shape[1]
    bodies = gal_pos.shape[1]
    leaves, kicks = star_leaf.shape
    slots = LANES // GROUPS
    step_sq = time_step * time_step
    tiles = bodies // LANES
    every = tuple(range(tiles))
    star_at = bodies
    cell_at = bodies + n_wide * stars

    fetches = [
        pltpu.make_async_copy(source, target, in_sem.at[i])
        for i, (source, target) in enumerate(
            (
                (star_pos_hbm, star_pos),
                (star_vel_hbm, star_vel),
                (star_mass_hbm, star_mass),
                (star_acc_hbm, star_acc),
                (star_jerk_hbm, star_jerk),
                (gal_pos_hbm, gal_pos),
                (gal_vel_hbm, gal_vel),
                (gal_mass_hbm, gal_mass),
                (group_of_hbm, group_of),
                (let_send_hbm, let_send),
                (star_leaf_hbm, star_leaf),
            )
        )
    ]
    for fetch in fetches:
        fetch.start()

    barrier = pltpu.get_barrier_semaphore()
    others = [lax.rem(narrow + m, n_narrow) for m in range(1, n_narrow)]

    def run(first, last, step):
        def body(i, carry):
            step(i)
            return carry

        lax.fori_loop(first, last, body, 0)

    def signal(sem, w, n):
        pl.semaphore_signal(sem, inc=1, device_id=(w, n), device_id_type=MESH)

    def signal_group(sem, w):
        for n in range(n_narrow):
            signal(sem, w, n)

    run(narrow + 1, n_narrow, lambda n: signal(barrier, wide, n))
    run(wide + 1, n_wide, lambda w: signal_group(barrier, w))

    lane = lax.broadcasted_iota(jnp.int32, (1, LANES), 1)
    lane4 = lax.broadcasted_iota(jnp.int32, (4, LANES), 1)
    lane8 = lax.broadcasted_iota(jnp.int32, (ROWS, LANES), 1)
    row8 = lax.broadcasted_iota(jnp.int32, (ROWS, LANES), 0)
    left = lane4 < stars

    for fetch in fetches[:5]:
        fetch.wait()

    spos, svel = star_pos[...], star_vel[...]
    sacc, sjerk = star_acc[...], star_jerk[...]
    pred_pos = (
        spos + time_step * svel + step_sq * 0.5 * sacc + step_sq * time_step / 6.0 * sjerk
    )
    pred_vel = svel + time_step * sacc + step_sq * 0.5 * sjerk
    pos4 = jnp.concatenate([pred_pos, star_mass[...]], axis=0)
    vel4 = jnp.concatenate([pred_vel, jnp.zeros((1, stars), jnp.float32)], axis=0)
    block = jnp.concatenate([pos4, vel4], axis=1)
    block = jnp.where(lax.rem(wide, 2) == 0, block, pltpu.roll(block, stars, 1))
    states[narrow, wide] = block

    smaller = wide * n_narrow + narrow

    @pl.when(smaller > 0)
    def _():
        pl.semaphore_wait(barrier, smaller)

    def send_state(w, n, sends, recvs):
        pltpu.make_async_remote_copy(
            src_ref=states.at[narrow, wide],
            dst_ref=states.at[narrow, wide],
            send_sem=sends,
            recv_sem=recvs.at[wide],
            device_id=(w, n),
            device_id_type=MESH,
        ).start()

    def send_group(w):
        send_state(w, narrow, send_sem, near_sem)
        for n in others:
            send_state(w, n, pass_send_sem, pass_recv_sem)

    def send_beside(n):
        send_state(wide, n, pass_send_sem, pass_recv_sem)

    def send_cells(w):
        pltpu.make_async_remote_copy(
            src_ref=cell_out.at[w],
            dst_ref=cell_in.at[wide],
            send_sem=cell_send_sem,
            recv_sem=cell_recv_sem.at[wide],
            device_id=(w, narrow),
            device_id_type=MESH,
        ).start()

    first = jnp.minimum(wide, 1)
    run(0, first, send_group)
    run(0, wide, lambda w: signal_group(enter_sem.at[wide], w))
    run(0, narrow, lambda n: signal(enter_sem.at[wide], wide, n))
    run(first, wide, send_group)
    run(0, narrow, send_beside)

    for fetch in fetches[5:]:
        fetch.wait()

    gpos, gmass = gal_pos[...], gal_mass[...]
    body_lane = lax.broadcasted_iota(jnp.int32, (1, bodies), 1)
    segment = group_of[...] + (body_lane // (bodies // leaves)) * GROUPS
    onehot = (
        lax.broadcasted_iota(jnp.int32, (LANES, bodies), 0)
        == jnp.broadcast_to(segment, (LANES, bodies))
    ).astype(jnp.float32)
    moments = jnp.concatenate(
        [gpos * gmass, gmass, jnp.zeros((4, bodies), jnp.float32)], axis=0
    )
    sums = lax.dot_general(
        moments,
        onehot,
        (((1,), (1,)), ((), ())),
        precision=lax.Precision.HIGHEST,
        preferred_element_type=jnp.float32,
    )
    cells = jnp.where(row8 < 3, sums / spread(sums[3:4]), sums)

    group = lane // GROUPS
    part = jnp.bitwise_and(group - lax.rem(wide, slots), slots - 1)
    square = (n_wide, n_wide)
    diagonal = lax.broadcasted_iota(jnp.int32, square, 0) == lax.broadcasted_iota(
        jnp.int32, square, 1
    )
    listed = jnp.broadcast_to(let_send[...].astype(jnp.float32), square)
    chosen = jnp.sum(jnp.where(diagonal, listed, 0.0), axis=1, keepdims=True)
    chosen = jnp.broadcast_to(chosen, (n_wide, LANES)).astype(jnp.int32)
    outgoing = jnp.zeros((n_wide, LANES), jnp.float32)
    pick = jnp.bitwise_and(group - chosen, slots - 1)
    for k in range(slots):
        turned = cells if k == 0 else pltpu.roll(cells, k * GROUPS, 1)
        base = jnp.zeros((1, LANES), jnp.float32)
        for c in range(4):
            base = jnp.where(part == c, turned[c : c + 1], base)
        outgoing = jnp.where(
            jnp.logical_and(pick == k, chosen >= 0),
            jnp.broadcast_to(base, (n_wide, LANES)),
            outgoing,
        )
    cell_out[:, 0, :] = outgoing
    cell_in[wide] = jnp.zeros((1, LANES), jnp.float32)
    run(0, wide, send_cells)

    both = jnp.concatenate([pos4, vel4], axis=0)
    targets = jnp.transpose(
        jnp.concatenate([both, jnp.zeros((ROWS, LANES - stars), jnp.float32)], axis=1)
    )
    body_rows = jnp.concatenate(
        [gpos, gmass, jnp.zeros((4, bodies), jnp.float32)], axis=0
    )
    for t in every:
        cols[t * LANES : (t + 1) * LANES, :] = jnp.transpose(
            body_rows[:, t * LANES : (t + 1) * LANES]
        )
    here = [
        [spread(gpos[c : c + 1, t * LANES : (t + 1) * LANES]) for c in range(3)]
        for t in every
    ]
    zero = jnp.zeros((ROWS, LANES), jnp.float32)

    def on_bodies(start, which, total):
        source = cols[pl.ds(pl.multiple_of(start, ROWS), ROWS), :]
        place = [column(source, c) for c in range(3)]
        mass = column(source, 3)
        return tuple(pull(place, mass, here[t], total[i]) for i, t in enumerate(which))

    def keep(total):
        for t in every:
            for c in range(3):
                body_sum[3 * t + c] = total[t][c]

    def kept():
        return tuple(tuple(body_sum[3 * t + c] for c in range(3)) for t in every)

    def sweep(start, count, total):
        return loop(
            count // ROWS,
            lambda g, acc: on_bodies(start + g * ROWS, every, acc),
            total,
            BODY_UNROLL,
        )

    def cells_on_stars(rows, t):
        place = [aims[t, c] for c in range(3)]
        return pull(rows[:3], rows[3], place, [star_sum[t, c] for c in range(3)])

    own = [spread(cells[c : c + 1, :]) for c in range(4)]
    star_groups = stars // ROWS
    for t in range(star_groups):
        mine = targets[t * ROWS : (t + 1) * ROWS, :]
        place = [column(mine, c) for c in range(3)]
        for c in range(3):
            aims[t, c] = place[c]
            aims[t, 3 + c] = column(mine, 4 + c)
            star_sum[t, 3 + c] = zero
        for c, value in enumerate(pull(own[:3], own[3], place, (zero,) * 3)):
            star_sum[t, c] = value

    keep(sweep(0, bodies, ((zero,) * 3,) * tiles))

    def answer(w):
        @pl.when(w == wide)
        def _():
            @pl.when(narrow < n_narrow - 1)
            def _():
                pl.semaphore_wait(enter_sem.at[wide], n_narrow - 1 - narrow)

            run(narrow + 1, n_narrow, send_beside)

        @pl.when(w > wide)
        def _():
            pl.semaphore_wait(enter_sem.at[w], n_narrow)
            send_group(w)
            send_cells(w)

    halves = n_wide // 2
    lower = wide < n_wide // 4


    def gather(n, even):
        even_block, odd_block = states[n, even], states[n, even + 1]
        rows = jnp.where(left, even_block, odd_block)
        speeds = pltpu.roll(jnp.where(left, odd_block, even_block), stars, 1)
        return rows, speeds

    def arrived(ref, sem, w):
        @pl.when(w != wide)
        def _():
            pltpu.make_async_copy(ref, ref, sem.at[w]).wait()

    def near_stars(even):
        for w in (even, even + 1):
            arrived(states.at[0, 0], near_sem, w)
        rows, _ = gather(narrow, even)
        rows = jnp.concatenate([rows, jnp.zeros((4, LANES), jnp.float32)], axis=0)
        start = pl.multiple_of(star_at + even * stars, LANES)
        cols[pl.ds(start, LANES), :] = jnp.transpose(rows)
        if kicks == n_wide:
            keep(sweep(start, LANES, kept()))

    def near_cells(e):
        for k in range(slots):
            arrived(cell_in.at[0], cell_recv_sem, e * slots + k)
        parts = []
        for c in range(4):
            row = jnp.zeros((1, LANES), jnp.float32)
            for k in range(slots):
                row = jnp.where(group == (c + k) % slots, cell_in[e * slots + k], row)
            parts.append(row if c == 0 else pltpu.roll(row, LANES - c * GROUPS, 1))
        rows = [spread(part) for part in parts]
        for t in range(star_groups):
            for c, value in enumerate(cells_on_stars(rows, t)):
                star_sum[t, c] = value
        parts.append(jnp.zeros((4, LANES), jnp.float32))
        start = pl.multiple_of(cell_at + e * LANES, LANES)
        cols[pl.ds(start, LANES), :] = jnp.transpose(jnp.concatenate(parts, axis=0))
        keep(sweep(start, LANES, kept()))

    def all_stars(even):
        for w in (even, even + 1):
            few = states.at[pl.ds(0, n_narrow - 1), 0]
            pltpu.make_async_copy(few, few, pass_recv_sem.at[w]).wait()
        for n in range(n_narrow):
            rows, speeds = gather(n, even)
            srow[n, 0:4, :] = rows
            srow[n, 4:8, :] = speeds
        sources = [
            [spread(srow[n, c : c + 1, :]) for c in range(7)] for n in range(n_narrow)
        ]
        for t in range(star_groups):
            place = [aims[t, c] for c in range(3)]
            speed = [aims[t, 3 + c] for c in range(3)]
            acc = [star_sum[t, c] for c in range(6)]
            for rows in sources:
                dx, dy, dz = (rows[c] - place[c] for c in range(3))
                ux, uy, uz = (rows[4 + c] - speed[c] for c in range(3))
                inverse = lax.rsqrt(dx * dx + dy * dy + dz * dz + soften_sq)
                square = inverse * inverse
                weight = rows[3] * inverse * square
                approach = 3.0 * (dx * ux + dy * uy + dz * uz) * square
                acc = [
                    acc[0] + dx * weight,
                    acc[1] + dy * weight,
                    acc[2] + dz * weight,
                    acc[3] + (ux - dx * approach) * weight,
                    acc[4] + (uy - dy * approach) * weight,
                    acc[5] + (uz - dz * approach) * weight,
                ]
            for c in range(6):
                star_sum[t, c] = acc[c]

    pairs_per_row = slots // 2

    early = jnp.where(lower, halves, n_wide)

    def turn(p):
        run(
            jnp.where(p == 0, wide, early),
            jnp.where(p == 0, early, jnp.where(p == 1, n_wide, 0)),
            answer,
        )
        q = jnp.where(lower, p, halves - 1 - p)
        near_stars(2 * q)

        @pl.when(lax.rem(p, pairs_per_row) == pairs_per_row - 1)
        def _():
            near_cells(q // pairs_per_row)

        all_stars(2 * q)

    run(0, halves, turn)

    total = kept()
    if kicks != n_wide:
        kicked = []
        for t in every:

            def one_block(k, acc):
                listed = star_leaf[t * leaves // tiles, k]
                start = star_at + listed * stars
                return loop(
                    stars // ROWS, lambda g, part: on_bodies(start + g * ROWS, (t,), part), acc
                )

            kicked.append(lax.fori_loop(0, kicks, one_block, (total[t],))[0])
        total = tuple(kicked)
    for t in every:
        for c in range(3):
            piece = jnp.sum(total[t][c], axis=0, keepdims=True)
            spot = (slice(c, c + 1), slice(t * LANES, (t + 1) * LANES))
            out[spot] = gal_vel[spot] + time_step * piece

    pieces = []
    for t in range(star_groups):
        piece = jnp.zeros((ROWS, LANES), jnp.float32)
        for c in range(6):
            piece = jnp.where(
                lane8 == c, jnp.sum(star_sum[t, c], axis=1, keepdims=True), piece
            )
        pieces.append(piece)
    result = jnp.transpose(jnp.concatenate(pieces, axis=0))
    new_acc, new_jerk = result[0:3], result[3:6]
    vel_new = (
        svel + time_step * 0.5 * (sacc + new_acc) + step_sq / 12.0 * (sjerk - new_jerk)
    )
    vel_at = bodies + LANES
    out[:, vel_at : vel_at + stars] = vel_new
    out[:, bodies : bodies + stars] = (
        spos + time_step * 0.5 * (svel + vel_new) + step_sq / 12.0 * (sacc - new_acc)
    )

    some = states.at[0, pl.ds(0, n_wide - 1)]
    few = cell_in.at[pl.ds(0, n_wide - 1)]
    rest = states.at[pl.ds(0, n_narrow - 1)]
    pltpu.make_async_copy(some, some, send_sem).wait()
    pltpu.make_async_copy(few, few, cell_send_sem).wait()
    pltpu.make_async_copy(rest, rest, pass_send_sem).wait()


def unpack(packed, gal_out, pos_out, vel_out):
    bodies, stars = gal_out.shape[1], pos_out.shape[1]
    gal_out[...] = packed[:, 0:bodies]
    pos_out[...] = packed[:, bodies : bodies + stars]
    vel_out[...] = packed[:, bodies + LANES : bodies + LANES + stars]


def body(
    n_wide,
    n_narrow,
    star_pos,
    star_vel,
    star_mass,
    star_acc,
    star_jerk,
    gal_pos,
    gal_vel,
    gal_mass,
    group_of,
    let_send,
    star_leaf,
):
    stars, bodies = star_pos.shape[1], gal_pos.shape[1]
    vmem = pl.BlockSpec(memory_space=pltpu.VMEM)
    f32 = jnp.float32
    i32 = jnp.int32
    hbm = pl.BlockSpec(memory_space=pltpu.HBM)
    packed = pl.pallas_call(
        functools.partial(kernel, n_wide, n_narrow),
        out_shape=jax.ShapeDtypeStruct((3, bodies + 2 * LANES), f32),
        in_specs=[hbm] * 11,
        out_specs=vmem,
        scratch_shapes=[
            pltpu.VMEM((3, stars), f32),
            pltpu.VMEM((3, stars), f32),
            pltpu.VMEM((1, stars), f32),
            pltpu.VMEM((3, stars), f32),
            pltpu.VMEM((3, stars), f32),
            pltpu.VMEM((3, bodies), f32),
            pltpu.VMEM((3, bodies), f32),
            pltpu.VMEM((1, bodies), f32),
            pltpu.VMEM((1, bodies), i32),
            pltpu.VMEM((1, n_wide), i32),
            pltpu.SMEM(star_leaf.shape, i32),
            pltpu.SemaphoreType.DMA((11,)),
            pltpu.VMEM((n_narrow, n_wide, 4, LANES), f32),
            pltpu.VMEM((n_wide, 1, LANES), f32),
            pltpu.VMEM((n_wide, 1, LANES), f32),
            pltpu.VMEM((bodies + n_wide * (stars + GROUPS), ROWS), f32),
            pltpu.VMEM((n_narrow, ROWS, LANES), f32),
            pltpu.VMEM((stars // ROWS, 6, ROWS, LANES), f32),
            pltpu.VMEM((3 * bodies // LANES, ROWS, LANES), f32),
            pltpu.VMEM((stars // ROWS, 6, ROWS, LANES), f32),
            pltpu.SemaphoreType.DMA,
            pltpu.SemaphoreType.DMA((n_wide,)),
            pltpu.SemaphoreType.DMA,
            pltpu.SemaphoreType.DMA((n_wide,)),
            pltpu.SemaphoreType.DMA,
            pltpu.SemaphoreType.DMA((n_wide,)),
            pltpu.SemaphoreType.REGULAR((n_wide,)),
        ],
        compiler_params=pltpu.CompilerParams(
            collective_id=0, has_side_effects=True, vmem_limit_bytes=24 << 20
        ),
    )(
        *(
            pltpu.with_memory_space_constraint(array, pltpu.HBM)
            for array in (
                star_pos,
                star_vel,
                star_mass.reshape(1, stars),
                star_acc,
                star_jerk,
                gal_pos,
                gal_vel,
                gal_mass.reshape(1, bodies),
                group_of.reshape(1, bodies),
                let_send.reshape(1, n_wide),
                star_leaf,
            )
        )
    )
    return pl.pallas_call(
        unpack,
        out_shape=(
            jax.ShapeDtypeStruct(gal_vel.shape, f32),
            jax.ShapeDtypeStruct(star_pos.shape, f32),
            jax.ShapeDtypeStruct(star_vel.shape, f32),
        ),
        in_specs=[vmem],
        out_specs=(vmem,) * 3,
        compiler_params=pltpu.CompilerParams(vmem_limit_bytes=1 << 20),
    )(packed)


def solution(mesh):
    both = ("wide", "narrow")
    columns, flat = P(None, both), P(both)
    return jax.shard_map(
        functools.partial(body, mesh.shape["wide"], mesh.shape["narrow"]),
        mesh=mesh,
        in_specs=(
            columns,
            columns,
            flat,
            columns,
            columns,
            columns,
            columns,
            flat,
            flat,
            P(both, None, None),
            P(both, None),
        ),
        out_specs=(columns, columns, columns),
        check_vma=False,
    )
```

```python
import functools

import jax
import jax.numpy as jnp
from jax import lax
from jax.experimental import pallas as pl
from jax.experimental.pallas import tpu as pltpu
from jax.sharding import PartitionSpec as P

GROUPS = 32
LANES = 128
ROWS = 8
MESH = pl.DeviceIdType.MESH

time_step = 0.25
soften_sq = 0.05


def loop(count, step, init, most=4):
    unroll = next(u for u in range(min(most, count), 0, -1) if count % u == 0)
    return lax.fori_loop(0, count, step, init, unroll=unroll)


def spread(row):
    return jnp.broadcast_to(row, (ROWS, row.shape[1]))


def column(block, index):
    return jnp.broadcast_to(block[:, index : index + 1], (ROWS, LANES))


def pull(source, mass, target, total):
    dx, dy, dz = (s - t for s, t in zip(source, target))
    inverse = lax.rsqrt(dx * dx + dy * dy + dz * dz + soften_sq)
    weight = mass * inverse * inverse * inverse
    return (total[0] + dx * weight, total[1] + dy * weight, total[2] + dz * weight)


def norm(rows):
    return rows[0:1] * rows[0:1] + rows[1:2] * rows[1:2] + rows[2:3] * rows[2:3]


def split(value):
    parts = []
    for _ in range(3):
        parts.append(value.astype(jnp.bfloat16).astype(jnp.float32))
        value = value - parts[-1]
    return parts


def kernel(
    n_wide,
    n_narrow,
    star_pos_hbm,
    star_vel_hbm,
    star_mass_hbm,
    star_acc_hbm,
    star_jerk_hbm,
    gal_pos_hbm,
    gal_vel_hbm,
    gal_mass_hbm,
    group_of_hbm,
    let_send_hbm,
    star_leaf_hbm,
    out,
    star_pos,
    star_vel,
    star_mass,
    star_acc,
    star_jerk,
    gal_pos,
    gal_vel,
    gal_mass,
    group_of,
    let_send,
    star_leaf,
    in_sem,
    states,
    cell_own,
    cell_out,
    cell_in,
    aimed,
    cols,
    srow,
    aims,
    body_sum,
    star_sum,
    send_sem,
    near_sem,
    cell_send_sem,
    cell_recv_sem,
    pass_send_sem,
    pass_recv_sem,
    enter_sem,
):
    wide, narrow = lax.axis_index("wide"), lax.axis_index("narrow")
    stars = star_pos.shape[1]
    bodies = gal_pos.shape[1]
    leaves, kicks = star_leaf.shape
    slots = LANES // GROUPS
    step_sq = time_step * time_step
    tiles = bodies // LANES
    every = tuple(range(tiles))

    fetches = [
        pltpu.make_async_copy(source, target, in_sem.at[i])
        for i, (source, target) in enumerate(
            (
                (star_pos_hbm, star_pos),
                (star_vel_hbm, star_vel),
                (star_mass_hbm, star_mass),
                (star_acc_hbm, star_acc),
                (star_jerk_hbm, star_jerk),
                (gal_pos_hbm, gal_pos),
                (gal_vel_hbm, gal_vel),
                (gal_mass_hbm, gal_mass),
                (group_of_hbm, group_of),
                (let_send_hbm, let_send),
                (star_leaf_hbm, star_leaf),
            )
        )
    ]
    for fetch in fetches:
        fetch.start()

    barrier = pltpu.get_barrier_semaphore()
    others = [lax.rem(narrow + m, n_narrow) for m in range(1, n_narrow)]

    def run(first, last, step):
        def body(i, carry):
            step(i)
            return carry

        lax.fori_loop(first, last, body, 0)

    def signal(sem, w, n):
        pl.semaphore_signal(sem, inc=1, device_id=(w, n), device_id_type=MESH)

    def signal_group(sem, w):
        for n in range(n_narrow):
            signal(sem, w, n)

    run(narrow + 1, n_narrow, lambda n: signal(barrier, wide, n))
    run(wide + 1, n_wide, lambda w: signal_group(barrier, w))

    lane = lax.broadcasted_iota(jnp.int32, (1, LANES), 1)
    lane4 = lax.broadcasted_iota(jnp.int32, (4, LANES), 1)
    lane8 = lax.broadcasted_iota(jnp.int32, (ROWS, LANES), 1)
    row8 = lax.broadcasted_iota(jnp.int32, (ROWS, LANES), 0)
    left = lane4 < stars

    for fetch in fetches[:5]:
        fetch.wait()

    spos, svel = star_pos[...], star_vel[...]
    sacc, sjerk = star_acc[...], star_jerk[...]
    pred_pos = (
        spos + time_step * svel + step_sq * 0.5 * sacc + step_sq * time_step / 6.0 * sjerk
    )
    pred_vel = svel + time_step * sacc + step_sq * 0.5 * sjerk
    pos4 = jnp.concatenate([pred_pos, star_mass[...]], axis=0)
    vel4 = jnp.concatenate([pred_vel, jnp.zeros((1, stars), jnp.float32)], axis=0)
    block = jnp.concatenate([pos4, vel4], axis=1)
    block = jnp.where(lax.rem(wide, 2) == 0, block, pltpu.roll(block, stars, 1))
    states[narrow, wide] = block

    def send_state(w, n, sends, recvs):
        pltpu.make_async_remote_copy(
            src_ref=states.at[narrow, wide],
            dst_ref=states.at[narrow, wide],
            send_sem=sends,
            recv_sem=recvs.at[wide],
            device_id=(w, n),
            device_id_type=MESH,
        ).start()

    def send_group(w):
        send_state(w, narrow, send_sem, near_sem)
        for n in others:
            send_state(w, n, pass_send_sem, pass_recv_sem)

    def send_beside(n):
        send_state(wide, n, pass_send_sem, pass_recv_sem)

    def send_cells(w):
        pltpu.make_async_remote_copy(
            src_ref=cell_out.at[w],
            dst_ref=cell_in.at[wide],
            send_sem=cell_send_sem,
            recv_sem=cell_recv_sem.at[wide],
            device_id=(w, narrow),
            device_id_type=MESH,
        ).start()

    group = lane // GROUPS

    def meet():
        smaller = wide * n_narrow + narrow

        @pl.when(smaller > 0)
        def _():
            pl.semaphore_wait(barrier, smaller)

        run(0, wide, lambda w: signal_group(enter_sem.at[wide], w))
        run(0, narrow, lambda n: signal(enter_sem.at[wide], wide, n))

        def send_down(w):
            send_group(w)

            @pl.when(cells_first)
            def _():
                send_cells(w)

        run(0, wide, send_down)
        run(0, narrow, send_beside)

    def make_cells():
        for fetch in fetches[5:]:
            fetch.wait()
        gpos, gmass = gal_pos[...], gal_mass[...]
        body_lane = lax.broadcasted_iota(jnp.int32, (1, bodies), 1)
        segment = group_of[...] + (body_lane // (bodies // leaves)) * GROUPS
        onehot = (
            lax.broadcasted_iota(jnp.int32, (LANES, bodies), 0)
            == jnp.broadcast_to(segment, (LANES, bodies))
        ).astype(jnp.bfloat16)
        moments = jnp.concatenate(
            [gpos * gmass, gmass, jnp.zeros((4, bodies), jnp.float32)], axis=0
        )
        sums = lax.dot_general(
            jnp.concatenate(split(moments), axis=0).astype(jnp.bfloat16),
            onehot,
            (((1,), (1,)), ((), ())),
            preferred_element_type=jnp.float32,
        )
        sums = sums[0:8] + sums[8:16] + sums[16:24]
        cells = jnp.where(row8 < 3, sums / spread(sums[3:4]), sums)
        cell_own[...] = cells

        part = jnp.bitwise_and(group - lax.rem(wide, slots), slots - 1)
        square = (n_wide, n_wide)
        diagonal = lax.broadcasted_iota(jnp.int32, square, 0) == lax.broadcasted_iota(
            jnp.int32, square, 1
        )
        listed = jnp.broadcast_to(let_send[...].astype(jnp.float32), square)
        chosen = jnp.sum(jnp.where(diagonal, listed, 0.0), axis=1, keepdims=True)
        chosen = jnp.broadcast_to(chosen, (n_wide, LANES)).astype(jnp.int32)
        outgoing = jnp.zeros((n_wide, LANES), jnp.float32)
        pick = jnp.bitwise_and(group - chosen, slots - 1)
        for k in range(slots):
            turned = cells if k == 0 else pltpu.roll(cells, k * GROUPS, 1)
            base = jnp.zeros((1, LANES), jnp.float32)
            for c in range(4):
                base = jnp.where(part == c, turned[c : c + 1], base)
            outgoing = jnp.where(
                jnp.logical_and(pick == k, chosen >= 0),
                jnp.broadcast_to(base, (n_wide, LANES)),
                outgoing,
            )
        cell_out[:, 0, :] = outgoing
        cell_in[wide] = jnp.zeros((1, LANES), jnp.float32)

    cells_first = jnp.logical_or(lax.rem(wide, 2) == 0, narrow < n_narrow // 2)

    def order(i):
        @pl.when(jnp.equal(i == 0, cells_first))
        def _():
            make_cells()

        @pl.when(jnp.not_equal(i == 0, cells_first))
        def _():
            meet()

    run(0, 2, order)

    @pl.when(jnp.logical_not(cells_first))
    def _():
        run(0, wide, send_cells)

    gpos, gmass = gal_pos[...], gal_mass[...]

    both = jnp.concatenate([pos4, vel4], axis=0)
    targets = jnp.transpose(
        jnp.concatenate([both, jnp.zeros((ROWS, LANES - stars), jnp.float32)], axis=1)
    )
    zero = jnp.zeros((ROWS, LANES), jnp.float32)

    own = [spread(cell_own[c : c + 1, :]) for c in range(4)]
    star_groups = stars // ROWS
    for t in range(star_groups):
        mine = targets[t * ROWS : (t + 1) * ROWS, :]
        place = [column(mine, c) for c in range(3)]
        for c in range(3):
            aims[t, c] = place[c]
            aims[t, 3 + c] = column(mine, 4 + c)
            star_sum[t, 3 + c] = zero
        for c, value in enumerate(pull(own[:3], own[3], place, (zero,) * 3)):
            star_sum[t, c] = value

    last4 = lax.broadcasted_iota(jnp.int32, (4, bodies), 0) == 3
    high, mid, low = split(jnp.concatenate([-2.0 * gpos, jnp.zeros_like(gmass)], axis=0))
    high = jnp.where(last4, 1.0, high)
    reach = split(norm(gpos) + soften_sq)
    blank = jnp.zeros_like(gmass)
    aimed[...] = jnp.concatenate(
        [high, mid, high, low, high, mid, *reach, blank, blank, blank, blank, blank],
        axis=0,
    ).astype(jnp.bfloat16)

    def on_bodies(rows, total):
        square = norm(rows[0:3])
        high, mid, low = split(jnp.concatenate([rows[0:3], square], axis=0))
        ones = jnp.ones((4, LANES), jnp.float32)
        turned = jnp.transpose(
            jnp.concatenate([high, high, mid, high, low, mid, ones, rows], axis=0)
        )
        reach = jnp.dot(
            turned.astype(jnp.bfloat16), aimed[...], preferred_element_type=jnp.float32
        )
        total = [list(part) for part in total]
        for g in range(LANES // ROWS):
            mine = turned[g * ROWS : (g + 1) * ROWS, :]
            place = [column(mine, 28 + c) for c in range(3)]
            mass = column(mine, 31)
            for t in every:
                inverse = lax.rsqrt(
                    reach[g * ROWS : (g + 1) * ROWS, t * LANES : (t + 1) * LANES]
                )
                weight = mass * inverse * (inverse * inverse)
                for c in range(3):
                    total[t][c] = total[t][c] + place[c] * weight
                total[t][3] = total[t][3] + weight
        return total

    def keep(total):
        for t in every:
            for c in range(4):
                body_sum[4 * t + c] = total[t][c]

    def kept():
        return [[body_sum[4 * t + c] for c in range(4)] for t in every]

    def cells_on_stars(rows, t):
        place = [aims[t, c] for c in range(3)]
        return pull(rows[:3], rows[3], place, [star_sum[t, c] for c in range(3)])

    total = [[zero] * 4 for _ in every]
    for t in every:
        tile = slice(t * LANES, (t + 1) * LANES)
        total = on_bodies(jnp.concatenate([gpos[:, tile], gmass[:, tile]], axis=0), total)
    keep(total)

    def answer(w):
        @pl.when(w == wide)
        def _():
            @pl.when(narrow < n_narrow - 1)
            def _():
                pl.semaphore_wait(enter_sem.at[wide], n_narrow - 1 - narrow)

            run(narrow + 1, n_narrow, send_beside)

        @pl.when(w > wide)
        def _():
            pl.semaphore_wait(enter_sem.at[w], n_narrow)
            send_group(w)
            send_cells(w)

    halves = n_wide // 2
    lower = wide < n_wide // 4


    def gather(n, even):
        even_block, odd_block = states[n, even], states[n, even + 1]
        rows = jnp.where(left, even_block, odd_block)
        speeds = pltpu.roll(jnp.where(left, odd_block, even_block), stars, 1)
        return rows, speeds

    def arrived(ref, sem, w):
        @pl.when(w != wide)
        def _():
            pltpu.make_async_copy(ref, ref, sem.at[w]).wait()

    def near_stars(even, total):
        near, _ = gather(narrow, even)
        if kicks == n_wide:
            return on_bodies(near, total)
        padded = jnp.concatenate([near, jnp.zeros((4, LANES), jnp.float32)], axis=0)
        cols[pl.ds(pl.multiple_of(even * stars, LANES), LANES), :] = jnp.transpose(padded)
        return total

    def near_cells(e, total):
        parts = []
        for c in range(4):
            row = jnp.zeros((1, LANES), jnp.float32)
            for k in range(slots):
                row = jnp.where(group == (c + k) % slots, cell_in[e * slots + k], row)
            parts.append(row if c == 0 else pltpu.roll(row, LANES - c * GROUPS, 1))
        rows = [spread(part) for part in parts]
        for t in range(star_groups):
            for c, value in enumerate(cells_on_stars(rows, t)):
                star_sum[t, c] = value
        return on_bodies(jnp.concatenate(parts, axis=0), total)

    def near_arrived(even):
        for w in (even, even + 1):
            arrived(states.at[0, 0], near_sem, w)

    def rest_arrived(even):
        for w in (even, even + 1):
            few = states.at[pl.ds(0, n_narrow - 1), 0]
            pltpu.make_async_copy(few, few, pass_recv_sem.at[w]).wait()

    def all_stars(even):
        for n in range(n_narrow):
            rows, speeds = gather(n, even)
            srow[n, 0:4, :] = rows
            srow[n, 4:8, :] = speeds
        sources = [
            [spread(srow[n, c : c + 1, :]) for c in range(7)] for n in range(n_narrow)
        ]
        for t in range(star_groups):
            place = [aims[t, c] for c in range(3)]
            speed = [aims[t, 3 + c] for c in range(3)]
            acc = [star_sum[t, c] for c in range(6)]
            for rows in sources:
                dx, dy, dz = (rows[c] - place[c] for c in range(3))
                ux, uy, uz = (rows[4 + c] - speed[c] for c in range(3))
                inverse = lax.rsqrt(dx * dx + dy * dy + dz * dz + soften_sq)
                square = inverse * inverse
                weight = rows[3] * inverse * square
                approach = 3.0 * (dx * ux + dy * uy + dz * uz) * square
                acc = [
                    acc[0] + dx * weight,
                    acc[1] + dy * weight,
                    acc[2] + dz * weight,
                    acc[3] + (ux - dx * approach) * weight,
                    acc[4] + (uy - dy * approach) * weight,
                    acc[5] + (uz - dz * approach) * weight,
                ]
            for c in range(6):
                star_sum[t, c] = acc[c]

    pairs_per_row = slots // 2

    early = jnp.where(lower, halves, n_wide)

    def turn(p):
        run(
            jnp.where(p == 0, wide, early),
            jnp.where(p == 0, early, jnp.where(p == 1, n_wide, 0)),
            answer,
        )
        q = jnp.where(lower, p, halves - 1 - p)
        near_arrived(2 * q)
        second = lax.rem(p, pairs_per_row) == pairs_per_row - 1

        @pl.when(second)
        def _():
            e = q // pairs_per_row
            for k in range(slots):
                arrived(cell_in.at[0], cell_recv_sem, e * slots + k)
            keep(near_cells(e, near_stars(2 * q, kept())))
            rest_arrived(2 * q)
            all_stars(2 * q)

        @pl.when(jnp.logical_not(second))
        def _():
            rest_arrived(2 * q)
            keep(near_stars(2 * q, kept()))
            all_stars(2 * q)

    run(0, halves, turn)

    total = kept()
    for t in every:
        tile = slice(t * LANES, (t + 1) * LANES)
        near = [gpos[c : c + 1, tile] for c in range(3)]
        pieces = [jnp.sum(part, axis=0, keepdims=True) for part in total[t]]
        pieces = [pieces[c] - near[c] * pieces[3] for c in range(3)]
        if kicks != n_wide:
            here = [spread(row) for row in near]

            def kick(k, acc):
                listed = star_leaf[t * leaves // tiles, k]

                def some(g, acc):
                    at = pl.multiple_of(listed * stars + g * ROWS, ROWS)
                    source = cols[pl.ds(at, ROWS), :]
                    place = [column(source, c) for c in range(3)]
                    return pull(place, column(source, 3), here, acc)

                return loop(stars // ROWS, some, acc)

            kicked = lax.fori_loop(0, kicks, kick, (zero,) * 3)
            for c in range(3):
                pieces[c] = pieces[c] + jnp.sum(kicked[c], axis=0, keepdims=True)
        for c in range(3):
            out[c : c + 1, tile] = gal_vel[c : c + 1, tile] + time_step * pieces[c]

    pieces = []
    for t in range(star_groups):
        piece = jnp.zeros((ROWS, LANES), jnp.float32)
        for c in range(6):
            piece = jnp.where(
                lane8 == c, jnp.sum(star_sum[t, c], axis=1, keepdims=True), piece
            )
        pieces.append(piece)
    result = jnp.transpose(jnp.concatenate(pieces, axis=0))
    new_acc, new_jerk = result[0:3], result[3:6]
    vel_new = (
        svel + time_step * 0.5 * (sacc + new_acc) + step_sq / 12.0 * (sjerk - new_jerk)
    )
    vel_at = bodies + LANES
    out[:, vel_at : vel_at + stars] = vel_new
    out[:, bodies : bodies + stars] = (
        spos + time_step * 0.5 * (svel + vel_new) + step_sq / 12.0 * (sacc - new_acc)
    )

    some = states.at[0, pl.ds(0, n_wide - 1)]
    few = cell_in.at[pl.ds(0, n_wide - 1)]
    rest = states.at[pl.ds(0, n_narrow - 1)]
    pltpu.make_async_copy(some, some, send_sem).wait()
    pltpu.make_async_copy(few, few, cell_send_sem).wait()
    pltpu.make_async_copy(rest, rest, pass_send_sem).wait()


def unpack(packed, gal_out, pos_out, vel_out):
    bodies, stars = gal_out.shape[1], pos_out.shape[1]
    gal_out[...] = packed[:, 0:bodies]
    pos_out[...] = packed[:, bodies : bodies + stars]
    vel_out[...] = packed[:, bodies + LANES : bodies + LANES + stars]


def body(
    n_wide,
    n_narrow,
    star_pos,
    star_vel,
    star_mass,
    star_acc,
    star_jerk,
    gal_pos,
    gal_vel,
    gal_mass,
    group_of,
    let_send,
    star_leaf,
):
    stars, bodies = star_pos.shape[1], gal_pos.shape[1]
    vmem = pl.BlockSpec(memory_space=pltpu.VMEM)
    f32 = jnp.float32
    i32 = jnp.int32
    hbm = pl.BlockSpec(memory_space=pltpu.HBM)
    packed = pl.pallas_call(
        functools.partial(kernel, n_wide, n_narrow),
        out_shape=jax.ShapeDtypeStruct((3, bodies + 2 * LANES), f32),
        in_specs=[hbm] * 11,
        out_specs=vmem,
        scratch_shapes=[
            pltpu.VMEM((3, stars), f32),
            pltpu.VMEM((3, stars), f32),
            pltpu.VMEM((1, stars), f32),
            pltpu.VMEM((3, stars), f32),
            pltpu.VMEM((3, stars), f32),
            pltpu.VMEM((3, bodies), f32),
            pltpu.VMEM((3, bodies), f32),
            pltpu.VMEM((1, bodies), f32),
            pltpu.VMEM((1, bodies), i32),
            pltpu.VMEM((1, n_wide), i32),
            pltpu.SMEM(star_leaf.shape, i32),
            pltpu.SemaphoreType.DMA((11,)),
            pltpu.VMEM((n_narrow, n_wide, 4, LANES), f32),
            pltpu.VMEM((ROWS, LANES), f32),
            pltpu.VMEM((n_wide, 1, LANES), f32),
            pltpu.VMEM((n_wide, 1, LANES), f32),
            pltpu.VMEM((32, bodies), jnp.bfloat16),
            pltpu.VMEM((n_wide * stars, ROWS), f32),
            pltpu.VMEM((n_narrow, ROWS, LANES), f32),
            pltpu.VMEM((stars // ROWS, 6, ROWS, LANES), f32),
            pltpu.VMEM((4 * bodies // LANES, ROWS, LANES), f32),
            pltpu.VMEM((stars // ROWS, 6, ROWS, LANES), f32),
            pltpu.SemaphoreType.DMA,
            pltpu.SemaphoreType.DMA((n_wide,)),
            pltpu.SemaphoreType.DMA,
            pltpu.SemaphoreType.DMA((n_wide,)),
            pltpu.SemaphoreType.DMA,
            pltpu.SemaphoreType.DMA((n_wide,)),
            pltpu.SemaphoreType.REGULAR((n_wide,)),
        ],
        compiler_params=pltpu.CompilerParams(
            collective_id=0, has_side_effects=True, vmem_limit_bytes=24 << 20
        ),
    )(
        *(
            pltpu.with_memory_space_constraint(array, pltpu.HBM)
            for array in (
                star_pos,
                star_vel,
                star_mass.reshape(1, stars),
                star_acc,
                star_jerk,
                gal_pos,
                gal_vel,
                gal_mass.reshape(1, bodies),
                group_of.reshape(1, bodies),
                let_send.reshape(1, n_wide),
                star_leaf,
            )
        )
    )
    return pl.pallas_call(
        unpack,
        out_shape=(
            jax.ShapeDtypeStruct(gal_vel.shape, f32),
            jax.ShapeDtypeStruct(star_pos.shape, f32),
            jax.ShapeDtypeStruct(star_vel.shape, f32),
        ),
        in_specs=[vmem],
        out_specs=(vmem,) * 3,
        compiler_params=pltpu.CompilerParams(vmem_limit_bytes=1 << 20),
    )(packed)


def solution(mesh):
    both = ("wide", "narrow")
    columns, flat = P(None, both), P(both)
    return jax.shard_map(
        functools.partial(body, mesh.shape["wide"], mesh.shape["narrow"]),
        mesh=mesh,
        in_specs=(
            columns,
            columns,
            flat,
            columns,
            columns,
            columns,
            columns,
            flat,
            flat,
            P(both, None, None),
            P(both, None),
        ),
        out_specs=(columns, columns, columns),
        check_vma=False,
    )
```

```python
import functools

import jax
import jax.numpy as jnp
from jax import lax
from jax.experimental import pallas as pl
from jax.experimental.pallas import tpu as pltpu
from jax.sharding import PartitionSpec as P

GROUPS = 32
LANES = 128
ROWS = 8
MESH = pl.DeviceIdType.MESH

time_step = 0.25
soften_sq = 0.05


def loop(count, step, init, most=4):
    unroll = next(u for u in range(min(most, count), 0, -1) if count % u == 0)
    return lax.fori_loop(0, count, step, init, unroll=unroll)


def spread(row):
    return jnp.broadcast_to(row, (ROWS, row.shape[1]))


def column(block, index):
    return jnp.broadcast_to(block[:, index : index + 1], (ROWS, LANES))


def pull(source, mass, target, total):
    dx, dy, dz = (s - t for s, t in zip(source, target))
    inverse = lax.rsqrt(dx * dx + dy * dy + dz * dz + soften_sq)
    weight = mass * inverse * inverse * inverse
    return (total[0] + dx * weight, total[1] + dy * weight, total[2] + dz * weight)


def norm(rows):
    return rows[0:1] * rows[0:1] + rows[1:2] * rows[1:2] + rows[2:3] * rows[2:3]


def split(value):
    parts = []
    for _ in range(3):
        parts.append(value.astype(jnp.bfloat16).astype(jnp.float32))
        value = value - parts[-1]
    return parts


def kernel(
    n_wide,
    n_narrow,
    star_pos_hbm,
    star_vel_hbm,
    star_mass_hbm,
    star_acc_hbm,
    star_jerk_hbm,
    gal_pos_hbm,
    gal_vel_hbm,
    gal_mass_hbm,
    group_of_hbm,
    let_send_hbm,
    star_leaf_hbm,
    out,
    star_pos,
    star_vel,
    star_mass,
    star_acc,
    star_jerk,
    gal_pos,
    gal_vel,
    gal_mass,
    group_of,
    let_send,
    star_leaf,
    in_sem,
    states,
    cell_own,
    cell_out,
    cell_in,
    aimed,
    cols,
    srow,
    aims,
    body_sum,
    star_sum,
    send_sem,
    near_sem,
    cell_send_sem,
    cell_recv_sem,
    pass_send_sem,
    pass_recv_sem,
    enter_sem,
):
    wide, narrow = lax.axis_index("wide"), lax.axis_index("narrow")
    stars = star_pos.shape[1]
    bodies = gal_pos.shape[1]
    leaves, kicks = star_leaf.shape
    slots = LANES // GROUPS
    step_sq = time_step * time_step
    tiles = bodies // LANES
    every = tuple(range(tiles))

    fetches = [
        pltpu.make_async_copy(source, target, in_sem.at[i])
        for i, (source, target) in enumerate(
            (
                (star_pos_hbm, star_pos),
                (star_vel_hbm, star_vel),
                (star_mass_hbm, star_mass),
                (star_acc_hbm, star_acc),
                (star_jerk_hbm, star_jerk),
                (gal_pos_hbm, gal_pos),
                (gal_vel_hbm, gal_vel),
                (gal_mass_hbm, gal_mass),
                (group_of_hbm, group_of),
                (let_send_hbm, let_send),
                (star_leaf_hbm, star_leaf),
            )
        )
    ]
    for fetch in fetches:
        fetch.start()

    barrier = pltpu.get_barrier_semaphore()
    others = [lax.rem(narrow + m, n_narrow) for m in range(1, n_narrow)]

    def run(first, last, step):
        def body(i, carry):
            step(i)
            return carry

        lax.fori_loop(first, last, body, 0)

    def signal(sem, w, n):
        pl.semaphore_signal(sem, inc=1, device_id=(w, n), device_id_type=MESH)

    def signal_group(sem, w):
        for n in range(n_narrow):
            signal(sem, w, n)

    run(narrow + 1, n_narrow, lambda n: signal(barrier, wide, n))
    run(wide + 1, n_wide, lambda w: signal_group(barrier, w))

    lane = lax.broadcasted_iota(jnp.int32, (1, LANES), 1)
    lane4 = lax.broadcasted_iota(jnp.int32, (4, LANES), 1)
    lane8 = lax.broadcasted_iota(jnp.int32, (ROWS, LANES), 1)
    row8 = lax.broadcasted_iota(jnp.int32, (ROWS, LANES), 0)
    left = lane4 < stars

    for fetch in fetches[:5]:
        fetch.wait()

    spos, svel = star_pos[...], star_vel[...]
    sacc, sjerk = star_acc[...], star_jerk[...]
    pred_pos = (
        spos + time_step * svel + step_sq * 0.5 * sacc + step_sq * time_step / 6.0 * sjerk
    )
    pred_vel = svel + time_step * sacc + step_sq * 0.5 * sjerk
    pos4 = jnp.concatenate([pred_pos, star_mass[...]], axis=0)
    vel4 = jnp.concatenate([pred_vel, jnp.zeros((1, stars), jnp.float32)], axis=0)
    block = jnp.concatenate([pos4, vel4], axis=1)
    block = jnp.where(lax.rem(wide, 2) == 0, block, pltpu.roll(block, stars, 1))
    states[narrow, wide] = block

    def send_state(w, n, sends, recvs):
        pltpu.make_async_remote_copy(
            src_ref=states.at[narrow, wide],
            dst_ref=states.at[narrow, wide],
            send_sem=sends,
            recv_sem=recvs.at[wide],
            device_id=(w, n),
            device_id_type=MESH,
        ).start()

    def send_group(w):
        send_state(w, narrow, send_sem, near_sem)
        for n in others:
            send_state(w, n, pass_send_sem, pass_recv_sem)

    def send_beside(n):
        send_state(wide, n, pass_send_sem, pass_recv_sem)

    def send_cells(w):
        pltpu.make_async_remote_copy(
            src_ref=cell_out.at[w],
            dst_ref=cell_in.at[wide],
            send_sem=cell_send_sem,
            recv_sem=cell_recv_sem.at[wide],
            device_id=(w, narrow),
            device_id_type=MESH,
        ).start()

    group = lane // GROUPS

    def meet():
        smaller = wide * n_narrow + narrow

        @pl.when(smaller > 0)
        def _():
            pl.semaphore_wait(barrier, smaller)


        def send_down(w):
            send_group(w)

            @pl.when(cells_first)
            def _():
                send_cells(w)

        one = jnp.minimum(wide, 1)
        run(0, one, send_down)
        run(0, wide, lambda w: signal_group(enter_sem.at[wide], w))
        run(0, narrow, lambda n: signal(enter_sem.at[wide], wide, n))
        run(one, wide, send_down)
        run(0, narrow, send_beside)

    def make_cells():
        for fetch in fetches[5:]:
            fetch.wait()
        gpos, gmass = gal_pos[...], gal_mass[...]
        body_lane = lax.broadcasted_iota(jnp.int32, (1, bodies), 1)
        segment = group_of[...] + (body_lane // (bodies // leaves)) * GROUPS
        onehot = (
            lax.broadcasted_iota(jnp.int32, (LANES, bodies), 0)
            == jnp.broadcast_to(segment, (LANES, bodies))
        ).astype(jnp.bfloat16)
        moments = jnp.concatenate(
            [gpos * gmass, gmass, jnp.zeros((4, bodies), jnp.float32)], axis=0
        )
        sums = lax.dot_general(
            jnp.concatenate(split(moments), axis=0).astype(jnp.bfloat16),
            onehot,
            (((1,), (1,)), ((), ())),
            preferred_element_type=jnp.float32,
        )
        sums = sums[0:8] + sums[8:16] + sums[16:24]
        cells = jnp.where(row8 < 3, sums / spread(sums[3:4]), sums)
        cell_own[...] = cells

        part = jnp.bitwise_and(group - lax.rem(wide, slots), slots - 1)
        square = (n_wide, n_wide)
        diagonal = lax.broadcasted_iota(jnp.int32, square, 0) == lax.broadcasted_iota(
            jnp.int32, square, 1
        )
        listed = jnp.broadcast_to(let_send[...].astype(jnp.float32), square)
        chosen = jnp.sum(jnp.where(diagonal, listed, 0.0), axis=1, keepdims=True)
        chosen = jnp.broadcast_to(chosen, (n_wide, LANES)).astype(jnp.int32)
        outgoing = jnp.zeros((n_wide, LANES), jnp.float32)
        pick = jnp.bitwise_and(group - chosen, slots - 1)
        for k in range(slots):
            turned = cells if k == 0 else pltpu.roll(cells, k * GROUPS, 1)
            base = jnp.zeros((1, LANES), jnp.float32)
            for c in range(4):
                base = jnp.where(part == c, turned[c : c + 1], base)
            outgoing = jnp.where(
                jnp.logical_and(pick == k, chosen >= 0),
                jnp.broadcast_to(base, (n_wide, LANES)),
                outgoing,
            )
        cell_out[:, 0, :] = outgoing
        cell_in[wide] = jnp.zeros((1, LANES), jnp.float32)

    cells_first = jnp.logical_or(lax.rem(wide, 2) == 0, narrow < n_narrow // 2)

    def order(i):
        @pl.when(jnp.equal(i == 0, cells_first))
        def _():
            make_cells()

        @pl.when(jnp.not_equal(i == 0, cells_first))
        def _():
            meet()

    run(0, 2, order)

    @pl.when(jnp.logical_not(cells_first))
    def _():
        run(0, wide, send_cells)

    gpos, gmass = gal_pos[...], gal_mass[...]

    both = jnp.concatenate([pos4, vel4], axis=0)
    targets = jnp.transpose(
        jnp.concatenate([both, jnp.zeros((ROWS, LANES - stars), jnp.float32)], axis=1)
    )
    zero = jnp.zeros((ROWS, LANES), jnp.float32)

    own = [spread(cell_own[c : c + 1, :]) for c in range(4)]
    star_groups = stars // ROWS
    for t in range(star_groups):
        mine = targets[t * ROWS : (t + 1) * ROWS, :]
        place = [column(mine, c) for c in range(3)]
        for c in range(3):
            aims[t, c] = place[c]
            aims[t, 3 + c] = column(mine, 4 + c)
            star_sum[t, 3 + c] = zero
        for c, value in enumerate(pull(own[:3], own[3], place, (zero,) * 3)):
            star_sum[t, c] = value

    last4 = lax.broadcasted_iota(jnp.int32, (4, bodies), 0) == 3
    high, mid, low = split(jnp.concatenate([-2.0 * gpos, jnp.zeros_like(gmass)], axis=0))
    high = jnp.where(last4, 1.0, high)
    reach = split(norm(gpos) + soften_sq)
    blank = jnp.zeros_like(gmass)
    aimed[...] = jnp.concatenate(
        [high, mid, high, low, high, mid, *reach, blank, blank, blank, blank, blank],
        axis=0,
    ).astype(jnp.bfloat16)

    def on_bodies(rows, total):
        square = norm(rows[0:3])
        high, mid, low = split(jnp.concatenate([rows[0:3], square], axis=0))
        ones = jnp.ones((4, LANES), jnp.float32)
        turned = jnp.transpose(
            jnp.concatenate([high, high, mid, high, low, mid, ones, rows], axis=0)
        )
        reach = jnp.dot(
            turned.astype(jnp.bfloat16), aimed[...], preferred_element_type=jnp.float32
        )
        total = [list(part) for part in total]
        for g in range(LANES // ROWS):
            mine = turned[g * ROWS : (g + 1) * ROWS, :]
            place = [column(mine, 28 + c) for c in range(3)]
            mass = column(mine, 31)
            for t in every:
                inverse = lax.rsqrt(
                    reach[g * ROWS : (g + 1) * ROWS, t * LANES : (t + 1) * LANES]
                )
                weight = mass * inverse * (inverse * inverse)
                for c in range(3):
                    total[t][c] = total[t][c] + place[c] * weight
                total[t][3] = total[t][3] + weight
        return total

    def keep(total):
        for t in every:
            for c in range(4):
                body_sum[4 * t + c] = total[t][c]

    def kept():
        return [[body_sum[4 * t + c] for c in range(4)] for t in every]

    def cells_on_stars(rows, t):
        place = [aims[t, c] for c in range(3)]
        return pull(rows[:3], rows[3], place, [star_sum[t, c] for c in range(3)])

    total = [[zero] * 4 for _ in every]
    for t in every:
        tile = slice(t * LANES, (t + 1) * LANES)
        total = on_bodies(jnp.concatenate([gpos[:, tile], gmass[:, tile]], axis=0), total)
    keep(total)

    def answer(w):
        @pl.when(w == wide)
        def _():
            @pl.when(narrow < n_narrow - 1)
            def _():
                pl.semaphore_wait(enter_sem.at[wide], n_narrow - 1 - narrow)

            run(narrow + 1, n_narrow, send_beside)

        @pl.when(w > wide)
        def _():
            pl.semaphore_wait(enter_sem.at[w], n_narrow)
            send_group(w)
            send_cells(w)

    halves = n_wide // 2
    lower = wide < n_wide // 4


    def gather(n, even):
        even_block, odd_block = states[n, even], states[n, even + 1]
        rows = jnp.where(left, even_block, odd_block)
        speeds = pltpu.roll(jnp.where(left, odd_block, even_block), stars, 1)
        return rows, speeds

    def arrived(ref, sem, w):
        @pl.when(w != wide)
        def _():
            pltpu.make_async_copy(ref, ref, sem.at[w]).wait()

    def near_stars(even, total):
        near, _ = gather(narrow, even)
        if kicks == n_wide:
            return on_bodies(near, total)
        padded = jnp.concatenate([near, jnp.zeros((4, LANES), jnp.float32)], axis=0)
        cols[pl.ds(pl.multiple_of(even * stars, LANES), LANES), :] = jnp.transpose(padded)
        return total

    def near_cells(e, total):
        parts = []
        for c in range(4):
            row = jnp.zeros((1, LANES), jnp.float32)
            for k in range(slots):
                row = jnp.where(group == (c + k) % slots, cell_in[e * slots + k], row)
            parts.append(row if c == 0 else pltpu.roll(row, LANES - c * GROUPS, 1))
        rows = [spread(part) for part in parts]
        for t in range(star_groups):
            for c, value in enumerate(cells_on_stars(rows, t)):
                star_sum[t, c] = value
        return on_bodies(jnp.concatenate(parts, axis=0), total)

    def near_arrived(even):
        for w in (even, even + 1):
            arrived(states.at[0, 0], near_sem, w)

    def rest_arrived(even):
        for w in (even, even + 1):
            few = states.at[pl.ds(0, n_narrow - 1), 0]
            pltpu.make_async_copy(few, few, pass_recv_sem.at[w]).wait()

    def all_stars(even, take):
        for n in range(n_narrow):
            rows, speeds = gather(n, even)
            srow[n, 0:4, :] = rows
            srow[n, 4:8, :] = speeds
        sources = [
            [spread(srow[n, c : c + 1, :]) for c in range(7)] for n in range(n_narrow)
        ]
        for t in range(star_groups):
            place = [aims[t, c] for c in range(3)]
            speed = [aims[t, 3 + c] for c in range(3)]
            acc = [star_sum[t, c] for c in range(6)]
            for rows in sources:
                dx, dy, dz = (rows[c] - place[c] for c in range(3))
                ux, uy, uz = (rows[4 + c] - speed[c] for c in range(3))
                inverse = lax.rsqrt(dx * dx + dy * dy + dz * dz + soften_sq)
                square = inverse * inverse
                weight = rows[3] * inverse * square
                approach = 3.0 * (dx * ux + dy * uy + dz * uz) * square
                acc = [
                    acc[0] + dx * weight,
                    acc[1] + dy * weight,
                    acc[2] + dz * weight,
                    acc[3] + (ux - dx * approach) * weight,
                    acc[4] + (uy - dy * approach) * weight,
                    acc[5] + (uz - dz * approach) * weight,
                ]
            take(t, acc)

    def store(t, acc):
        for c in range(6):
            star_sum[t, c] = acc[c]

    pairs_per_row = slots // 2

    def nearby(q):
        e = q // pairs_per_row
        for k in range(slots):
            arrived(cell_in.at[0], cell_recv_sem, e * slots + k)
        return near_cells(e, near_stars(2 * q, kept()))

    first = wide < n_wide // 8

    def turn(p):
        run(
            jnp.where(p == 0, wide, jnp.where(first, 2 * p + 2, n_wide)),
            jnp.where(first, jnp.minimum(2 * p + 4, n_wide), n_wide),
            answer,
        )
        q = jnp.where(lower, p, halves - 1 - p)
        near_arrived(2 * q)
        second = lax.rem(p, pairs_per_row) == pairs_per_row - 1

        @pl.when(second)
        def _():
            keep(nearby(q))
            rest_arrived(2 * q)
            all_stars(2 * q, store)

        @pl.when(jnp.logical_not(second))
        def _():
            rest_arrived(2 * q)
            keep(near_stars(2 * q, kept()))
            all_stars(2 * q, store)

    run(0, halves - 1, turn)

    last = 2 * jnp.where(lower, halves - 1, 0)
    near_arrived(last)
    total = nearby(last // 2)
    for t in every:
        tile = slice(t * LANES, (t + 1) * LANES)
        near = [gpos[c : c + 1, tile] for c in range(3)]
        pieces = [jnp.sum(part, axis=0, keepdims=True) for part in total[t]]
        pieces = [pieces[c] - near[c] * pieces[3] for c in range(3)]
        if kicks != n_wide:
            here = [spread(row) for row in near]

            def kick(k, acc):
                listed = star_leaf[t * leaves // tiles, k]

                def some(g, acc):
                    at = pl.multiple_of(listed * stars + g * ROWS, ROWS)
                    source = cols[pl.ds(at, ROWS), :]
                    place = [column(source, c) for c in range(3)]
                    return pull(place, column(source, 3), here, acc)

                return loop(stars // ROWS, some, acc)

            kicked = lax.fori_loop(0, kicks, kick, (zero,) * 3)
            for c in range(3):
                pieces[c] = pieces[c] + jnp.sum(kicked[c], axis=0, keepdims=True)
        for c in range(3):
            out[c : c + 1, tile] = gal_vel[c : c + 1, tile] + time_step * pieces[c]

    pieces = []

    def finish(t, acc):
        piece = jnp.zeros((ROWS, LANES), jnp.float32)
        for c in range(6):
            piece = jnp.where(lane8 == c, jnp.sum(acc[c], axis=1, keepdims=True), piece)
        pieces.append(piece)

    rest_arrived(last)
    all_stars(last, finish)
    result = jnp.transpose(jnp.concatenate(pieces, axis=0))
    new_acc, new_jerk = result[0:3], result[3:6]
    vel_new = (
        svel + time_step * 0.5 * (sacc + new_acc) + step_sq / 12.0 * (sjerk - new_jerk)
    )
    vel_at = bodies + LANES
    out[:, vel_at : vel_at + stars] = vel_new
    out[:, bodies : bodies + stars] = (
        spos + time_step * 0.5 * (svel + vel_new) + step_sq / 12.0 * (sacc - new_acc)
    )

    some = states.at[0, pl.ds(0, n_wide - 1)]
    few = cell_in.at[pl.ds(0, n_wide - 1)]
    rest = states.at[pl.ds(0, n_narrow - 1)]
    pltpu.make_async_copy(some, some, send_sem).wait()
    pltpu.make_async_copy(few, few, cell_send_sem).wait()
    pltpu.make_async_copy(rest, rest, pass_send_sem).wait()


def unpack(packed, gal_out, pos_out, vel_out):
    bodies, stars = gal_out.shape[1], pos_out.shape[1]
    gal_out[...] = packed[:, 0:bodies]
    pos_out[...] = packed[:, bodies : bodies + stars]
    vel_out[...] = packed[:, bodies + LANES : bodies + LANES + stars]


def body(
    n_wide,
    n_narrow,
    star_pos,
    star_vel,
    star_mass,
    star_acc,
    star_jerk,
    gal_pos,
    gal_vel,
    gal_mass,
    group_of,
    let_send,
    star_leaf,
):
    stars, bodies = star_pos.shape[1], gal_pos.shape[1]
    vmem = pl.BlockSpec(memory_space=pltpu.VMEM)
    f32 = jnp.float32
    i32 = jnp.int32
    hbm = pl.BlockSpec(memory_space=pltpu.HBM)
    packed = pl.pallas_call(
        functools.partial(kernel, n_wide, n_narrow),
        out_shape=jax.ShapeDtypeStruct((3, bodies + 2 * LANES), f32),
        in_specs=[hbm] * 11,
        out_specs=vmem,
        scratch_shapes=[
            pltpu.VMEM((3, stars), f32),
            pltpu.VMEM((3, stars), f32),
            pltpu.VMEM((1, stars), f32),
            pltpu.VMEM((3, stars), f32),
            pltpu.VMEM((3, stars), f32),
            pltpu.VMEM((3, bodies), f32),
            pltpu.VMEM((3, bodies), f32),
            pltpu.VMEM((1, bodies), f32),
            pltpu.VMEM((1, bodies), i32),
            pltpu.VMEM((1, n_wide), i32),
            pltpu.SMEM(star_leaf.shape, i32),
            pltpu.SemaphoreType.DMA((11,)),
            pltpu.VMEM((n_narrow, n_wide, 4, LANES), f32),
            pltpu.VMEM((ROWS, LANES), f32),
            pltpu.VMEM((n_wide, 1, LANES), f32),
            pltpu.VMEM((n_wide, 1, LANES), f32),
            pltpu.VMEM((32, bodies), jnp.bfloat16),
            pltpu.VMEM((n_wide * stars, ROWS), f32),
            pltpu.VMEM((n_narrow, ROWS, LANES), f32),
            pltpu.VMEM((stars // ROWS, 6, ROWS, LANES), f32),
            pltpu.VMEM((4 * bodies // LANES, ROWS, LANES), f32),
            pltpu.VMEM((stars // ROWS, 6, ROWS, LANES), f32),
            pltpu.SemaphoreType.DMA,
            pltpu.SemaphoreType.DMA((n_wide,)),
            pltpu.SemaphoreType.DMA,
            pltpu.SemaphoreType.DMA((n_wide,)),
            pltpu.SemaphoreType.DMA,
            pltpu.SemaphoreType.DMA((n_wide,)),
            pltpu.SemaphoreType.REGULAR((n_wide,)),
        ],
        compiler_params=pltpu.CompilerParams(
            collective_id=0, has_side_effects=True, vmem_limit_bytes=24 << 20
        ),
    )(
        *(
            pltpu.with_memory_space_constraint(array, pltpu.HBM)
            for array in (
                star_pos,
                star_vel,
                star_mass.reshape(1, stars),
                star_acc,
                star_jerk,
                gal_pos,
                gal_vel,
                gal_mass.reshape(1, bodies),
                group_of.reshape(1, bodies),
                let_send.reshape(1, n_wide),
                star_leaf,
            )
        )
    )
    return pl.pallas_call(
        unpack,
        out_shape=(
            jax.ShapeDtypeStruct(gal_vel.shape, f32),
            jax.ShapeDtypeStruct(star_pos.shape, f32),
            jax.ShapeDtypeStruct(star_vel.shape, f32),
        ),
        in_specs=[vmem],
        out_specs=(vmem,) * 3,
        compiler_params=pltpu.CompilerParams(vmem_limit_bytes=1 << 20),
    )(packed)


def solution(mesh):
    both = ("wide", "narrow")
    columns, flat = P(None, both), P(both)
    return jax.shard_map(
        functools.partial(body, mesh.shape["wide"], mesh.shape["narrow"]),
        mesh=mesh,
        in_specs=(
            columns,
            columns,
            flat,
            columns,
            columns,
            columns,
            columns,
            flat,
            flat,
            P(both, None, None),
            P(both, None),
        ),
        out_specs=(columns, columns, columns),
        check_vma=False,
    )
```

```python
import functools

import jax
import jax.numpy as jnp
from jax import lax
from jax.experimental import pallas as pl
from jax.experimental.pallas import tpu as pltpu
from jax.sharding import PartitionSpec as P

GROUPS = 32
LANES = 128
ROWS = 8
MESH = pl.DeviceIdType.MESH

time_step = 0.25
soften_sq = 0.05


def loop(count, step, init, most=4):
    unroll = next(u for u in range(min(most, count), 0, -1) if count % u == 0)
    return lax.fori_loop(0, count, step, init, unroll=unroll)


def spread(row):
    return jnp.broadcast_to(row, (ROWS, row.shape[1]))


def column(block, index):
    return jnp.broadcast_to(block[:, index : index + 1], (ROWS, LANES))


def pull(source, mass, target, total):
    dx, dy, dz = (s - t for s, t in zip(source, target))
    inverse = lax.rsqrt(dx * dx + dy * dy + dz * dz + soften_sq)
    weight = mass * inverse * inverse * inverse
    return (total[0] + dx * weight, total[1] + dy * weight, total[2] + dz * weight)


def norm(rows):
    return rows[0:1] * rows[0:1] + rows[1:2] * rows[1:2] + rows[2:3] * rows[2:3]


def split(value):
    parts = []
    for _ in range(3):
        parts.append(value.astype(jnp.bfloat16).astype(jnp.float32))
        value = value - parts[-1]
    return parts


def kernel(
    n_wide,
    n_narrow,
    star_pos_hbm,
    star_vel_hbm,
    star_mass_hbm,
    star_acc_hbm,
    star_jerk_hbm,
    gal_pos_hbm,
    gal_vel_hbm,
    gal_mass_hbm,
    group_of_hbm,
    let_send_hbm,
    star_leaf_hbm,
    out,
    star_in,
    star_mass,
    gal_in,
    masses,
    group_of,
    let_send,
    star_leaf,
    in_sem,
    states,
    cell_own,
    cell_out,
    cell_in,
    aimed,
    cols,
    srow,
    aims,
    body_sum,
    star_sum,
    send_sem,
    near_sem,
    pass_sem,
    cell_send_sem,
    cell_recv_sem,
    enter_sem,
):
    wide, narrow = lax.axis_index("wide"), lax.axis_index("narrow")
    stars, bodies = star_in.shape[2], gal_in.shape[2]
    leaves, kicks = star_leaf.shape
    slots = LANES // GROUPS
    step_sq = time_step * time_step
    tiles = bodies // LANES
    every = tuple(range(tiles))

    fetches = [
        (star_pos_hbm, star_in.at[0], 0),
        (star_vel_hbm, star_in.at[1], 0),
        (star_acc_hbm, star_in.at[2], 0),
        (star_jerk_hbm, star_in.at[3], 0),
        (star_mass_hbm, star_mass, 1),
        (gal_pos_hbm, gal_in.at[0], 2),
        (gal_vel_hbm, gal_in.at[1], 2),
        (gal_mass_hbm, masses.at[0], 3),
        (group_of_hbm, group_of, 3),
        (let_send_hbm, let_send, 4),
    ]
    if kicks != n_wide:
        fetches.append((star_leaf_hbm, star_leaf, 5))
    for source, target, i in fetches:
        pltpu.make_async_copy(source, target, in_sem.at[i]).start()

    def fetched(*refs):
        for ref, i in refs:
            pltpu.make_async_copy(ref, ref, in_sem.at[i]).wait()

    barrier = pltpu.get_barrier_semaphore()
    others = [lax.rem(narrow + m, n_narrow) for m in range(1, n_narrow)]

    def run(first, last, step):
        def body(i, carry):
            step(i)
            return carry

        lax.fori_loop(first, last, body, 0)

    def signal(sem, w, n):
        pl.semaphore_signal(sem, inc=1, device_id=(w, n), device_id_type=MESH)

    def signal_group(sem, w):
        for n in range(n_narrow):
            signal(sem, w, n)

    run(narrow + 1, n_narrow, lambda n: signal(barrier, wide, n))
    run(wide + 1, n_wide, lambda w: signal_group(barrier, w))

    lane = lax.broadcasted_iota(jnp.int32, (1, LANES), 1)
    lane4 = lax.broadcasted_iota(jnp.int32, (4, LANES), 1)
    lane8 = lax.broadcasted_iota(jnp.int32, (ROWS, LANES), 1)
    row8 = lax.broadcasted_iota(jnp.int32, (ROWS, LANES), 0)
    left = lane4 < stars

    fetched((star_in, 0), (star_mass, 1))
    spos, svel, sacc, sjerk = (star_in[i] for i in range(4))
    pred_pos = (
        spos + time_step * svel + step_sq * 0.5 * sacc + step_sq * time_step / 6.0 * sjerk
    )
    pred_vel = svel + time_step * sacc + step_sq * 0.5 * sjerk
    pos4 = jnp.concatenate([pred_pos, star_mass[...]], axis=0)
    vel4 = jnp.concatenate([pred_vel, jnp.zeros((1, stars), jnp.float32)], axis=0)
    block = jnp.concatenate([pos4, vel4], axis=1)
    block = jnp.where(lax.rem(wide, 2) == 0, block, pltpu.roll(block, stars, 1))
    mine = narrow * n_wide + wide
    states[mine] = block

    def send_state(w, n, recvs):
        pltpu.make_async_remote_copy(
            src_ref=states.at[mine],
            dst_ref=states.at[mine],
            send_sem=send_sem,
            recv_sem=recvs.at[wide // 2],
            device_id=(w, n),
            device_id_type=MESH,
        ).start()

    def send_group(w):
        send_state(w, narrow, near_sem)
        for n in others:
            send_state(w, n, pass_sem)

    def send_beside(n):
        send_state(wide, n, pass_sem)

    def send_cells(w):
        pltpu.make_async_remote_copy(
            src_ref=cell_out.at[w],
            dst_ref=cell_in.at[wide],
            send_sem=cell_send_sem,
            recv_sem=cell_recv_sem.at[wide // slots],
            device_id=(w, narrow),
            device_id_type=MESH,
        ).start()

    group = lane // GROUPS

    def meet():
        smaller = wide * n_narrow + narrow

        @pl.when(smaller > 0)
        def _():
            pl.semaphore_wait(barrier, smaller)

        def send_down(w):
            send_group(w)

            @pl.when(cells_first)
            def _():
                send_cells(w)

        one = jnp.minimum(wide, 1)
        run(0, one, send_down)
        run(0, wide, lambda w: signal_group(enter_sem.at[wide // 2], w))
        run(0, narrow, lambda n: signal(enter_sem.at[wide // 2], wide, n))
        run(one, wide, send_down)
        run(0, narrow, send_beside)

    def make_cells():
        fetched((gal_in, 2), (masses, 3), (let_send, 4))
        if kicks != n_wide:
            fetched((star_leaf, 5))
        gpos, gmass = gal_in[0], masses[0]
        body_lane = lax.broadcasted_iota(jnp.int32, (1, bodies), 1)
        segment = group_of[...] + (body_lane // (bodies // leaves)) * GROUPS
        onehot = (
            lax.broadcasted_iota(jnp.int32, (LANES, bodies), 0)
            == jnp.broadcast_to(segment, (LANES, bodies))
        ).astype(jnp.bfloat16)
        moments = jnp.concatenate(
            [gpos * gmass, gmass, jnp.zeros((4, bodies), jnp.float32)], axis=0
        )
        sums = lax.dot_general(
            jnp.concatenate(split(moments), axis=0).astype(jnp.bfloat16),
            onehot,
            (((1,), (1,)), ((), ())),
            preferred_element_type=jnp.float32,
        )
        sums = sums[0:8] + sums[8:16] + sums[16:24]
        cells = jnp.where(row8 < 3, sums / spread(sums[3:4]), sums)
        cell_own[...] = cells

        part = jnp.bitwise_and(group - lax.rem(wide, slots), slots - 1)
        square = (n_wide, n_wide)
        diagonal = lax.broadcasted_iota(jnp.int32, square, 0) == lax.broadcasted_iota(
            jnp.int32, square, 1
        )
        listed = jnp.broadcast_to(let_send[...].astype(jnp.float32), square)
        chosen = jnp.sum(jnp.where(diagonal, listed, 0.0), axis=1, keepdims=True)
        chosen = jnp.broadcast_to(chosen, (n_wide, LANES)).astype(jnp.int32)
        outgoing = jnp.zeros((n_wide, LANES), jnp.float32)
        pick = jnp.bitwise_and(group - chosen, slots - 1)
        for k in range(slots):
            turned = cells if k == 0 else pltpu.roll(cells, k * GROUPS, 1)
            base = jnp.zeros((1, LANES), jnp.float32)
            for c in range(4):
                base = jnp.where(part == c, turned[c : c + 1], base)
            outgoing = jnp.where(
                jnp.logical_and(pick == k, chosen >= 0),
                jnp.broadcast_to(base, (n_wide, LANES)),
                outgoing,
            )
        cell_out[:, 0, :] = outgoing
        cell_in[wide] = jnp.zeros((1, LANES), jnp.float32)

    cells_first = jnp.logical_or(lax.rem(wide, 2) == 0, narrow < n_narrow // 2)

    def order(i):
        @pl.when(jnp.equal(i == 0, cells_first))
        def _():
            make_cells()

        @pl.when(jnp.not_equal(i == 0, cells_first))
        def _():
            meet()

    run(0, 2, order)

    @pl.when(jnp.logical_not(cells_first))
    def _():
        run(0, wide, send_cells)

    gpos, gmass = gal_in[0], masses[0]

    both = jnp.concatenate([pos4, vel4], axis=0)
    targets = jnp.transpose(
        jnp.concatenate([both, jnp.zeros((ROWS, LANES - stars), jnp.float32)], axis=1)
    )
    zero = jnp.zeros((ROWS, LANES), jnp.float32)

    own = [spread(cell_own[c : c + 1, :]) for c in range(4)]
    star_groups = stars // ROWS
    for t in range(star_groups):
        rows = targets[t * ROWS : (t + 1) * ROWS, :]
        place = [column(rows, c) for c in range(3)]
        for c in range(3):
            aims[t, c] = place[c]
            aims[t, 3 + c] = column(rows, 4 + c)
            star_sum[t, 3 + c] = zero
        for c, value in enumerate(pull(own[:3], own[3], place, (zero,) * 3)):
            star_sum[t, c] = value

    last4 = lax.broadcasted_iota(jnp.int32, (4, bodies), 0) == 3
    high, mid, low = split(jnp.concatenate([-2.0 * gpos, jnp.zeros_like(gmass)], axis=0))
    high = jnp.where(last4, 1.0, high)
    reach = split(norm(gpos) + soften_sq)
    blank = jnp.zeros_like(gmass)
    aimed[...] = jnp.concatenate(
        [high, mid, high, low, high, mid, *reach, blank, blank, blank, blank, blank],
        axis=0,
    ).astype(jnp.bfloat16)

    def on_bodies(rows, total):
        square = norm(rows[0:3])
        high, mid, low = split(jnp.concatenate([rows[0:3], square], axis=0))
        ones = jnp.ones((4, LANES), jnp.float32)
        turned = jnp.transpose(
            jnp.concatenate([high, high, mid, high, low, mid, ones, rows], axis=0)
        )
        reach = jnp.dot(
            turned.astype(jnp.bfloat16), aimed[...], preferred_element_type=jnp.float32
        )
        total = [list(part) for part in total]
        for g in range(LANES // ROWS):
            some = turned[g * ROWS : (g + 1) * ROWS, :]
            place = [column(some, 28 + c) for c in range(3)]
            mass = column(some, 31)
            for t in every:
                inverse = lax.rsqrt(
                    reach[g * ROWS : (g + 1) * ROWS, t * LANES : (t + 1) * LANES]
                )
                weight = mass * inverse * (inverse * inverse)
                for c in range(3):
                    total[t][c] = total[t][c] + place[c] * weight
                total[t][3] = total[t][3] + weight
        return total

    def keep(total):
        for t in every:
            for c in range(4):
                body_sum[4 * t + c] = total[t][c]

    def kept():
        return [[body_sum[4 * t + c] for c in range(4)] for t in every]

    def cells_on_stars(rows, t):
        place = [aims[t, c] for c in range(3)]
        return pull(rows[:3], rows[3], place, [star_sum[t, c] for c in range(3)])

    total = [[zero] * 4 for _ in every]
    for t in every:
        tile = slice(t * LANES, (t + 1) * LANES)
        total = on_bodies(jnp.concatenate([gpos[:, tile], gmass[:, tile]], axis=0), total)
    keep(total)

    def larger(w):
        rest = jnp.where(w == wide, n_narrow - 1 - narrow, 0)
        return jnp.where(w > wide, n_narrow, rest)

    def answer(q):
        count = larger(2 * q) + larger(2 * q + 1)

        @pl.when(count > 0)
        def _():
            pl.semaphore_wait(enter_sem.at[q], count)

        def to_group(w):
            @pl.when(w == wide)
            def _():
                run(narrow + 1, n_narrow, send_beside)

            @pl.when(w > wide)
            def _():
                send_group(w)
                send_cells(w)

        run(2 * q, 2 * q + 2, to_group)

    halves = n_wide // 2
    lower = wide < n_wide // 4


    def gather(n, even):
        even_block, odd_block = states[n * n_wide + even], states[n * n_wide + even + 1]
        rows = jnp.where(left, even_block, odd_block)
        speeds = pltpu.roll(jnp.where(left, odd_block, even_block), stars, 1)
        return rows, speeds

    def arrived(ref, size, sem, i):
        own = wide // size == i

        def wait(count):
            some = ref.at[pl.ds(0, count)]
            pltpu.make_async_copy(some, some, sem.at[i]).wait()

        @pl.when(own)
        def _():
            wait(size - 1)

        @pl.when(jnp.logical_not(own))
        def _():
            wait(size)

    def near_stars(even, total):
        near, _ = gather(narrow, even)
        if kicks == n_wide:
            return on_bodies(near, total)
        padded = jnp.concatenate([near, jnp.zeros((4, LANES), jnp.float32)], axis=0)
        cols[pl.ds(pl.multiple_of(even * stars, LANES), LANES), :] = jnp.transpose(padded)
        return total

    def near_cells(e, total):
        parts = []
        for c in range(4):
            row = jnp.zeros((1, LANES), jnp.float32)
            for k in range(slots):
                row = jnp.where(group == (c + k) % slots, cell_in[e * slots + k], row)
            parts.append(row if c == 0 else pltpu.roll(row, LANES - c * GROUPS, 1))
        rows = [spread(part) for part in parts]
        for t in range(star_groups):
            for c, value in enumerate(cells_on_stars(rows, t)):
                star_sum[t, c] = value
        return on_bodies(jnp.concatenate(parts, axis=0), total)

    def rest_arrived(q):
        some = states.at[pl.ds(0, 2 * (n_narrow - 1))]
        pltpu.make_async_copy(some, some, pass_sem.at[q]).wait()

    def all_stars(even, take):
        for n in range(n_narrow):
            rows, speeds = gather(n, even)
            srow[n, 0:4, :] = rows
            srow[n, 4:8, :] = speeds
        sources = [
            [spread(srow[n, c : c + 1, :]) for c in range(7)] for n in range(n_narrow)
        ]
        for t in range(star_groups):
            place = [aims[t, c] for c in range(3)]
            speed = [aims[t, 3 + c] for c in range(3)]
            acc = [star_sum[t, c] for c in range(6)]
            for rows in sources:
                dx, dy, dz = (rows[c] - place[c] for c in range(3))
                ux, uy, uz = (rows[4 + c] - speed[c] for c in range(3))
                inverse = lax.rsqrt(dx * dx + dy * dy + dz * dz + soften_sq)
                square = inverse * inverse
                weight = rows[3] * inverse * square
                approach = 3.0 * (dx * ux + dy * uy + dz * uz) * square
                acc = [
                    acc[0] + dx * weight,
                    acc[1] + dy * weight,
                    acc[2] + dz * weight,
                    acc[3] + (ux - dx * approach) * weight,
                    acc[4] + (uy - dy * approach) * weight,
                    acc[5] + (uz - dz * approach) * weight,
                ]
            take(t, acc)

    def store(t, acc):
        for c in range(6):
            star_sum[t, c] = acc[c]

    pairs_per_row = slots // 2

    def nearby(q):
        e = q // pairs_per_row
        arrived(cell_in, slots, cell_recv_sem, e)
        return near_cells(e, near_stars(2 * q, kept()))

    first = wide < n_wide // 8

    def turn(p):
        run(
            jnp.where(p == 0, wide // 2, jnp.where(first, p + 1, halves)),
            jnp.where(first, jnp.minimum(p + 2, halves), halves),
            answer,
        )
        q = jnp.where(lower, p, halves - 1 - p)
        arrived(states, 2, near_sem, q)
        second = lax.rem(p, pairs_per_row) == pairs_per_row - 1

        @pl.when(second)
        def _():
            keep(nearby(q))
            rest_arrived(q)
            all_stars(2 * q, store)

        @pl.when(jnp.logical_not(second))
        def _():
            rest_arrived(q)
            keep(near_stars(2 * q, kept()))
            all_stars(2 * q, store)

    run(0, halves - 1, turn)

    last = jnp.where(lower, halves - 1, 0)
    arrived(states, 2, near_sem, last)
    total = nearby(last)
    for t in every:
        tile = slice(t * LANES, (t + 1) * LANES)
        near = [gpos[c : c + 1, tile] for c in range(3)]
        pieces = [jnp.sum(part, axis=0, keepdims=True) for part in total[t]]
        pieces = [pieces[c] - near[c] * pieces[3] for c in range(3)]
        if kicks != n_wide:
            here = [spread(row) for row in near]

            def kick(k, acc):
                listed = star_leaf[t * leaves // tiles, k]

                def some(g, acc):
                    at = pl.multiple_of(listed * stars + g * ROWS, ROWS)
                    source = cols[pl.ds(at, ROWS), :]
                    place = [column(source, c) for c in range(3)]
                    return pull(place, column(source, 3), here, acc)

                return loop(stars // ROWS, some, acc)

            kicked = lax.fori_loop(0, kicks, kick, (zero,) * 3)
            for c in range(3):
                pieces[c] = pieces[c] + jnp.sum(kicked[c], axis=0, keepdims=True)
        for c in range(3):
            out[c : c + 1, tile] = gal_in[1, c : c + 1, tile] + time_step * pieces[c]

    pieces = []

    def finish(t, acc):
        piece = jnp.zeros((ROWS, LANES), jnp.float32)
        for c in range(6):
            piece = jnp.where(lane8 == c, jnp.sum(acc[c], axis=1, keepdims=True), piece)
        pieces.append(piece)

    rest_arrived(last)
    all_stars(2 * last, finish)
    result = jnp.transpose(jnp.concatenate(pieces, axis=0))
    new_acc, new_jerk = result[0:3], result[3:6]
    vel_new = (
        svel + time_step * 0.5 * (sacc + new_acc) + step_sq / 12.0 * (sjerk - new_jerk)
    )
    vel_at = bodies + LANES
    out[:, vel_at : vel_at + stars] = vel_new
    out[:, bodies : bodies + stars] = (
        spos + time_step * 0.5 * (svel + vel_new) + step_sq / 12.0 * (sacc - new_acc)
    )

    some = states.at[pl.ds(0, n_wide * n_narrow - 1)]
    pltpu.make_async_copy(some, some, send_sem).wait()
    few = cell_in.at[pl.ds(0, n_wide - 1)]
    pltpu.make_async_copy(few, few, cell_send_sem).wait()


def unpack(packed, gal_out, pos_out, vel_out):
    bodies, stars = gal_out.shape[1], pos_out.shape[1]
    gal_out[...] = packed[:, 0:bodies]
    pos_out[...] = packed[:, bodies : bodies + stars]
    vel_out[...] = packed[:, bodies + LANES : bodies + LANES + stars]


def body(
    n_wide,
    n_narrow,
    star_pos,
    star_vel,
    star_mass,
    star_acc,
    star_jerk,
    gal_pos,
    gal_vel,
    gal_mass,
    group_of,
    let_send,
    star_leaf,
):
    stars, bodies = star_pos.shape[1], gal_pos.shape[1]
    vmem = pl.BlockSpec(memory_space=pltpu.VMEM)
    f32 = jnp.float32
    i32 = jnp.int32
    hbm = pl.BlockSpec(memory_space=pltpu.HBM)
    packed = pl.pallas_call(
        functools.partial(kernel, n_wide, n_narrow),
        out_shape=jax.ShapeDtypeStruct((3, bodies + 2 * LANES), f32),
        in_specs=[hbm] * 11,
        out_specs=vmem,
        scratch_shapes=[
            pltpu.VMEM((4, 3, stars), f32),
            pltpu.VMEM((1, stars), f32),
            pltpu.VMEM((2, 3, bodies), f32),
            pltpu.VMEM((2, 1, bodies), f32),
            pltpu.VMEM((1, bodies), i32),
            pltpu.VMEM((1, n_wide), i32),
            pltpu.SMEM(star_leaf.shape, i32),
            pltpu.SemaphoreType.DMA((5 + (star_leaf.shape[1] != n_wide),)),
            pltpu.VMEM((n_narrow * n_wide, 4, LANES), f32),
            pltpu.VMEM((ROWS, LANES), f32),
            pltpu.VMEM((n_wide, 1, LANES), f32),
            pltpu.VMEM((n_wide, 1, LANES), f32),
            pltpu.VMEM((32, bodies), jnp.bfloat16),
            pltpu.VMEM((n_wide * stars, ROWS), f32),
            pltpu.VMEM((n_narrow, ROWS, LANES), f32),
            pltpu.VMEM((stars // ROWS, 6, ROWS, LANES), f32),
            pltpu.VMEM((4 * bodies // LANES, ROWS, LANES), f32),
            pltpu.VMEM((stars // ROWS, 6, ROWS, LANES), f32),
            pltpu.SemaphoreType.DMA,
            pltpu.SemaphoreType.DMA((n_wide // 2,)),
            pltpu.SemaphoreType.DMA((n_wide // 2,)),
            pltpu.SemaphoreType.DMA,
            pltpu.SemaphoreType.DMA((n_wide * GROUPS // LANES,)),
            pltpu.SemaphoreType.REGULAR((n_wide // 2,)),
        ],
        compiler_params=pltpu.CompilerParams(
            collective_id=0, has_side_effects=True, vmem_limit_bytes=24 << 20
        ),
    )(
        *(
            pltpu.with_memory_space_constraint(array, pltpu.HBM)
            for array in (
                star_pos,
                star_vel,
                star_mass.reshape(1, stars),
                star_acc,
                star_jerk,
                gal_pos,
                gal_vel,
                gal_mass.reshape(1, bodies),
                group_of.reshape(1, bodies),
                let_send.reshape(1, n_wide),
                star_leaf,
            )
        )
    )
    return pl.pallas_call(
        unpack,
        out_shape=(
            jax.ShapeDtypeStruct(gal_vel.shape, f32),
            jax.ShapeDtypeStruct(star_pos.shape, f32),
            jax.ShapeDtypeStruct(star_vel.shape, f32),
        ),
        in_specs=[vmem],
        out_specs=(vmem,) * 3,
        compiler_params=pltpu.CompilerParams(vmem_limit_bytes=1 << 20),
    )(packed)


def solution(mesh):
    both = ("wide", "narrow")
    columns, flat = P(None, both), P(both)
    return jax.shard_map(
        functools.partial(body, mesh.shape["wide"], mesh.shape["narrow"]),
        mesh=mesh,
        in_specs=(
            columns,
            columns,
            flat,
            columns,
            columns,
            columns,
            columns,
            flat,
            flat,
            P(both, None, None),
            P(both, None),
        ),
        out_specs=(columns, columns, columns),
        check_vma=False,
    )
```

```python
import functools

import jax
import jax.numpy as jnp
from jax import lax
from jax.experimental import pallas as pl
from jax.experimental.pallas import tpu as pltpu
from jax.sharding import PartitionSpec as P

GROUPS = 32
LANES = 128
ROWS = 8
MESH = pl.DeviceIdType.MESH

time_step = 0.25
soften_sq = 0.05


def loop(count, step, init, most=4):
    unroll = next(u for u in range(min(most, count), 0, -1) if count % u == 0)
    return lax.fori_loop(0, count, step, init, unroll=unroll)


def spread(row):
    return jnp.broadcast_to(row, (ROWS, row.shape[1]))


def column(block, index):
    return jnp.broadcast_to(block[:, index : index + 1], (ROWS, LANES))


def pull(source, mass, target, total):
    dx, dy, dz = (s - t for s, t in zip(source, target))
    inverse = lax.rsqrt(dx * dx + dy * dy + dz * dz + soften_sq)
    weight = mass * inverse * inverse * inverse
    return (total[0] + dx * weight, total[1] + dy * weight, total[2] + dz * weight)


def norm(rows):
    return rows[0:1] * rows[0:1] + rows[1:2] * rows[1:2] + rows[2:3] * rows[2:3]


def split(value):
    parts = []
    for _ in range(3):
        parts.append(value.astype(jnp.bfloat16).astype(jnp.float32))
        value = value - parts[-1]
    return parts


def kernel(
    n_wide,
    n_narrow,
    star_pos_hbm,
    star_vel_hbm,
    star_mass_hbm,
    star_acc_hbm,
    star_jerk_hbm,
    gal_pos_hbm,
    gal_vel_hbm,
    gal_mass_hbm,
    group_of_hbm,
    let_send_hbm,
    star_leaf_hbm,
    out,
    star_in,
    star_mass,
    gal_in,
    masses,
    group_of,
    let_send,
    star_leaf,
    in_sem,
    states,
    cell_own,
    cell_out,
    cell_in,
    aimed,
    cols,
    srow,
    aims,
    body_sum,
    star_sum,
    send_sem,
    near_sem,
    pass_sem,
    enter_sem,
):
    wide, narrow = lax.axis_index("wide"), lax.axis_index("narrow")
    stars, bodies = star_in.shape[2], gal_in.shape[2]
    leaves, kicks = star_leaf.shape
    slots = LANES // GROUPS
    step_sq = time_step * time_step
    tiles = bodies // LANES
    every = tuple(range(tiles))

    fetches = [
        (star_pos_hbm, star_in.at[0], 0),
        (star_vel_hbm, star_in.at[1], 0),
        (star_acc_hbm, star_in.at[2], 0),
        (star_jerk_hbm, star_in.at[3], 0),
        (star_mass_hbm, star_mass, 1),
        (gal_pos_hbm, gal_in.at[0], 2),
        (gal_vel_hbm, gal_in.at[1], 2),
        (gal_mass_hbm, masses.at[0], 3),
        (group_of_hbm, group_of, 3),
        (let_send_hbm, let_send, 4),
    ]
    if kicks != n_wide:
        fetches.append((star_leaf_hbm, star_leaf, 5))
    for source, target, i in fetches:
        pltpu.make_async_copy(source, target, in_sem.at[i]).start()

    def fetched(*refs):
        for ref, i in refs:
            pltpu.make_async_copy(ref, ref, in_sem.at[i]).wait()

    barrier = pltpu.get_barrier_semaphore()
    others = [lax.rem(narrow + m, n_narrow) for m in range(1, n_narrow)]

    def run(first, last, step):
        def body(i, carry):
            step(i)
            return carry

        lax.fori_loop(first, last, body, 0)

    def signal(sem, w, n):
        pl.semaphore_signal(sem, inc=1, device_id=(w, n), device_id_type=MESH)

    def signal_group(sem, w):
        for n in range(n_narrow):
            signal(sem, w, n)

    run(narrow + 1, n_narrow, lambda n: signal(barrier, wide, n))
    run(wide + 1, n_wide, lambda w: signal_group(barrier, w))

    lane = lax.broadcasted_iota(jnp.int32, (1, LANES), 1)
    lane4 = lax.broadcasted_iota(jnp.int32, (4, LANES), 1)
    lane8 = lax.broadcasted_iota(jnp.int32, (ROWS, LANES), 1)
    row8 = lax.broadcasted_iota(jnp.int32, (ROWS, LANES), 0)
    left = lane4 < stars

    fetched((star_in, 0), (star_mass, 1))
    spos, svel, sacc, sjerk = (star_in[i] for i in range(4))
    pred_pos = (
        spos + time_step * svel + step_sq * 0.5 * sacc + step_sq * time_step / 6.0 * sjerk
    )
    pred_vel = svel + time_step * sacc + step_sq * 0.5 * sjerk
    pos4 = jnp.concatenate([pred_pos, star_mass[...]], axis=0)
    vel4 = jnp.concatenate([pred_vel, jnp.zeros((1, stars), jnp.float32)], axis=0)
    block = jnp.concatenate([pos4, vel4], axis=1)
    block = jnp.where(lax.rem(wide, 2) == 0, block, pltpu.roll(block, stars, 1))
    mine = narrow * n_wide + wide
    states[mine] = block

    def send_state(w, n, recvs):
        pltpu.make_async_remote_copy(
            src_ref=states.at[mine],
            dst_ref=states.at[mine],
            send_sem=send_sem,
            recv_sem=recvs.at[wide // 2],
            device_id=(w, n),
            device_id_type=MESH,
        ).start()

    def send_group(w):
        send_state(w, narrow, near_sem)
        for n in others:
            send_state(w, n, pass_sem)

    def send_beside(n):
        send_state(wide, n, pass_sem)

    def send_cells(w):
        pltpu.make_async_remote_copy(
            src_ref=cell_out.at[w],
            dst_ref=cell_in.at[wide],
            send_sem=send_sem,
            recv_sem=near_sem.at[wide // 2],
            device_id=(w, narrow),
            device_id_type=MESH,
        ).start()

    group = lane // GROUPS

    def meet():
        smaller = wide * n_narrow + narrow

        @pl.when(smaller > 0)
        def _():
            pl.semaphore_wait(barrier, smaller)

        def send_down(w):
            send_group(w)

            @pl.when(cells_first)
            def _():
                send_cells(w)

        one = jnp.minimum(wide, 1)
        run(0, one, send_down)
        run(0, wide, lambda w: signal_group(enter_sem.at[wide // 2], w))
        run(0, narrow, lambda n: signal(enter_sem.at[wide // 2], wide, n))
        run(one, wide, send_down)
        run(0, narrow, send_beside)

    def make_cells():
        fetched((gal_in, 2), (masses, 3), (let_send, 4))
        if kicks != n_wide:
            fetched((star_leaf, 5))
        gpos, gmass = gal_in[0], masses[0]
        body_lane = lax.broadcasted_iota(jnp.int32, (1, bodies), 1)
        segment = group_of[...] + (body_lane // (bodies // leaves)) * GROUPS
        onehot = (
            lax.broadcasted_iota(jnp.int32, (LANES, bodies), 0)
            == jnp.broadcast_to(segment, (LANES, bodies))
        ).astype(jnp.bfloat16)
        moments = jnp.concatenate(
            [gpos * gmass, gmass, jnp.zeros((4, bodies), jnp.float32)], axis=0
        )
        sums = lax.dot_general(
            jnp.concatenate(split(moments), axis=0).astype(jnp.bfloat16),
            onehot,
            (((1,), (1,)), ((), ())),
            preferred_element_type=jnp.float32,
        )
        sums = sums[0:8] + sums[8:16] + sums[16:24]
        cells = jnp.where(row8 < 3, sums / spread(sums[3:4]), sums)
        cell_own[...] = cells

        square = (n_wide, n_wide)
        diagonal = lax.broadcasted_iota(jnp.int32, square, 0) == lax.broadcasted_iota(
            jnp.int32, square, 1
        )
        listed = jnp.broadcast_to(let_send[...].astype(jnp.float32), square)
        chosen = jnp.sum(jnp.where(diagonal, listed, 0.0), axis=1, keepdims=True)
        chosen = jnp.broadcast_to(chosen, (n_wide, LANES)).astype(jnp.int32)
        place = lax.rem(wide, slots)
        turn = jnp.bitwise_and(place - chosen, slots - 1)
        turn = jnp.where(jnp.logical_and(group == place, chosen >= 0), turn, slots)
        turned = [
            (cells if k == 0 else pltpu.roll(cells, k * GROUPS, 1))[0:4] for k in range(slots)
        ]
        for w in range(n_wide):
            taken = jnp.broadcast_to(turn[w : w + 1], (4, LANES))
            outgoing = jnp.zeros((4, LANES), jnp.float32)
            for k in range(slots):
                outgoing = jnp.where(taken == k, turned[k], outgoing)
            cell_out[w] = outgoing
        cell_in[wide] = jnp.zeros((4, LANES), jnp.float32)

    cells_first = jnp.logical_or(lax.rem(wide, 2) == 0, narrow < n_narrow // 2)

    def order(i):
        @pl.when(jnp.equal(i == 0, cells_first))
        def _():
            make_cells()

        @pl.when(jnp.not_equal(i == 0, cells_first))
        def _():
            meet()

    run(0, 2, order)

    @pl.when(jnp.logical_not(cells_first))
    def _():
        run(0, wide, send_cells)

    gpos, gmass = gal_in[0], masses[0]

    both = jnp.concatenate([pos4, vel4], axis=0)
    targets = jnp.transpose(
        jnp.concatenate([both, jnp.zeros((ROWS, LANES - stars), jnp.float32)], axis=1)
    )
    zero = jnp.zeros((ROWS, LANES), jnp.float32)

    own = [spread(cell_own[c : c + 1, :]) for c in range(4)]
    star_groups = stars // ROWS
    for t in range(star_groups):
        rows = targets[t * ROWS : (t + 1) * ROWS, :]
        place = [column(rows, c) for c in range(3)]
        for c in range(3):
            aims[t, c] = place[c]
            aims[t, 3 + c] = column(rows, 4 + c)
            star_sum[t, 3 + c] = zero
        for c, value in enumerate(pull(own[:3], own[3], place, (zero,) * 3)):
            star_sum[t, c] = value

    last4 = lax.broadcasted_iota(jnp.int32, (4, bodies), 0) == 3
    high, mid, low = split(jnp.concatenate([-2.0 * gpos, jnp.zeros_like(gmass)], axis=0))
    high = jnp.where(last4, 1.0, high)
    reach = split(norm(gpos) + soften_sq)
    blank = jnp.zeros_like(gmass)
    aimed[...] = jnp.concatenate(
        [high, mid, high, low, high, mid, *reach, blank, blank, blank, blank, blank],
        axis=0,
    ).astype(jnp.bfloat16)

    def on_bodies(rows, total):
        square = norm(rows[0:3])
        high, mid, low = split(jnp.concatenate([rows[0:3], square], axis=0))
        ones = jnp.ones((4, LANES), jnp.float32)
        turned = jnp.transpose(
            jnp.concatenate([high, high, mid, high, low, mid, ones, rows], axis=0)
        )
        reach = jnp.dot(
            turned.astype(jnp.bfloat16), aimed[...], preferred_element_type=jnp.float32
        )
        total = [list(part) for part in total]
        for g in range(LANES // ROWS):
            some = turned[g * ROWS : (g + 1) * ROWS, :]
            place = [column(some, 28 + c) for c in range(3)]
            mass = column(some, 31)
            for t in every:
                inverse = lax.rsqrt(
                    reach[g * ROWS : (g + 1) * ROWS, t * LANES : (t + 1) * LANES]
                )
                weight = mass * inverse * (inverse * inverse)
                for c in range(3):
                    total[t][c] = total[t][c] + place[c] * weight
                total[t][3] = total[t][3] + weight
        return total

    def keep(total):
        for t in every:
            for c in range(4):
                body_sum[4 * t + c] = total[t][c]

    def kept():
        return [[body_sum[4 * t + c] for c in range(4)] for t in every]

    def cells_on_stars(rows, t):
        place = [aims[t, c] for c in range(3)]
        return pull(rows[:3], rows[3], place, [star_sum[t, c] for c in range(3)])

    total = [[zero] * 4 for _ in every]
    for t in every:
        tile = slice(t * LANES, (t + 1) * LANES)
        total = on_bodies(jnp.concatenate([gpos[:, tile], gmass[:, tile]], axis=0), total)
    keep(total)

    def larger(w):
        rest = jnp.where(w == wide, n_narrow - 1 - narrow, 0)
        return jnp.where(w > wide, n_narrow, rest)

    def answer(q):
        count = larger(2 * q) + larger(2 * q + 1)

        @pl.when(count > 0)
        def _():
            pl.semaphore_wait(enter_sem.at[q], count)

        def to_group(w):
            @pl.when(w == wide)
            def _():
                run(narrow + 1, n_narrow, send_beside)

            @pl.when(w > wide)
            def _():
                send_group(w)
                send_cells(w)

        run(2 * q, 2 * q + 2, to_group)

    halves = n_wide // 2
    lower = wide < n_wide // 4


    def gather(n, even):
        even_block, odd_block = states[n * n_wide + even], states[n * n_wide + even + 1]
        rows = jnp.where(left, even_block, odd_block)
        speeds = pltpu.roll(jnp.where(left, odd_block, even_block), stars, 1)
        return rows, speeds

    def near_arrived(q):
        own = wide // 2 == q

        def wait(count):
            some = states.at[pl.ds(0, count)]
            pltpu.make_async_copy(some, some, near_sem.at[q]).wait()

        @pl.when(own)
        def _():
            wait(2)

        @pl.when(jnp.logical_not(own))
        def _():
            wait(4)

    def near_stars(even, total):
        near, _ = gather(narrow, even)
        if kicks == n_wide:
            return on_bodies(near, total)
        padded = jnp.concatenate([near, jnp.zeros((4, LANES), jnp.float32)], axis=0)
        cols[pl.ds(pl.multiple_of(even * stars, LANES), LANES), :] = jnp.transpose(padded)
        return total

    def near_cells(e, total):
        cells = cell_in[e * slots]
        for k in range(1, slots):
            cells = cells + cell_in[e * slots + k]
        rows = [spread(cells[c : c + 1]) for c in range(4)]
        for t in range(star_groups):
            for c, value in enumerate(cells_on_stars(rows, t)):
                star_sum[t, c] = value
        return on_bodies(cells, total)

    def rest_arrived(q):
        some = states.at[pl.ds(0, 2 * (n_narrow - 1))]
        pltpu.make_async_copy(some, some, pass_sem.at[q]).wait()

    def all_stars(even, take):
        for n in range(n_narrow):
            rows, speeds = gather(n, even)
            srow[n, 0:4, :] = rows
            srow[n, 4:8, :] = speeds
        sources = [
            [spread(srow[n, c : c + 1, :]) for c in range(7)] for n in range(n_narrow)
        ]
        for t in range(star_groups):
            place = [aims[t, c] for c in range(3)]
            speed = [aims[t, 3 + c] for c in range(3)]
            acc = [star_sum[t, c] for c in range(6)]
            for rows in sources:
                dx, dy, dz = (rows[c] - place[c] for c in range(3))
                ux, uy, uz = (rows[4 + c] - speed[c] for c in range(3))
                inverse = lax.rsqrt(dx * dx + dy * dy + dz * dz + soften_sq)
                square = inverse * inverse
                weight = rows[3] * inverse * square
                approach = 3.0 * (dx * ux + dy * uy + dz * uz) * square
                acc = [
                    acc[0] + dx * weight,
                    acc[1] + dy * weight,
                    acc[2] + dz * weight,
                    acc[3] + (ux - dx * approach) * weight,
                    acc[4] + (uy - dy * approach) * weight,
                    acc[5] + (uz - dz * approach) * weight,
                ]
            take(t, acc)

    def store(t, acc):
        for c in range(6):
            star_sum[t, c] = acc[c]

    pairs_per_row = slots // 2

    def nearby(q):
        return near_cells(q // pairs_per_row, near_stars(2 * q, kept()))

    first = wide < n_wide // 8

    def turn(p):
        run(
            jnp.where(p == 0, wide // 2, jnp.where(first, p + 1, halves)),
            jnp.where(first, jnp.minimum(p + 2, halves), halves),
            answer,
        )
        q = jnp.where(lower, p, halves - 1 - p)
        near_arrived(q)
        second = lax.rem(p, pairs_per_row) == pairs_per_row - 1

        @pl.when(second)
        def _():
            keep(nearby(q))
            rest_arrived(q)
            all_stars(2 * q, store)

        @pl.when(jnp.logical_not(second))
        def _():
            rest_arrived(q)
            keep(near_stars(2 * q, kept()))
            all_stars(2 * q, store)

    run(0, halves - 1, turn)

    last = jnp.where(lower, halves - 1, 0)
    near_arrived(last)
    total = nearby(last)
    for t in every:
        tile = slice(t * LANES, (t + 1) * LANES)
        near = [gpos[c : c + 1, tile] for c in range(3)]
        pieces = [jnp.sum(part, axis=0, keepdims=True) for part in total[t]]
        pieces = [pieces[c] - near[c] * pieces[3] for c in range(3)]
        if kicks != n_wide:
            here = [spread(row) for row in near]

            def kick(k, acc):
                listed = star_leaf[t * leaves // tiles, k]

                def some(g, acc):
                    at = pl.multiple_of(listed * stars + g * ROWS, ROWS)
                    source = cols[pl.ds(at, ROWS), :]
                    place = [column(source, c) for c in range(3)]
                    return pull(place, column(source, 3), here, acc)

                return loop(stars // ROWS, some, acc)

            kicked = lax.fori_loop(0, kicks, kick, (zero,) * 3)
            for c in range(3):
                pieces[c] = pieces[c] + jnp.sum(kicked[c], axis=0, keepdims=True)
        for c in range(3):
            out[c : c + 1, tile] = gal_in[1, c : c + 1, tile] + time_step * pieces[c]

    pieces = []

    def finish(t, acc):
        piece = jnp.zeros((ROWS, LANES), jnp.float32)
        for c in range(6):
            piece = jnp.where(lane8 == c, jnp.sum(acc[c], axis=1, keepdims=True), piece)
        pieces.append(piece)

    rest_arrived(last)
    all_stars(2 * last, finish)
    result = jnp.transpose(jnp.concatenate(pieces, axis=0))
    new_acc, new_jerk = result[0:3], result[3:6]
    vel_new = (
        svel + time_step * 0.5 * (sacc + new_acc) + step_sq / 12.0 * (sjerk - new_jerk)
    )
    vel_at = bodies + LANES
    out[:, vel_at : vel_at + stars] = vel_new
    out[:, bodies : bodies + stars] = (
        spos + time_step * 0.5 * (svel + vel_new) + step_sq / 12.0 * (sacc - new_acc)
    )

    sent = states.at[pl.ds(0, n_wide * (n_narrow + 1) - 2)]
    pltpu.make_async_copy(sent, sent, send_sem).wait()


def unpack(packed, gal_out, pos_out, vel_out):
    bodies, stars = gal_out.shape[1], pos_out.shape[1]
    gal_out[...] = packed[:, 0:bodies]
    pos_out[...] = packed[:, bodies : bodies + stars]
    vel_out[...] = packed[:, bodies + LANES : bodies + LANES + stars]


def body(
    n_wide,
    n_narrow,
    star_pos,
    star_vel,
    star_mass,
    star_acc,
    star_jerk,
    gal_pos,
    gal_vel,
    gal_mass,
    group_of,
    let_send,
    star_leaf,
):
    stars, bodies = star_pos.shape[1], gal_pos.shape[1]
    vmem = pl.BlockSpec(memory_space=pltpu.VMEM)
    f32 = jnp.float32
    i32 = jnp.int32
    hbm = pl.BlockSpec(memory_space=pltpu.HBM)
    packed = pl.pallas_call(
        functools.partial(kernel, n_wide, n_narrow),
        out_shape=jax.ShapeDtypeStruct((3, bodies + 2 * LANES), f32),
        in_specs=[hbm] * 11,
        out_specs=vmem,
        scratch_shapes=[
            pltpu.VMEM((4, 3, stars), f32),
            pltpu.VMEM((1, stars), f32),
            pltpu.VMEM((2, 3, bodies), f32),
            pltpu.VMEM((2, 1, bodies), f32),
            pltpu.VMEM((1, bodies), i32),
            pltpu.VMEM((1, n_wide), i32),
            pltpu.SMEM(star_leaf.shape, i32),
            pltpu.SemaphoreType.DMA((5 + (star_leaf.shape[1] != n_wide),)),
            pltpu.VMEM(((n_narrow + 1) * n_wide, 4, LANES), f32),
            pltpu.VMEM((ROWS, LANES), f32),
            pltpu.VMEM((n_wide, 4, LANES), f32),
            pltpu.VMEM((n_wide, 4, LANES), f32),
            pltpu.VMEM((32, bodies), jnp.bfloat16),
            pltpu.VMEM((n_wide * stars, ROWS), f32),
            pltpu.VMEM((n_narrow, ROWS, LANES), f32),
            pltpu.VMEM((stars // ROWS, 6, ROWS, LANES), f32),
            pltpu.VMEM((4 * bodies // LANES, ROWS, LANES), f32),
            pltpu.VMEM((stars // ROWS, 6, ROWS, LANES), f32),
            pltpu.SemaphoreType.DMA,
            pltpu.SemaphoreType.DMA((n_wide // 2,)),
            pltpu.SemaphoreType.DMA((n_wide // 2,)),
            pltpu.SemaphoreType.REGULAR((n_wide // 2,)),
        ],
        compiler_params=pltpu.CompilerParams(
            collective_id=0, has_side_effects=True, vmem_limit_bytes=24 << 20
        ),
    )(
        *(
            pltpu.with_memory_space_constraint(array, pltpu.HBM)
            for array in (
                star_pos,
                star_vel,
                star_mass.reshape(1, stars),
                star_acc,
                star_jerk,
                gal_pos,
                gal_vel,
                gal_mass.reshape(1, bodies),
                group_of.reshape(1, bodies),
                let_send.reshape(1, n_wide),
                star_leaf,
            )
        )
    )
    return pl.pallas_call(
        unpack,
        out_shape=(
            jax.ShapeDtypeStruct(gal_vel.shape, f32),
            jax.ShapeDtypeStruct(star_pos.shape, f32),
            jax.ShapeDtypeStruct(star_vel.shape, f32),
        ),
        in_specs=[vmem],
        out_specs=(vmem,) * 3,
        compiler_params=pltpu.CompilerParams(vmem_limit_bytes=1 << 20),
    )(packed)


def solution(mesh):
    both = ("wide", "narrow")
    columns, flat = P(None, both), P(both)
    return jax.shard_map(
        functools.partial(body, mesh.shape["wide"], mesh.shape["narrow"]),
        mesh=mesh,
        in_specs=(
            columns,
            columns,
            flat,
            columns,
            columns,
            columns,
            columns,
            flat,
            flat,
            P(both, None, None),
            P(both, None),
        ),
        out_specs=(columns, columns, columns),
        check_vma=False,
    )
```

```python
import functools

import jax
import jax.numpy as jnp
from jax import lax
from jax.experimental import pallas as pl
from jax.experimental.pallas import tpu as pltpu
from jax.sharding import PartitionSpec as P

GROUPS = 32
LANES = 128
ROWS = 8
MESH = pl.DeviceIdType.MESH

time_step = 0.25
soften_sq = 0.05


def loop(count, step, init, most=4):
    unroll = next(u for u in range(min(most, count), 0, -1) if count % u == 0)
    return lax.fori_loop(0, count, step, init, unroll=unroll)


def spread(row):
    return jnp.broadcast_to(row, (ROWS, row.shape[1]))


def column(block, index):
    return jnp.broadcast_to(block[:, index : index + 1], (ROWS, LANES))


def pull(source, mass, target, total):
    dx, dy, dz = (s - t for s, t in zip(source, target))
    inverse = lax.rsqrt(dx * dx + dy * dy + dz * dz + soften_sq)
    weight = mass * inverse * inverse * inverse
    return (total[0] + dx * weight, total[1] + dy * weight, total[2] + dz * weight)


def norm(rows):
    return rows[0:1] * rows[0:1] + rows[1:2] * rows[1:2] + rows[2:3] * rows[2:3]


def split(value):
    parts = []
    for _ in range(3):
        parts.append(value.astype(jnp.bfloat16).astype(jnp.float32))
        value = value - parts[-1]
    return parts


def kernel(
    n_wide,
    n_narrow,
    star_pos_hbm,
    star_vel_hbm,
    star_mass_hbm,
    star_acc_hbm,
    star_jerk_hbm,
    gal_pos_hbm,
    gal_vel_hbm,
    gal_mass_hbm,
    group_of_hbm,
    let_send_hbm,
    star_leaf_hbm,
    out,
    star_in,
    star_mass,
    gal_in,
    masses,
    group_of,
    let_send,
    star_leaf,
    in_sem,
    states,
    cell_own,
    cell_out,
    cell_in,
    aimed,
    cols,
    srow,
    aims,
    body_sum,
    star_sum,
    send_sem,
    near_sem,
    pass_sem,
    enter_sem,
):
    wide, narrow = lax.axis_index("wide"), lax.axis_index("narrow")
    stars, bodies = star_in.shape[2], gal_in.shape[2]
    leaves, kicks = star_leaf.shape
    slots = LANES // GROUPS
    step_sq = time_step * time_step
    tiles = bodies // LANES
    every = tuple(range(tiles))

    fetches = [
        (star_pos_hbm, star_in.at[0], 0),
        (star_vel_hbm, star_in.at[1], 0),
        (star_acc_hbm, star_in.at[2], 0),
        (star_jerk_hbm, star_in.at[3], 0),
        (star_mass_hbm, star_mass, 1),
        (gal_pos_hbm, gal_in.at[0], 2),
        (gal_vel_hbm, gal_in.at[1], 2),
        (gal_mass_hbm, masses.at[0], 3),
        (group_of_hbm, group_of, 3),
        (let_send_hbm, let_send, 4),
    ]
    if kicks != n_wide:
        fetches.append((star_leaf_hbm, star_leaf, 5))
    for source, target, i in fetches:
        pltpu.make_async_copy(source, target, in_sem.at[i]).start()

    def fetched(*refs):
        for ref, i in refs:
            pltpu.make_async_copy(ref, ref, in_sem.at[i]).wait()

    barrier = pltpu.get_barrier_semaphore()
    half = n_narrow // 2
    others = [lax.rem(narrow + half + m, n_narrow) for m in range(n_narrow) if m != half]

    def run(first, last, step):
        def body(i, carry):
            step(i)
            return carry

        lax.fori_loop(first, last, body, 0)

    def signal(sem, w, n):
        pl.semaphore_signal(sem, inc=1, device_id=(w, n), device_id_type=MESH)

    def signal_group(sem, w):
        for n in range(n_narrow):
            signal(sem, w, n)

    run(narrow + 1, n_narrow, lambda n: signal(barrier, wide, n))
    run(wide + 1, n_wide, lambda w: signal_group(barrier, w))

    lane = lax.broadcasted_iota(jnp.int32, (1, LANES), 1)
    lane4 = lax.broadcasted_iota(jnp.int32, (4, LANES), 1)
    lane8 = lax.broadcasted_iota(jnp.int32, (ROWS, LANES), 1)
    row8 = lax.broadcasted_iota(jnp.int32, (ROWS, LANES), 0)
    left = lane4 < stars

    fetched((star_in, 0), (star_mass, 1))
    spos, svel, sacc, sjerk = (star_in[i] for i in range(4))
    pred_pos = (
        spos + time_step * svel + step_sq * 0.5 * sacc + step_sq * time_step / 6.0 * sjerk
    )
    pred_vel = svel + time_step * sacc + step_sq * 0.5 * sjerk
    pos4 = jnp.concatenate([pred_pos, star_mass[...]], axis=0)
    vel4 = jnp.concatenate([pred_vel, jnp.zeros((1, stars), jnp.float32)], axis=0)
    block = jnp.concatenate([pos4, vel4], axis=1)
    block = jnp.where(lax.rem(wide, 2) == 0, block, pltpu.roll(block, stars, 1))
    mine = narrow * n_wide + wide
    states[mine] = block

    def send_state(w, n, recvs):
        pltpu.make_async_remote_copy(
            src_ref=states.at[mine],
            dst_ref=states.at[mine],
            send_sem=send_sem,
            recv_sem=recvs.at[wide // 2],
            device_id=(w, n),
            device_id_type=MESH,
        ).start()

    def send_group(w):
        send_state(w, narrow, near_sem)
        for n in others:
            send_state(w, n, pass_sem)

    def answer_group(w):
        for n in others:
            send_state(w, n, pass_sem)
        send_state(w, narrow, near_sem)

    def send_beside(n):
        send_state(wide, n, pass_sem)

    def send_cells(w):
        pltpu.make_async_remote_copy(
            src_ref=cell_out.at[w],
            dst_ref=cell_in.at[wide],
            send_sem=send_sem,
            recv_sem=near_sem.at[wide // 2],
            device_id=(w, narrow),
            device_id_type=MESH,
        ).start()

    group = lane // GROUPS

    def meet():
        smaller = wide * n_narrow + narrow

        @pl.when(smaller > 0)
        def _():
            pl.semaphore_wait(barrier, smaller)

        def send_down(w):
            send_group(w)

            @pl.when(cells_first)
            def _():
                send_cells(w)

        one = jnp.where(lax.rem(wide, 2) == 0, 0, jnp.minimum(wide, 1))
        run(0, one, send_down)
        run(0, wide, lambda w: signal_group(enter_sem.at[wide // 2], w))
        run(0, narrow, lambda n: signal(enter_sem.at[wide // 2], wide, n))
        run(one, wide, send_down)
        run(0, narrow, send_beside)

    def make_cells():
        fetched((gal_in, 2), (masses, 3), (let_send, 4))
        if kicks != n_wide:
            fetched((star_leaf, 5))
        gpos, gmass = gal_in[0], masses[0]
        body_lane = lax.broadcasted_iota(jnp.int32, (1, bodies), 1)
        segment = group_of[...] + (body_lane // (bodies // leaves)) * GROUPS
        onehot = (
            lax.broadcasted_iota(jnp.int32, (LANES, bodies), 0)
            == jnp.broadcast_to(segment, (LANES, bodies))
        ).astype(jnp.bfloat16)
        moments = jnp.concatenate(
            [gpos * gmass, gmass, jnp.zeros((4, bodies), jnp.float32)], axis=0
        )
        sums = lax.dot_general(
            jnp.concatenate(split(moments), axis=0).astype(jnp.bfloat16),
            onehot,
            (((1,), (1,)), ((), ())),
            preferred_element_type=jnp.float32,
        )
        sums = sums[0:8] + sums[8:16] + sums[16:24]
        cells = jnp.where(row8 < 3, sums / spread(sums[3:4]), sums)
        cell_own[...] = cells

        square = (n_wide, n_wide)
        diagonal = lax.broadcasted_iota(jnp.int32, square, 0) == lax.broadcasted_iota(
            jnp.int32, square, 1
        )
        listed = jnp.broadcast_to(let_send[...].astype(jnp.float32), square)
        chosen = jnp.sum(jnp.where(diagonal, listed, 0.0), axis=1, keepdims=True)
        chosen = jnp.broadcast_to(chosen, (n_wide, LANES)).astype(jnp.int32)
        place = lax.rem(wide, slots)
        turn = jnp.bitwise_and(place - chosen, slots - 1)
        turn = jnp.where(jnp.logical_and(group == place, chosen >= 0), turn, slots)
        turned = [
            (cells if k == 0 else pltpu.roll(cells, k * GROUPS, 1))[0:4] for k in range(slots)
        ]
        for w in range(n_wide):
            taken = jnp.broadcast_to(turn[w : w + 1], (4, LANES))
            outgoing = jnp.zeros((4, LANES), jnp.float32)
            for k in range(slots):
                outgoing = jnp.where(taken == k, turned[k], outgoing)
            cell_out[w] = outgoing
        cell_in[wide] = jnp.zeros((4, LANES), jnp.float32)

    cells_first = jnp.logical_or(lax.rem(wide, 2) == 0, narrow < n_narrow // 2)

    def order(i):
        @pl.when(jnp.equal(i == 0, cells_first))
        def _():
            make_cells()

        @pl.when(jnp.not_equal(i == 0, cells_first))
        def _():
            meet()

    run(0, 2, order)

    @pl.when(jnp.logical_not(cells_first))
    def _():
        run(0, wide, send_cells)

    gpos, gmass = gal_in[0], masses[0]

    both = jnp.concatenate([pos4, vel4], axis=0)
    targets = jnp.transpose(
        jnp.concatenate([both, jnp.zeros((ROWS, LANES - stars), jnp.float32)], axis=1)
    )
    zero = jnp.zeros((ROWS, LANES), jnp.float32)

    own = [spread(cell_own[c : c + 1, :]) for c in range(4)]
    star_groups = stars // ROWS
    for t in range(star_groups):
        rows = targets[t * ROWS : (t + 1) * ROWS, :]
        place = [column(rows, c) for c in range(3)]
        for c in range(3):
            aims[t, c] = place[c]
            aims[t, 3 + c] = column(rows, 4 + c)
            star_sum[t, 3 + c] = zero
        for c, value in enumerate(pull(own[:3], own[3], place, (zero,) * 3)):
            star_sum[t, c] = value

    last4 = lax.broadcasted_iota(jnp.int32, (4, bodies), 0) == 3
    high, mid, low = split(jnp.concatenate([-2.0 * gpos, jnp.zeros_like(gmass)], axis=0))
    high = jnp.where(last4, 1.0, high)
    reach = split(norm(gpos) + soften_sq)
    blank = jnp.zeros_like(gmass)
    aimed[...] = jnp.concatenate(
        [high, mid, high, low, high, mid, *reach, blank, blank, blank, blank, blank],
        axis=0,
    ).astype(jnp.bfloat16)

    def on_bodies(rows, total):
        square = norm(rows[0:3])
        high, mid, low = split(jnp.concatenate([rows[0:3], square], axis=0))
        ones = jnp.ones((4, LANES), jnp.float32)
        turned = jnp.transpose(
            jnp.concatenate([high, high, mid, high, low, mid, ones, rows], axis=0)
        )
        reach = jnp.dot(
            turned.astype(jnp.bfloat16), aimed[...], preferred_element_type=jnp.float32
        )
        total = [list(part) for part in total]
        for g in range(LANES // ROWS):
            some = turned[g * ROWS : (g + 1) * ROWS, :]
            place = [column(some, 28 + c) for c in range(3)]
            mass = column(some, 31)
            for t in every:
                inverse = lax.rsqrt(
                    reach[g * ROWS : (g + 1) * ROWS, t * LANES : (t + 1) * LANES]
                )
                weight = mass * inverse * (inverse * inverse)
                for c in range(3):
                    total[t][c] = total[t][c] + place[c] * weight
                total[t][3] = total[t][3] + weight
        return total

    def keep(total):
        for t in every:
            for c in range(4):
                body_sum[4 * t + c] = total[t][c]

    def kept():
        return [[body_sum[4 * t + c] for c in range(4)] for t in every]

    def cells_on_stars(rows, t):
        place = [aims[t, c] for c in range(3)]
        return pull(rows[:3], rows[3], place, [star_sum[t, c] for c in range(3)])

    total = [[zero] * 4 for _ in every]
    for t in every:
        tile = slice(t * LANES, (t + 1) * LANES)
        total = on_bodies(jnp.concatenate([gpos[:, tile], gmass[:, tile]], axis=0), total)
    keep(total)

    def larger(w):
        rest = jnp.where(w == wide, n_narrow - 1 - narrow, 0)
        return jnp.where(w > wide, n_narrow, rest)

    def answer(q):
        count = larger(2 * q) + larger(2 * q + 1)

        @pl.when(count > 0)
        def _():
            pl.semaphore_wait(enter_sem.at[q], count)

        def to_group(w):
            @pl.when(w == wide)
            def _():
                run(narrow + 1, n_narrow, send_beside)

            @pl.when(w > wide)
            def _():
                answer_group(w)
                send_cells(w)

        run(2 * q, 2 * q + 2, to_group)

    halves = n_wide // 2
    lower = wide < n_wide // 4


    def gather(n, even):
        even_block, odd_block = states[n * n_wide + even], states[n * n_wide + even + 1]
        rows = jnp.where(left, even_block, odd_block)
        speeds = pltpu.roll(jnp.where(left, odd_block, even_block), stars, 1)
        return rows, speeds

    def near_arrived(q):
        own = wide // 2 == q

        def wait(count):
            some = states.at[pl.ds(0, count)]
            pltpu.make_async_copy(some, some, near_sem.at[q]).wait()

        @pl.when(own)
        def _():
            wait(2)

        @pl.when(jnp.logical_not(own))
        def _():
            wait(4)

    def near_stars(even, total):
        near, _ = gather(narrow, even)
        if kicks == n_wide:
            return on_bodies(near, total)
        padded = jnp.concatenate([near, jnp.zeros((4, LANES), jnp.float32)], axis=0)
        cols[pl.ds(pl.multiple_of(even * stars, LANES), LANES), :] = jnp.transpose(padded)
        return total

    def near_cells(e, total):
        cells = cell_in[e * slots]
        for k in range(1, slots):
            cells = cells + cell_in[e * slots + k]
        rows = [spread(cells[c : c + 1]) for c in range(4)]
        for t in range(star_groups):
            for c, value in enumerate(cells_on_stars(rows, t)):
                star_sum[t, c] = value
        return on_bodies(cells, total)

    def rest_arrived(q):
        some = states.at[pl.ds(0, 2 * (n_narrow - 1))]
        pltpu.make_async_copy(some, some, pass_sem.at[q]).wait()

    def all_stars(even, take):
        for n in range(n_narrow):
            rows, speeds = gather(n, even)
            srow[n, 0:4, :] = rows
            srow[n, 4:8, :] = speeds
        sources = [
            [spread(srow[n, c : c + 1, :]) for c in range(7)] for n in range(n_narrow)
        ]
        for t in range(star_groups):
            place = [aims[t, c] for c in range(3)]
            speed = [aims[t, 3 + c] for c in range(3)]
            acc = [star_sum[t, c] for c in range(6)]
            for rows in sources:
                dx, dy, dz = (rows[c] - place[c] for c in range(3))
                ux, uy, uz = (rows[4 + c] - speed[c] for c in range(3))
                inverse = lax.rsqrt(dx * dx + dy * dy + dz * dz + soften_sq)
                square = inverse * inverse
                weight = rows[3] * inverse * square
                approach = 3.0 * (dx * ux + dy * uy + dz * uz) * square
                acc = [
                    acc[0] + dx * weight,
                    acc[1] + dy * weight,
                    acc[2] + dz * weight,
                    acc[3] + (ux - dx * approach) * weight,
                    acc[4] + (uy - dy * approach) * weight,
                    acc[5] + (uz - dz * approach) * weight,
                ]
            take(t, acc)

    def store(t, acc):
        for c in range(6):
            star_sum[t, c] = acc[c]

    pairs_per_row = slots // 2

    def nearby(q):
        return near_cells(q // pairs_per_row, near_stars(2 * q, kept()))

    first = wide < n_wide // 8

    def turn(p):
        run(
            jnp.where(p == 0, wide // 2, jnp.where(jnp.logical_and(first, p == 1), 2, halves)),
            jnp.where(jnp.logical_and(first, p == 0), 2, halves),
            answer,
        )
        q = jnp.where(lower, p, halves - 1 - p)
        near_arrived(q)
        second = lax.rem(p, pairs_per_row) == pairs_per_row - 1

        @pl.when(second)
        def _():
            keep(nearby(q))
            rest_arrived(q)
            all_stars(2 * q, store)

        @pl.when(jnp.logical_not(second))
        def _():
            rest_arrived(q)
            keep(near_stars(2 * q, kept()))
            all_stars(2 * q, store)

    run(0, halves - 1, turn)

    last = jnp.where(lower, halves - 1, 0)
    near_arrived(last)
    total = nearby(last)
    for t in every:
        tile = slice(t * LANES, (t + 1) * LANES)
        near = [gpos[c : c + 1, tile] for c in range(3)]
        pieces = [jnp.sum(part, axis=0, keepdims=True) for part in total[t]]
        pieces = [pieces[c] - near[c] * pieces[3] for c in range(3)]
        if kicks != n_wide:
            here = [spread(row) for row in near]

            def kick(k, acc):
                listed = star_leaf[t * leaves // tiles, k]

                def some(g, acc):
                    at = pl.multiple_of(listed * stars + g * ROWS, ROWS)
                    source = cols[pl.ds(at, ROWS), :]
                    place = [column(source, c) for c in range(3)]
                    return pull(place, column(source, 3), here, acc)

                return loop(stars // ROWS, some, acc)

            kicked = lax.fori_loop(0, kicks, kick, (zero,) * 3)
            for c in range(3):
                pieces[c] = pieces[c] + jnp.sum(kicked[c], axis=0, keepdims=True)
        for c in range(3):
            out[c : c + 1, tile] = gal_in[1, c : c + 1, tile] + time_step * pieces[c]

    pieces = []

    def finish(t, acc):
        piece = jnp.zeros((ROWS, LANES), jnp.float32)
        for c in range(6):
            piece = jnp.where(lane8 == c, jnp.sum(acc[c], axis=1, keepdims=True), piece)
        pieces.append(piece)

    rest_arrived(last)
    all_stars(2 * last, finish)
    result = jnp.transpose(jnp.concatenate(pieces, axis=0))
    new_acc, new_jerk = result[0:3], result[3:6]
    vel_new = (
        svel + time_step * 0.5 * (sacc + new_acc) + step_sq / 12.0 * (sjerk - new_jerk)
    )
    vel_at = bodies + LANES
    out[:, vel_at : vel_at + stars] = vel_new
    out[:, bodies : bodies + stars] = (
        spos + time_step * 0.5 * (svel + vel_new) + step_sq / 12.0 * (sacc - new_acc)
    )

    sent = states.at[pl.ds(0, n_wide * (n_narrow + 1) - 2)]
    pltpu.make_async_copy(sent, sent, send_sem).wait()


def unpack(packed, gal_out, pos_out, vel_out):
    bodies, stars = gal_out.shape[1], pos_out.shape[1]
    gal_out[...] = packed[:, 0:bodies]
    pos_out[...] = packed[:, bodies : bodies + stars]
    vel_out[...] = packed[:, bodies + LANES : bodies + LANES + stars]


def body(
    n_wide,
    n_narrow,
    star_pos,
    star_vel,
    star_mass,
    star_acc,
    star_jerk,
    gal_pos,
    gal_vel,
    gal_mass,
    group_of,
    let_send,
    star_leaf,
):
    stars, bodies = star_pos.shape[1], gal_pos.shape[1]
    vmem = pl.BlockSpec(memory_space=pltpu.VMEM)
    f32 = jnp.float32
    i32 = jnp.int32
    hbm = pl.BlockSpec(memory_space=pltpu.HBM)
    packed = pl.pallas_call(
        functools.partial(kernel, n_wide, n_narrow),
        out_shape=jax.ShapeDtypeStruct((3, bodies + 2 * LANES), f32),
        in_specs=[hbm] * 11,
        out_specs=vmem,
        scratch_shapes=[
            pltpu.VMEM((4, 3, stars), f32),
            pltpu.VMEM((1, stars), f32),
            pltpu.VMEM((2, 3, bodies), f32),
            pltpu.VMEM((2, 1, bodies), f32),
            pltpu.VMEM((1, bodies), i32),
            pltpu.VMEM((1, n_wide), i32),
            pltpu.SMEM(star_leaf.shape, i32),
            pltpu.SemaphoreType.DMA((5 + (star_leaf.shape[1] != n_wide),)),
            pltpu.VMEM(((n_narrow + 1) * n_wide, 4, LANES), f32),
            pltpu.VMEM((ROWS, LANES), f32),
            pltpu.VMEM((n_wide, 4, LANES), f32),
            pltpu.VMEM((n_wide, 4, LANES), f32),
            pltpu.VMEM((32, bodies), jnp.bfloat16),
            pltpu.VMEM((n_wide * stars, ROWS), f32),
            pltpu.VMEM((n_narrow, ROWS, LANES), f32),
            pltpu.VMEM((stars // ROWS, 6, ROWS, LANES), f32),
            pltpu.VMEM((4 * bodies // LANES, ROWS, LANES), f32),
            pltpu.VMEM((stars // ROWS, 6, ROWS, LANES), f32),
            pltpu.SemaphoreType.DMA,
            pltpu.SemaphoreType.DMA((n_wide // 2,)),
            pltpu.SemaphoreType.DMA((n_wide // 2,)),
            pltpu.SemaphoreType.REGULAR((n_wide // 2,)),
        ],
        compiler_params=pltpu.CompilerParams(
            collective_id=0, has_side_effects=True, vmem_limit_bytes=24 << 20
        ),
    )(
        *(
            pltpu.with_memory_space_constraint(array, pltpu.HBM)
            for array in (
                star_pos,
                star_vel,
                star_mass.reshape(1, stars),
                star_acc,
                star_jerk,
                gal_pos,
                gal_vel,
                gal_mass.reshape(1, bodies),
                group_of.reshape(1, bodies),
                let_send.reshape(1, n_wide),
                star_leaf,
            )
        )
    )
    return pl.pallas_call(
        unpack,
        out_shape=(
            jax.ShapeDtypeStruct(gal_vel.shape, f32),
            jax.ShapeDtypeStruct(star_pos.shape, f32),
            jax.ShapeDtypeStruct(star_vel.shape, f32),
        ),
        in_specs=[vmem],
        out_specs=(vmem,) * 3,
        compiler_params=pltpu.CompilerParams(vmem_limit_bytes=1 << 20),
    )(packed)


def solution(mesh):
    both = ("wide", "narrow")
    columns, flat = P(None, both), P(both)
    return jax.shard_map(
        functools.partial(body, mesh.shape["wide"], mesh.shape["narrow"]),
        mesh=mesh,
        in_specs=(
            columns,
            columns,
            flat,
            columns,
            columns,
            columns,
            columns,
            flat,
            flat,
            P(both, None, None),
            P(both, None),
        ),
        out_specs=(columns, columns, columns),
        check_vma=False,
    )
```

```python
import functools

import jax
import jax.numpy as jnp
from jax import lax
from jax.experimental import pallas as pl
from jax.experimental.pallas import tpu as pltpu
from jax.sharding import PartitionSpec as P

GROUPS = 32
LANES = 128
ROWS = 8
MESH = pl.DeviceIdType.MESH

time_step = 0.25
soften_sq = 0.05


def loop(count, step, init, most=4):
    unroll = next(u for u in range(min(most, count), 0, -1) if count % u == 0)
    return lax.fori_loop(0, count, step, init, unroll=unroll)


def spread(row):
    return jnp.broadcast_to(row, (ROWS, row.shape[1]))


def column(block, index):
    return jnp.broadcast_to(block[:, index : index + 1], (ROWS, LANES))


def pull(source, mass, target, total):
    dx, dy, dz = (s - t for s, t in zip(source, target))
    inverse = lax.rsqrt(dx * dx + dy * dy + dz * dz + soften_sq)
    weight = mass * inverse * inverse * inverse
    return (total[0] + dx * weight, total[1] + dy * weight, total[2] + dz * weight)


def norm(rows):
    return rows[0:1] * rows[0:1] + rows[1:2] * rows[1:2] + rows[2:3] * rows[2:3]


def split(value):
    parts = []
    for _ in range(3):
        parts.append(value.astype(jnp.bfloat16).astype(jnp.float32))
        value = value - parts[-1]
    return parts


def kernel(
    n_wide,
    n_narrow,
    star_pos_hbm,
    star_vel_hbm,
    star_mass_hbm,
    star_acc_hbm,
    star_jerk_hbm,
    gal_pos_hbm,
    gal_vel_hbm,
    gal_mass_hbm,
    group_of_hbm,
    let_send_hbm,
    star_leaf_hbm,
    out,
    star_in,
    star_mass,
    gal_in,
    masses,
    group_of,
    let_send,
    star_leaf,
    in_sem,
    states,
    cell_own,
    cell_out,
    cell_in,
    aimed,
    cols,
    srow,
    aims,
    body_sum,
    star_sum,
    send_sem,
    near_sem,
    pass_sem,
    enter_sem,
):
    wide, narrow = lax.axis_index("wide"), lax.axis_index("narrow")
    stars, bodies = star_in.shape[2], gal_in.shape[2]
    leaves, kicks = star_leaf.shape
    slots = LANES // GROUPS
    step_sq = time_step * time_step
    tiles = bodies // LANES
    every = tuple(range(tiles))

    fetches = [
        (star_pos_hbm, star_in.at[0], 0),
        (star_vel_hbm, star_in.at[1], 0),
        (star_acc_hbm, star_in.at[2], 0),
        (star_jerk_hbm, star_in.at[3], 0),
        (star_mass_hbm, star_mass, 1),
        (gal_pos_hbm, gal_in.at[0], 2),
        (gal_vel_hbm, gal_in.at[1], 2),
        (gal_mass_hbm, masses.at[0], 3),
        (group_of_hbm, group_of, 3),
        (let_send_hbm, let_send, 4),
    ]
    if kicks != n_wide:
        fetches.append((star_leaf_hbm, star_leaf, 5))
    for source, target, i in fetches:
        pltpu.make_async_copy(source, target, in_sem.at[i]).start()

    def fetched(*refs):
        for ref, i in refs:
            pltpu.make_async_copy(ref, ref, in_sem.at[i]).wait()

    barrier = pltpu.get_barrier_semaphore()
    half = n_narrow // 2
    others = [lax.rem(narrow + half + m, n_narrow) for m in range(n_narrow) if m != half]

    def run(first, last, step):
        def body(i, carry):
            step(i)
            return carry

        lax.fori_loop(first, last, body, 0)

    def signal(sem, w, n):
        pl.semaphore_signal(sem, inc=1, device_id=(w, n), device_id_type=MESH)

    def signal_group(sem, w):
        for n in range(n_narrow):
            signal(sem, w, n)

    run(narrow + 1, n_narrow, lambda n: signal(barrier, wide, n))
    run(wide + 1, n_wide, lambda w: signal_group(barrier, w))

    lane = lax.broadcasted_iota(jnp.int32, (1, LANES), 1)
    lane4 = lax.broadcasted_iota(jnp.int32, (4, LANES), 1)
    lane8 = lax.broadcasted_iota(jnp.int32, (ROWS, LANES), 1)
    row8 = lax.broadcasted_iota(jnp.int32, (ROWS, LANES), 0)
    left = lane4 < stars

    fetched((star_in, 0), (star_mass, 1))
    spos, svel, sacc, sjerk = (star_in[i] for i in range(4))
    pred_pos = (
        spos + time_step * svel + step_sq * 0.5 * sacc + step_sq * time_step / 6.0 * sjerk
    )
    pred_vel = svel + time_step * sacc + step_sq * 0.5 * sjerk
    pos4 = jnp.concatenate([pred_pos, star_mass[...]], axis=0)
    vel4 = jnp.concatenate([pred_vel, jnp.zeros((1, stars), jnp.float32)], axis=0)
    block = jnp.concatenate([pos4, vel4], axis=1)
    block = jnp.where(lax.rem(wide, 2) == 0, block, pltpu.roll(block, stars, 1))
    mine = narrow * n_wide + wide
    states[mine] = block

    def send_state(w, n, recvs):
        pltpu.make_async_remote_copy(
            src_ref=states.at[mine],
            dst_ref=states.at[mine],
            send_sem=send_sem,
            recv_sem=recvs.at[wide // 2],
            device_id=(w, n),
            device_id_type=MESH,
        ).start()

    def send_group(w):
        send_state(w, narrow, near_sem)
        for n in others:
            send_state(w, n, pass_sem)

    def answer_group(w):
        for n in others:
            send_state(w, n, pass_sem)
        send_state(w, narrow, near_sem)

    def send_beside(n):
        send_state(wide, n, pass_sem)

    def send_cells(w):
        pltpu.make_async_remote_copy(
            src_ref=cell_out.at[w],
            dst_ref=cell_in.at[wide],
            send_sem=send_sem,
            recv_sem=near_sem.at[wide // 2],
            device_id=(w, narrow),
            device_id_type=MESH,
        ).start()

    group = lane // GROUPS

    def meet():
        smaller = wide * n_narrow + narrow

        @pl.when(smaller > 0)
        def _():
            pl.semaphore_wait(barrier, smaller)

        def send_down(w):
            send_group(w)

            @pl.when(cells_first)
            def _():
                send_cells(w)

        one = jnp.where(lax.rem(wide, 2) == 0, 0, jnp.minimum(wide, 1))
        run(0, one, send_down)
        run(0, wide, lambda w: signal_group(enter_sem.at[wide // 2], w))
        run(0, narrow, lambda n: signal(enter_sem.at[wide // 2], wide, n))
        run(one, wide, send_down)
        run(0, narrow, send_beside)

    def make_cells():
        fetched((gal_in, 2), (masses, 3), (let_send, 4))
        if kicks != n_wide:
            fetched((star_leaf, 5))
        gpos, gmass = gal_in[0], masses[0]
        body_lane = lax.broadcasted_iota(jnp.int32, (1, bodies), 1)
        segment = group_of[...] + (body_lane // (bodies // leaves)) * GROUPS
        onehot = (
            lax.broadcasted_iota(jnp.int32, (LANES, bodies), 0)
            == jnp.broadcast_to(segment, (LANES, bodies))
        ).astype(jnp.bfloat16)
        moments = jnp.concatenate(
            [gpos * gmass, gmass, jnp.zeros((4, bodies), jnp.float32)], axis=0
        )
        sums = lax.dot_general(
            jnp.concatenate(split(moments), axis=0).astype(jnp.bfloat16),
            onehot,
            (((1,), (1,)), ((), ())),
            preferred_element_type=jnp.float32,
        )
        sums = sums[0:8] + sums[8:16] + sums[16:24]
        cells = jnp.where(row8 < 3, sums / spread(sums[3:4]), sums)
        cell_own[...] = cells

        square = (n_wide, n_wide)
        diagonal = lax.broadcasted_iota(jnp.int32, square, 0) == lax.broadcasted_iota(
            jnp.int32, square, 1
        )
        listed = jnp.broadcast_to(let_send[...].astype(jnp.float32), square)
        chosen = jnp.sum(jnp.where(diagonal, listed, 0.0), axis=1, keepdims=True)
        chosen = jnp.broadcast_to(chosen, (n_wide, LANES)).astype(jnp.int32)
        place = lax.rem(wide, slots)
        turn = jnp.bitwise_and(place - chosen, slots - 1)
        turn = jnp.where(jnp.logical_and(group == place, chosen >= 0), turn, slots)
        turned = [
            (cells if k == 0 else pltpu.roll(cells, k * GROUPS, 1))[0:4] for k in range(slots)
        ]
        for w in range(n_wide):
            taken = jnp.broadcast_to(turn[w : w + 1], (4, LANES))
            outgoing = jnp.zeros((4, LANES), jnp.float32)
            for k in range(slots):
                outgoing = jnp.where(taken == k, turned[k], outgoing)
            cell_out[w] = outgoing
        cell_in[wide] = jnp.zeros((4, LANES), jnp.float32)

    cells_first = jnp.logical_or(lax.rem(wide, 2) == 0, narrow < n_narrow // 2)

    def order(i):
        @pl.when(jnp.equal(i == 0, cells_first))
        def _():
            make_cells()

        @pl.when(jnp.not_equal(i == 0, cells_first))
        def _():
            meet()

    run(0, 2, order)

    @pl.when(jnp.logical_not(cells_first))
    def _():
        run(0, wide, send_cells)

    gpos, gmass = gal_in[0], masses[0]

    both = jnp.concatenate([pos4, vel4], axis=0)
    targets = jnp.transpose(
        jnp.concatenate([both, jnp.zeros((ROWS, LANES - stars), jnp.float32)], axis=1)
    )
    zero = jnp.zeros((ROWS, LANES), jnp.float32)

    own = [spread(cell_own[c : c + 1, :]) for c in range(4)]
    star_groups = stars // ROWS
    for t in range(star_groups):
        rows = targets[t * ROWS : (t + 1) * ROWS, :]
        place = [column(rows, c) for c in range(3)]
        for c in range(3):
            aims[t, c] = place[c]
            aims[t, 3 + c] = column(rows, 4 + c)
            star_sum[t, 3 + c] = zero
        for c, value in enumerate(pull(own[:3], own[3], place, (zero,) * 3)):
            star_sum[t, c] = value

    last4 = lax.broadcasted_iota(jnp.int32, (4, bodies), 0) == 3
    high, mid, low = split(jnp.concatenate([-2.0 * gpos, jnp.zeros_like(gmass)], axis=0))
    high = jnp.where(last4, 1.0, high)
    reach = split(norm(gpos) + soften_sq)
    blank = jnp.zeros_like(gmass)
    aimed[...] = jnp.concatenate(
        [high, mid, high, low, high, mid, *reach, blank, blank, blank, blank, blank],
        axis=0,
    ).astype(jnp.bfloat16)

    def on_bodies(rows, total):
        square = norm(rows[0:3])
        high, mid, low = split(jnp.concatenate([rows[0:3], square], axis=0))
        ones = jnp.ones(rows.shape, jnp.float32)
        turned = jnp.transpose(
            jnp.concatenate([high, high, mid, high, low, mid, ones, rows], axis=0)
        )
        reach = jnp.dot(
            turned.astype(jnp.bfloat16), aimed[...], preferred_element_type=jnp.float32
        )
        total = [list(part) for part in total]
        for g in range(rows.shape[1] // ROWS):
            some = turned[g * ROWS : (g + 1) * ROWS, :]
            place = [column(some, 28 + c) for c in range(3)]
            mass = column(some, 31)
            for t in every:
                inverse = lax.rsqrt(
                    reach[g * ROWS : (g + 1) * ROWS, t * LANES : (t + 1) * LANES]
                )
                weight = mass * inverse * (inverse * inverse)
                for c in range(3):
                    total[t][c] = total[t][c] + place[c] * weight
                total[t][3] = total[t][3] + weight
        return total

    def keep(total):
        for t in every:
            for c in range(4):
                body_sum[4 * t + c] = total[t][c]

    def kept():
        return [[body_sum[4 * t + c] for c in range(4)] for t in every]

    def cells_on_stars(rows, t):
        place = [aims[t, c] for c in range(3)]
        return pull(rows[:3], rows[3], place, [star_sum[t, c] for c in range(3)])

    total = [[zero] * 4 for _ in every]
    for t in every:
        tile = slice(t * LANES, (t + 1) * LANES)
        total = on_bodies(jnp.concatenate([gpos[:, tile], gmass[:, tile]], axis=0), total)
    keep(total)

    def larger(w):
        rest = jnp.where(w == wide, n_narrow - 1 - narrow, 0)
        return jnp.where(w > wide, n_narrow, rest)

    def answer(q):
        count = larger(2 * q) + larger(2 * q + 1)

        @pl.when(count > 0)
        def _():
            pl.semaphore_wait(enter_sem.at[q], count)

        def to_group(w):
            @pl.when(w == wide)
            def _():
                run(narrow + 1, n_narrow, send_beside)

            @pl.when(w > wide)
            def _():
                answer_group(w)
                send_cells(w)

        run(2 * q, 2 * q + 2, to_group)

    halves = n_wide // 2
    lower = wide < n_wide // 4


    def gather(n, even):
        even_block, odd_block = states[n * n_wide + even], states[n * n_wide + even + 1]
        rows = jnp.where(left, even_block, odd_block)
        speeds = pltpu.roll(jnp.where(left, odd_block, even_block), stars, 1)
        return rows, speeds

    def near_arrived(q):
        own = wide // 2 == q

        def wait(count):
            some = states.at[pl.ds(0, count)]
            pltpu.make_async_copy(some, some, near_sem.at[q]).wait()

        @pl.when(own)
        def _():
            wait(2)

        @pl.when(jnp.logical_not(own))
        def _():
            wait(4)

    def near_stars(even):
        near, _ = gather(narrow, even)
        if kicks == n_wide:
            return [near]
        padded = jnp.concatenate([near, jnp.zeros((4, LANES), jnp.float32)], axis=0)
        cols[pl.ds(pl.multiple_of(even * stars, LANES), LANES), :] = jnp.transpose(padded)
        return []

    def near_cells(e):
        cells = cell_in[e * slots]
        for k in range(1, slots):
            cells = cells + cell_in[e * slots + k]
        rows = [spread(cells[c : c + 1]) for c in range(4)]
        for t in range(star_groups):
            for c, value in enumerate(cells_on_stars(rows, t)):
                star_sum[t, c] = value
        return [cells]

    def rest_arrived(q):
        some = states.at[pl.ds(0, 2 * (n_narrow - 1))]
        pltpu.make_async_copy(some, some, pass_sem.at[q]).wait()

    def all_stars(even, take):
        for n in range(n_narrow):
            rows, speeds = gather(n, even)
            srow[n, 0:4, :] = rows
            srow[n, 4:8, :] = speeds
        sources = [
            [spread(srow[n, c : c + 1, :]) for c in range(7)] for n in range(n_narrow)
        ]
        for t in range(star_groups):
            place = [aims[t, c] for c in range(3)]
            speed = [aims[t, 3 + c] for c in range(3)]
            acc = [star_sum[t, c] for c in range(6)]
            for rows in sources:
                dx, dy, dz = (rows[c] - place[c] for c in range(3))
                ux, uy, uz = (rows[4 + c] - speed[c] for c in range(3))
                inverse = lax.rsqrt(dx * dx + dy * dy + dz * dz + soften_sq)
                square = inverse * inverse
                weight = rows[3] * inverse * square
                approach = 3.0 * (dx * ux + dy * uy + dz * uz) * square
                acc = [
                    acc[0] + dx * weight,
                    acc[1] + dy * weight,
                    acc[2] + dz * weight,
                    acc[3] + (ux - dx * approach) * weight,
                    acc[4] + (uy - dy * approach) * weight,
                    acc[5] + (uz - dz * approach) * weight,
                ]
            take(t, acc)

    def store(t, acc):
        for c in range(6):
            star_sum[t, c] = acc[c]

    pairs_per_row = slots // 2

    def nearby(q):
        near = near_stars(2 * q) + near_cells(q // pairs_per_row)
        return on_bodies(jnp.concatenate(near, axis=1), kept())

    first = wide < n_wide // 8

    def turn(p):
        run(
            jnp.where(p == 0, wide // 2, jnp.where(jnp.logical_and(first, p == 1), 2, halves)),
            jnp.where(jnp.logical_and(first, p == 0), 2, halves),
            answer,
        )
        q = jnp.where(lower, p, halves - 1 - p)
        near_arrived(q)
        second = lax.rem(p, pairs_per_row) == pairs_per_row - 1

        @pl.when(second)
        def _():
            keep(nearby(q))
            rest_arrived(q)
            all_stars(2 * q, store)

        @pl.when(jnp.logical_not(second))
        def _():
            rest_arrived(q)
            for rows in near_stars(2 * q):
                keep(on_bodies(rows, kept()))
            all_stars(2 * q, store)

    run(0, halves - 1, turn)

    last = jnp.where(lower, halves - 1, 0)
    near_arrived(last)
    total = nearby(last)
    for t in every:
        tile = slice(t * LANES, (t + 1) * LANES)
        near = [gpos[c : c + 1, tile] for c in range(3)]
        pieces = [jnp.sum(part, axis=0, keepdims=True) for part in total[t]]
        pieces = [pieces[c] - near[c] * pieces[3] for c in range(3)]
        if kicks != n_wide:
            here = [spread(row) for row in near]

            def kick(k, acc):
                listed = star_leaf[t * leaves // tiles, k]

                def some(g, acc):
                    at = pl.multiple_of(listed * stars + g * ROWS, ROWS)
                    source = cols[pl.ds(at, ROWS), :]
                    place = [column(source, c) for c in range(3)]
                    return pull(place, column(source, 3), here, acc)

                return loop(stars // ROWS, some, acc)

            kicked = lax.fori_loop(0, kicks, kick, (zero,) * 3)
            for c in range(3):
                pieces[c] = pieces[c] + jnp.sum(kicked[c], axis=0, keepdims=True)
        for c in range(3):
            out[c : c + 1, tile] = gal_in[1, c : c + 1, tile] + time_step * pieces[c]

    pieces = []

    def finish(t, acc):
        piece = jnp.zeros((ROWS, LANES), jnp.float32)
        for c in range(6):
            piece = jnp.where(lane8 == c, jnp.sum(acc[c], axis=1, keepdims=True), piece)
        pieces.append(piece)

    rest_arrived(last)
    all_stars(2 * last, finish)
    result = jnp.transpose(jnp.concatenate(pieces, axis=0))
    new_acc, new_jerk = result[0:3], result[3:6]
    vel_new = (
        svel + time_step * 0.5 * (sacc + new_acc) + step_sq / 12.0 * (sjerk - new_jerk)
    )
    vel_at = bodies + LANES
    out[:, vel_at : vel_at + stars] = vel_new
    out[:, bodies : bodies + stars] = (
        spos + time_step * 0.5 * (svel + vel_new) + step_sq / 12.0 * (sacc - new_acc)
    )

    sent = states.at[pl.ds(0, n_wide * (n_narrow + 1) - 2)]
    pltpu.make_async_copy(sent, sent, send_sem).wait()


def unpack(packed, gal_out, pos_out, vel_out):
    bodies, stars = gal_out.shape[1], pos_out.shape[1]
    gal_out[...] = packed[:, 0:bodies]
    pos_out[...] = packed[:, bodies : bodies + stars]
    vel_out[...] = packed[:, bodies + LANES : bodies + LANES + stars]


def body(
    n_wide,
    n_narrow,
    star_pos,
    star_vel,
    star_mass,
    star_acc,
    star_jerk,
    gal_pos,
    gal_vel,
    gal_mass,
    group_of,
    let_send,
    star_leaf,
):
    stars, bodies = star_pos.shape[1], gal_pos.shape[1]
    vmem = pl.BlockSpec(memory_space=pltpu.VMEM)
    f32 = jnp.float32
    i32 = jnp.int32
    hbm = pl.BlockSpec(memory_space=pltpu.HBM)
    packed = pl.pallas_call(
        functools.partial(kernel, n_wide, n_narrow),
        out_shape=jax.ShapeDtypeStruct((3, bodies + 2 * LANES), f32),
        in_specs=[hbm] * 11,
        out_specs=vmem,
        scratch_shapes=[
            pltpu.VMEM((4, 3, stars), f32),
            pltpu.VMEM((1, stars), f32),
            pltpu.VMEM((2, 3, bodies), f32),
            pltpu.VMEM((2, 1, bodies), f32),
            pltpu.VMEM((1, bodies), i32),
            pltpu.VMEM((1, n_wide), i32),
            pltpu.SMEM(star_leaf.shape, i32),
            pltpu.SemaphoreType.DMA((5 + (star_leaf.shape[1] != n_wide),)),
            pltpu.VMEM(((n_narrow + 1) * n_wide, 4, LANES), f32),
            pltpu.VMEM((ROWS, LANES), f32),
            pltpu.VMEM((n_wide, 4, LANES), f32),
            pltpu.VMEM((n_wide, 4, LANES), f32),
            pltpu.VMEM((32, bodies), jnp.bfloat16),
            pltpu.VMEM((n_wide * stars, ROWS), f32),
            pltpu.VMEM((n_narrow, ROWS, LANES), f32),
            pltpu.VMEM((stars // ROWS, 6, ROWS, LANES), f32),
            pltpu.VMEM((4 * bodies // LANES, ROWS, LANES), f32),
            pltpu.VMEM((stars // ROWS, 6, ROWS, LANES), f32),
            pltpu.SemaphoreType.DMA,
            pltpu.SemaphoreType.DMA((n_wide // 2,)),
            pltpu.SemaphoreType.DMA((n_wide // 2,)),
            pltpu.SemaphoreType.REGULAR((n_wide // 2,)),
        ],
        compiler_params=pltpu.CompilerParams(
            collective_id=0, has_side_effects=True, vmem_limit_bytes=24 << 20
        ),
    )(
        *(
            pltpu.with_memory_space_constraint(array, pltpu.HBM)
            for array in (
                star_pos,
                star_vel,
                star_mass.reshape(1, stars),
                star_acc,
                star_jerk,
                gal_pos,
                gal_vel,
                gal_mass.reshape(1, bodies),
                group_of.reshape(1, bodies),
                let_send.reshape(1, n_wide),
                star_leaf,
            )
        )
    )
    return pl.pallas_call(
        unpack,
        out_shape=(
            jax.ShapeDtypeStruct(gal_vel.shape, f32),
            jax.ShapeDtypeStruct(star_pos.shape, f32),
            jax.ShapeDtypeStruct(star_vel.shape, f32),
        ),
        in_specs=[vmem],
        out_specs=(vmem,) * 3,
        compiler_params=pltpu.CompilerParams(vmem_limit_bytes=1 << 20),
    )(packed)


def solution(mesh):
    both = ("wide", "narrow")
    columns, flat = P(None, both), P(both)
    return jax.shard_map(
        functools.partial(body, mesh.shape["wide"], mesh.shape["narrow"]),
        mesh=mesh,
        in_specs=(
            columns,
            columns,
            flat,
            columns,
            columns,
            columns,
            columns,
            flat,
            flat,
            P(both, None, None),
            P(both, None),
        ),
        out_specs=(columns, columns, columns),
        check_vma=False,
    )
```

```python
import functools

import jax
import jax.numpy as jnp
from jax import lax
from jax.experimental import pallas as pl
from jax.experimental.pallas import tpu as pltpu
from jax.sharding import PartitionSpec as P

GROUPS = 32
LANES = 128
ROWS = 8
MESH = pl.DeviceIdType.MESH

time_step = 0.25
soften_sq = 0.05


def loop(count, step, init, most=4):
    unroll = next(u for u in range(min(most, count), 0, -1) if count % u == 0)
    return lax.fori_loop(0, count, step, init, unroll=unroll)


def spread(row):
    return jnp.broadcast_to(row, (ROWS, row.shape[1]))


def column(block, index):
    return jnp.broadcast_to(block[:, index : index + 1], (ROWS, LANES))


def pull(source, mass, target, total):
    dx, dy, dz = (s - t for s, t in zip(source, target))
    inverse = lax.rsqrt(dx * dx + dy * dy + dz * dz + soften_sq)
    weight = mass * inverse * inverse * inverse
    return (total[0] + dx * weight, total[1] + dy * weight, total[2] + dz * weight)


def norm(rows):
    return rows[0:1] * rows[0:1] + rows[1:2] * rows[1:2] + rows[2:3] * rows[2:3]


def split(value):
    parts = []
    for _ in range(3):
        parts.append(value.astype(jnp.bfloat16).astype(jnp.float32))
        value = value - parts[-1]
    return parts


def kernel(
    n_wide,
    n_narrow,
    star_pos_hbm,
    star_vel_hbm,
    star_mass_hbm,
    star_acc_hbm,
    star_jerk_hbm,
    gal_pos_hbm,
    gal_vel_hbm,
    gal_mass_hbm,
    group_of_hbm,
    let_send_hbm,
    star_leaf_hbm,
    out,
    star_in,
    star_mass,
    gal_in,
    masses,
    group_of,
    let_send,
    star_leaf,
    in_sem,
    states,
    cell_own,
    cell_out,
    cell_in,
    aimed,
    cols,
    srow,
    aims,
    body_sum,
    star_sum,
    send_sem,
    near_sem,
    pass_sem,
    enter_sem,
):
    wide, narrow = lax.axis_index("wide"), lax.axis_index("narrow")
    stars, bodies = star_in.shape[2], gal_in.shape[2]
    leaves, kicks = star_leaf.shape
    slots = LANES // GROUPS
    step_sq = time_step * time_step
    tiles = bodies // LANES
    every = tuple(range(tiles))

    fetches = [
        (star_pos_hbm, star_in.at[0], 0),
        (star_vel_hbm, star_in.at[1], 0),
        (star_acc_hbm, star_in.at[2], 0),
        (star_jerk_hbm, star_in.at[3], 0),
        (star_mass_hbm, star_mass, 1),
        (gal_pos_hbm, gal_in.at[0], 2),
        (gal_vel_hbm, gal_in.at[1], 2),
        (gal_mass_hbm, masses.at[0], 3),
        (group_of_hbm, group_of, 3),
        (let_send_hbm, let_send, 4),
    ]
    if kicks != n_wide:
        fetches.append((star_leaf_hbm, star_leaf, 5))
    for source, target, i in fetches:
        pltpu.make_async_copy(source, target, in_sem.at[i]).start()

    def fetched(*refs):
        for ref, i in refs:
            pltpu.make_async_copy(ref, ref, in_sem.at[i]).wait()

    barrier = pltpu.get_barrier_semaphore()
    half = n_narrow // 2
    others = [lax.rem(narrow + half + m, n_narrow) for m in range(n_narrow) if m != half]

    def run(first, last, step):
        def body(i, carry):
            step(i)
            return carry

        lax.fori_loop(first, last, body, 0)

    def signal(sem, w, n):
        pl.semaphore_signal(sem, inc=1, device_id=(w, n), device_id_type=MESH)

    def signal_group(sem, w):
        for n in range(n_narrow):
            signal(sem, w, n)

    run(narrow + 1, n_narrow, lambda n: signal(barrier, wide, n))
    run(wide + 1, n_wide, lambda w: signal_group(barrier, w))

    lane = lax.broadcasted_iota(jnp.int32, (1, LANES), 1)
    lane4 = lax.broadcasted_iota(jnp.int32, (4, LANES), 1)
    lane8 = lax.broadcasted_iota(jnp.int32, (ROWS, LANES), 1)
    row8 = lax.broadcasted_iota(jnp.int32, (ROWS, LANES), 0)
    left = lane4 < stars

    fetched((star_in, 0), (star_mass, 1))
    spos, svel, sacc, sjerk = (star_in[i] for i in range(4))
    pred_pos = (
        spos + time_step * svel + step_sq * 0.5 * sacc + step_sq * time_step / 6.0 * sjerk
    )
    pred_vel = svel + time_step * sacc + step_sq * 0.5 * sjerk
    pos4 = jnp.concatenate([pred_pos, star_mass[...]], axis=0)
    vel4 = jnp.concatenate([pred_vel, jnp.zeros((1, stars), jnp.float32)], axis=0)
    block = jnp.concatenate([pos4, vel4], axis=1)
    block = jnp.where(lax.rem(wide, 2) == 0, block, pltpu.roll(block, stars, 1))
    mine = narrow * n_wide + wide
    states[mine] = block

    def send_state(w, n, recvs):
        pltpu.make_async_remote_copy(
            src_ref=states.at[mine],
            dst_ref=states.at[mine],
            send_sem=send_sem,
            recv_sem=recvs.at[wide // 2],
            device_id=(w, n),
            device_id_type=MESH,
        ).start()

    def send_group(w):
        send_state(w, narrow, near_sem)
        for n in others:
            send_state(w, n, pass_sem)

    def answer_group(w):
        for n in others:
            send_state(w, n, pass_sem)
        send_state(w, narrow, near_sem)

    def send_beside(n):
        send_state(wide, n, pass_sem)

    def send_cells(w):
        pltpu.make_async_remote_copy(
            src_ref=cell_out.at[w],
            dst_ref=cell_in.at[wide],
            send_sem=send_sem,
            recv_sem=near_sem.at[wide // 2],
            device_id=(w, narrow),
            device_id_type=MESH,
        ).start()

    group = lane // GROUPS

    def meet():
        smaller = wide * n_narrow + narrow

        @pl.when(smaller > 0)
        def _():
            pl.semaphore_wait(barrier, smaller)

        def send_down(w):
            send_group(w)

            @pl.when(cells_first)
            def _():
                send_cells(w)

        one = jnp.where(lax.rem(wide, 2) == 0, 0, jnp.minimum(wide, 1))
        run(0, one, send_down)
        run(0, wide, lambda w: signal_group(enter_sem.at[wide // 2], w))
        run(0, narrow, lambda n: signal(enter_sem.at[wide // 2], wide, n))
        run(one, wide, send_down)
        run(0, narrow, send_beside)

    def make_cells():
        fetched((gal_in, 2), (masses, 3), (let_send, 4))
        if kicks != n_wide:
            fetched((star_leaf, 5))
        gpos, gmass = gal_in[0], masses[0]
        body_lane = lax.broadcasted_iota(jnp.int32, (1, bodies), 1)
        segment = group_of[...] + (body_lane // (bodies // leaves)) * GROUPS
        onehot = (
            lax.broadcasted_iota(jnp.int32, (LANES, bodies), 0)
            == jnp.broadcast_to(segment, (LANES, bodies))
        ).astype(jnp.bfloat16)
        moments = jnp.concatenate(
            [gpos * gmass, gmass, jnp.zeros((4, bodies), jnp.float32)], axis=0
        )
        sums = lax.dot_general(
            jnp.concatenate(split(moments), axis=0).astype(jnp.bfloat16),
            onehot,
            (((1,), (1,)), ((), ())),
            preferred_element_type=jnp.float32,
        )
        sums = sums[0:8] + sums[8:16] + sums[16:24]
        cells = jnp.where(row8 < 3, sums / spread(sums[3:4]), sums)
        cell_own[...] = cells

        square = (n_wide, n_wide)
        diagonal = lax.broadcasted_iota(jnp.int32, square, 0) == lax.broadcasted_iota(
            jnp.int32, square, 1
        )
        listed = jnp.broadcast_to(let_send[...].astype(jnp.float32), square)
        chosen = jnp.sum(jnp.where(diagonal, listed, 0.0), axis=1, keepdims=True)
        chosen = jnp.broadcast_to(chosen, (n_wide, LANES)).astype(jnp.int32)
        place = lax.rem(wide, slots)
        turn = jnp.bitwise_and(place - chosen, slots - 1)
        turn = jnp.where(jnp.logical_and(group == place, chosen >= 0), turn, slots)
        turned = [
            (cells if k == 0 else pltpu.roll(cells, k * GROUPS, 1))[0:4] for k in range(slots)
        ]
        for w in range(n_wide):
            taken = jnp.broadcast_to(turn[w : w + 1], (4, LANES))
            outgoing = jnp.zeros((4, LANES), jnp.float32)
            for k in range(slots):
                outgoing = jnp.where(taken == k, turned[k], outgoing)
            cell_out[w] = outgoing
        cell_in[wide] = jnp.zeros((4, LANES), jnp.float32)

    cells_first = jnp.logical_or(lax.rem(wide, 2) == 0, narrow < n_narrow // 2)

    def order(i):
        @pl.when(jnp.equal(i == 0, cells_first))
        def _():
            make_cells()

        @pl.when(jnp.not_equal(i == 0, cells_first))
        def _():
            meet()

    run(0, 2, order)

    @pl.when(jnp.logical_not(cells_first))
    def _():
        run(0, wide, send_cells)

    gpos, gmass = gal_in[0], masses[0]

    both = jnp.concatenate([pos4, vel4], axis=0)
    targets = jnp.transpose(
        jnp.concatenate([both, jnp.zeros((ROWS, LANES - stars), jnp.float32)], axis=1)
    )
    zero = jnp.zeros((ROWS, LANES), jnp.float32)

    own = [spread(cell_own[c : c + 1, :]) for c in range(4)]
    star_groups = stars // ROWS
    for t in range(star_groups):
        rows = targets[t * ROWS : (t + 1) * ROWS, :]
        place = [column(rows, c) for c in range(3)]
        for c in range(3):
            aims[t, c] = place[c]
            aims[t, 3 + c] = column(rows, 4 + c)
            star_sum[t, 3 + c] = zero
        for c, value in enumerate(pull(own[:3], own[3], place, (zero,) * 3)):
            star_sum[t, c] = value

    last4 = lax.broadcasted_iota(jnp.int32, (4, bodies), 0) == 3
    high, mid, low = split(jnp.concatenate([-2.0 * gpos, jnp.zeros_like(gmass)], axis=0))
    high = jnp.where(last4, 1.0, high)
    reach = split(norm(gpos) + soften_sq)
    blank = jnp.zeros_like(gmass)
    aimed[...] = jnp.concatenate(
        [high, mid, high, low, high, mid, *reach, blank, blank, blank, blank, blank],
        axis=0,
    ).astype(jnp.bfloat16)

    def on_bodies(rows, total):
        square = norm(rows[0:3])
        high, mid, low = split(jnp.concatenate([rows[0:3], square], axis=0))
        ones = jnp.ones(rows.shape, jnp.float32)
        turned = jnp.transpose(
            jnp.concatenate([high, high, mid, high, low, mid, ones, rows], axis=0)
        )
        reach = jnp.dot(
            turned.astype(jnp.bfloat16), aimed[...], preferred_element_type=jnp.float32
        )
        total = [list(part) for part in total]
        for g in range(rows.shape[1] // ROWS):
            some = turned[g * ROWS : (g + 1) * ROWS, :]
            place = [column(some, 28 + c) for c in range(3)]
            mass = column(some, 31)
            for t in every:
                inverse = lax.rsqrt(
                    reach[g * ROWS : (g + 1) * ROWS, t * LANES : (t + 1) * LANES]
                )
                weight = mass * inverse * (inverse * inverse)
                for c in range(3):
                    total[t][c] = total[t][c] + place[c] * weight
                total[t][3] = total[t][3] + weight
        return total

    def keep(total):
        for t in every:
            for c in range(4):
                body_sum[4 * t + c] = total[t][c]

    def kept():
        return [[body_sum[4 * t + c] for c in range(4)] for t in every]

    def cells_on_stars(rows, t):
        place = [aims[t, c] for c in range(3)]
        return pull(rows[:3], rows[3], place, [star_sum[t, c] for c in range(3)])

    total = [[zero] * 4 for _ in every]
    for t in every:
        tile = slice(t * LANES, (t + 1) * LANES)
        total = on_bodies(jnp.concatenate([gpos[:, tile], gmass[:, tile]], axis=0), total)
    keep(total)

    def larger(w):
        rest = jnp.where(w == wide, n_narrow - 1 - narrow, 0)
        return jnp.where(w > wide, n_narrow, rest)

    def answer(q):
        count = larger(2 * q) + larger(2 * q + 1)

        @pl.when(count > 0)
        def _():
            pl.semaphore_wait(enter_sem.at[q], count)

        def to_group(w):
            @pl.when(w == wide)
            def _():
                run(narrow + 1, n_narrow, send_beside)

            @pl.when(w > wide)
            def _():
                answer_group(w)
                send_cells(w)

        run(2 * q, 2 * q + 2, to_group)

    halves = n_wide // 2
    lower = wide < n_wide // 4


    def gather(n, even):
        even_block, odd_block = states[n * n_wide + even], states[n * n_wide + even + 1]
        rows = jnp.where(left, even_block, odd_block)
        speeds = pltpu.roll(jnp.where(left, odd_block, even_block), stars, 1)
        return rows, speeds

    def near_arrived(q):
        own = wide // 2 == q

        def wait(count):
            some = states.at[pl.ds(0, count)]
            pltpu.make_async_copy(some, some, near_sem.at[q]).wait()

        @pl.when(own)
        def _():
            wait(2)

        @pl.when(jnp.logical_not(own))
        def _():
            wait(4)

    def near_stars(even):
        near, _ = gather(narrow, even)
        if kicks == n_wide:
            return [near]
        padded = jnp.concatenate([near, jnp.zeros((4, LANES), jnp.float32)], axis=0)
        cols[pl.ds(pl.multiple_of(even * stars, LANES), LANES), :] = jnp.transpose(padded)
        return []

    def near_cells(e):
        cells = cell_in[e * slots]
        for k in range(1, slots):
            cells = cells + cell_in[e * slots + k]
        rows = [spread(cells[c : c + 1]) for c in range(4)]
        for t in range(star_groups):
            for c, value in enumerate(cells_on_stars(rows, t)):
                star_sum[t, c] = value
        return [cells]

    def rest_arrived(q):
        some = states.at[pl.ds(0, 2 * (n_narrow - 1))]
        pltpu.make_async_copy(some, some, pass_sem.at[q]).wait()

    def all_stars(even, take):
        for n in range(n_narrow):
            rows, speeds = gather(n, even)
            srow[n, 0:4, :] = rows
            srow[n, 4:8, :] = speeds
        sources = [
            [spread(srow[n, c : c + 1, :]) for c in range(7)] for n in range(n_narrow)
        ]
        for t in range(star_groups):
            place = [aims[t, c] for c in range(3)]
            speed = [aims[t, 3 + c] for c in range(3)]
            acc = [star_sum[t, c] for c in range(6)]
            for rows in sources:
                dx, dy, dz = (rows[c] - place[c] for c in range(3))
                ux, uy, uz = (rows[4 + c] - speed[c] for c in range(3))
                inverse = lax.rsqrt(dx * dx + dy * dy + dz * dz + soften_sq)
                square = inverse * inverse
                weight = rows[3] * inverse * square
                approach = 3.0 * (dx * ux + dy * uy + dz * uz) * square
                acc = [
                    acc[0] + dx * weight,
                    acc[1] + dy * weight,
                    acc[2] + dz * weight,
                    acc[3] + (ux - dx * approach) * weight,
                    acc[4] + (uy - dy * approach) * weight,
                    acc[5] + (uz - dz * approach) * weight,
                ]
            take(t, acc)

    def store(t, acc):
        for c in range(6):
            star_sum[t, c] = acc[c]

    pairs_per_row = slots // 2

    def nearby(q):
        near = near_stars(2 * q) + near_cells(q // pairs_per_row)
        return on_bodies(jnp.concatenate(near, axis=1), kept())

    first = wide < n_wide // 8

    def turn(p):
        run(
            jnp.where(p == 0, wide // 2, jnp.where(jnp.logical_and(first, p == 1), 2, halves)),
            jnp.where(jnp.logical_and(first, p == 0), 2, halves),
            answer,
        )
        q = jnp.where(lower, p, halves - 1 - p)
        near_arrived(q)
        second = lax.rem(p, pairs_per_row) == pairs_per_row - 1

        @pl.when(second)
        def _():
            rest_arrived(q)
            keep(nearby(q))
            all_stars(2 * q, store)

        @pl.when(jnp.logical_not(second))
        def _():
            rest_arrived(q)
            for rows in near_stars(2 * q):
                keep(on_bodies(rows, kept()))
            all_stars(2 * q, store)

    run(0, halves - 1, turn)

    last = jnp.where(lower, halves - 1, 0)
    near_arrived(last)
    total = nearby(last)
    for t in every:
        tile = slice(t * LANES, (t + 1) * LANES)
        near = [gpos[c : c + 1, tile] for c in range(3)]
        pieces = [jnp.sum(part, axis=0, keepdims=True) for part in total[t]]
        pieces = [pieces[c] - near[c] * pieces[3] for c in range(3)]
        if kicks != n_wide:
            here = [spread(row) for row in near]

            def kick(k, acc):
                listed = star_leaf[t * leaves // tiles, k]

                def some(g, acc):
                    at = pl.multiple_of(listed * stars + g * ROWS, ROWS)
                    source = cols[pl.ds(at, ROWS), :]
                    place = [column(source, c) for c in range(3)]
                    return pull(place, column(source, 3), here, acc)

                return loop(stars // ROWS, some, acc)

            kicked = lax.fori_loop(0, kicks, kick, (zero,) * 3)
            for c in range(3):
                pieces[c] = pieces[c] + jnp.sum(kicked[c], axis=0, keepdims=True)
        for c in range(3):
            out[c : c + 1, tile] = gal_in[1, c : c + 1, tile] + time_step * pieces[c]

    pieces = []

    def finish(t, acc):
        piece = jnp.zeros((ROWS, LANES), jnp.float32)
        for c in range(6):
            piece = jnp.where(lane8 == c, jnp.sum(acc[c], axis=1, keepdims=True), piece)
        pieces.append(piece)

    sent = states.at[pl.ds(0, n_wide * (n_narrow + 1) - 2)]
    pltpu.make_async_copy(sent, sent, send_sem).wait()
    rest_arrived(last)
    all_stars(2 * last, finish)
    result = jnp.transpose(jnp.concatenate(pieces, axis=0))
    new_acc, new_jerk = result[0:3], result[3:6]
    vel_new = (
        svel + time_step * 0.5 * (sacc + new_acc) + step_sq / 12.0 * (sjerk - new_jerk)
    )
    vel_at = bodies + LANES
    out[:, vel_at : vel_at + stars] = vel_new
    out[:, bodies : bodies + stars] = (
        spos + time_step * 0.5 * (svel + vel_new) + step_sq / 12.0 * (sacc - new_acc)
    )


def unpack(packed, gal_out, pos_out, vel_out):
    bodies, stars = gal_out.shape[1], pos_out.shape[1]
    gal_out[...] = packed[:, 0:bodies]
    pos_out[...] = packed[:, bodies : bodies + stars]
    vel_out[...] = packed[:, bodies + LANES : bodies + LANES + stars]


def body(
    n_wide,
    n_narrow,
    star_pos,
    star_vel,
    star_mass,
    star_acc,
    star_jerk,
    gal_pos,
    gal_vel,
    gal_mass,
    group_of,
    let_send,
    star_leaf,
):
    stars, bodies = star_pos.shape[1], gal_pos.shape[1]
    vmem = pl.BlockSpec(memory_space=pltpu.VMEM)
    f32 = jnp.float32
    i32 = jnp.int32
    hbm = pl.BlockSpec(memory_space=pltpu.HBM)
    packed = pl.pallas_call(
        functools.partial(kernel, n_wide, n_narrow),
        out_shape=jax.ShapeDtypeStruct((3, bodies + 2 * LANES), f32),
        in_specs=[hbm] * 11,
        out_specs=vmem,
        scratch_shapes=[
            pltpu.VMEM((4, 3, stars), f32),
            pltpu.VMEM((1, stars), f32),
            pltpu.VMEM((2, 3, bodies), f32),
            pltpu.VMEM((2, 1, bodies), f32),
            pltpu.VMEM((1, bodies), i32),
            pltpu.VMEM((1, n_wide), i32),
            pltpu.SMEM(star_leaf.shape, i32),
            pltpu.SemaphoreType.DMA((5 + (star_leaf.shape[1] != n_wide),)),
            pltpu.VMEM(((n_narrow + 1) * n_wide, 4, LANES), f32),
            pltpu.VMEM((ROWS, LANES), f32),
            pltpu.VMEM((n_wide, 4, LANES), f32),
            pltpu.VMEM((n_wide, 4, LANES), f32),
            pltpu.VMEM((32, bodies), jnp.bfloat16),
            pltpu.VMEM((n_wide * stars, ROWS), f32),
            pltpu.VMEM((n_narrow, ROWS, LANES), f32),
            pltpu.VMEM((stars // ROWS, 6, ROWS, LANES), f32),
            pltpu.VMEM((4 * bodies // LANES, ROWS, LANES), f32),
            pltpu.VMEM((stars // ROWS, 6, ROWS, LANES), f32),
            pltpu.SemaphoreType.DMA,
            pltpu.SemaphoreType.DMA((n_wide // 2,)),
            pltpu.SemaphoreType.DMA((n_wide // 2,)),
            pltpu.SemaphoreType.REGULAR((n_wide // 2,)),
        ],
        compiler_params=pltpu.CompilerParams(
            collective_id=0, has_side_effects=True, vmem_limit_bytes=24 << 20
        ),
    )(
        *(
            pltpu.with_memory_space_constraint(array, pltpu.HBM)
            for array in (
                star_pos,
                star_vel,
                star_mass.reshape(1, stars),
                star_acc,
                star_jerk,
                gal_pos,
                gal_vel,
                gal_mass.reshape(1, bodies),
                group_of.reshape(1, bodies),
                let_send.reshape(1, n_wide),
                star_leaf,
            )
        )
    )
    return pl.pallas_call(
        unpack,
        out_shape=(
            jax.ShapeDtypeStruct(gal_vel.shape, f32),
            jax.ShapeDtypeStruct(star_pos.shape, f32),
            jax.ShapeDtypeStruct(star_vel.shape, f32),
        ),
        in_specs=[vmem],
        out_specs=(vmem,) * 3,
        compiler_params=pltpu.CompilerParams(vmem_limit_bytes=1 << 20),
    )(packed)


def solution(mesh):
    both = ("wide", "narrow")
    columns, flat = P(None, both), P(both)
    return jax.shard_map(
        functools.partial(body, mesh.shape["wide"], mesh.shape["narrow"]),
        mesh=mesh,
        in_specs=(
            columns,
            columns,
            flat,
            columns,
            columns,
            columns,
            columns,
            flat,
            flat,
            P(both, None, None),
            P(both, None),
        ),
        out_specs=(columns, columns, columns),
        check_vma=False,
    )
```

```python
import functools

import jax
import jax.numpy as jnp
from jax import lax
from jax.experimental import pallas as pl
from jax.experimental.pallas import tpu as pltpu
from jax.sharding import PartitionSpec as P

GROUPS = 32
LANES = 128
ROWS = 8
MESH = pl.DeviceIdType.MESH

time_step = 0.25
soften_sq = 0.05


def loop(count, step, init, most=4):
    unroll = next(u for u in range(min(most, count), 0, -1) if count % u == 0)
    return lax.fori_loop(0, count, step, init, unroll=unroll)


def spread(row):
    return jnp.broadcast_to(row, (ROWS, row.shape[1]))


def column(block, index):
    return jnp.broadcast_to(block[:, index : index + 1], (ROWS, LANES))


def pull(source, mass, target, total):
    dx, dy, dz = (s - t for s, t in zip(source, target))
    inverse = lax.rsqrt(dx * dx + dy * dy + dz * dz + soften_sq)
    weight = mass * inverse * inverse * inverse
    return (total[0] + dx * weight, total[1] + dy * weight, total[2] + dz * weight)


def norm(rows):
    return rows[0:1] * rows[0:1] + rows[1:2] * rows[1:2] + rows[2:3] * rows[2:3]


def split(value):
    parts = []
    for _ in range(3):
        parts.append(value.astype(jnp.bfloat16).astype(jnp.float32))
        value = value - parts[-1]
    return parts


def kernel(
    n_wide,
    n_narrow,
    star_pos_hbm,
    star_vel_hbm,
    star_mass_hbm,
    star_acc_hbm,
    star_jerk_hbm,
    gal_pos_hbm,
    gal_vel_hbm,
    gal_mass_hbm,
    group_of_hbm,
    let_send_hbm,
    star_leaf_hbm,
    out,
    star_in,
    star_mass,
    star_rows,
    gal_in,
    masses,
    group_of,
    let_send,
    star_leaf,
    in_sem,
    states,
    cell_own,
    cell_out,
    cell_in,
    aimed,
    cols,
    srow,
    aims,
    body_sum,
    star_sum,
    send_sem,
    near_sem,
    pass_sem,
    enter_sem,
):
    wide, narrow = lax.axis_index("wide"), lax.axis_index("narrow")
    stars, bodies = star_in.shape[2], gal_in.shape[2]
    leaves, kicks = star_leaf.shape
    slots = LANES // GROUPS
    step_sq = time_step * time_step
    tiles = bodies // LANES
    every = tuple(range(tiles))

    fetches = [
        (star_pos_hbm, star_in.at[0], 0),
        (star_vel_hbm, star_in.at[1], 0),
        (star_acc_hbm, star_in.at[2], 0),
        (star_jerk_hbm, star_in.at[3], 0),
        (star_mass_hbm, star_mass, 0),
        (gal_pos_hbm, gal_in.at[0], 1),
        (gal_vel_hbm, gal_in.at[1], 1),
        (gal_mass_hbm, masses.at[0], 2),
        (group_of_hbm, group_of, 2),
        (let_send_hbm, let_send, 3),
    ]
    if kicks != n_wide:
        fetches.append((star_leaf_hbm, star_leaf, 4))
    for source, target, i in fetches:
        pltpu.make_async_copy(source, target, in_sem.at[i]).start()

    def fetched(*refs):
        for ref, i in refs:
            pltpu.make_async_copy(ref, ref, in_sem.at[i]).wait()

    barrier = pltpu.get_barrier_semaphore()
    half = n_narrow // 2
    others = [lax.rem(narrow + half + m, n_narrow) for m in range(n_narrow) if m != half]

    def run(first, last, step):
        def body(i, carry):
            step(i)
            return carry

        lax.fori_loop(first, last, body, 0)

    def signal(sem, w, n):
        pl.semaphore_signal(sem, inc=1, device_id=(w, n), device_id_type=MESH)

    def signal_group(sem, w):
        for n in range(n_narrow):
            signal(sem, w, n)

    run(narrow + 1, n_narrow, lambda n: signal(barrier, wide, n))
    run(wide + 1, n_wide, lambda w: signal_group(barrier, w))

    lane = lax.broadcasted_iota(jnp.int32, (1, LANES), 1)
    lane4 = lax.broadcasted_iota(jnp.int32, (4, LANES), 1)
    lane8 = lax.broadcasted_iota(jnp.int32, (ROWS, LANES), 1)
    row8 = lax.broadcasted_iota(jnp.int32, (ROWS, LANES), 0)
    left = lane4 < stars

    fetched((star_rows, 0))
    spos, svel, sacc, sjerk = (star_in[i] for i in range(4))
    pred_pos = (
        spos + time_step * svel + step_sq * 0.5 * sacc + step_sq * time_step / 6.0 * sjerk
    )
    pred_vel = svel + time_step * sacc + step_sq * 0.5 * sjerk
    pos4 = jnp.concatenate([pred_pos, star_mass[...]], axis=0)
    vel4 = jnp.concatenate([pred_vel, jnp.zeros((1, stars), jnp.float32)], axis=0)
    block = jnp.concatenate([pos4, vel4], axis=1)
    block = jnp.where(lax.rem(wide, 2) == 0, block, pltpu.roll(block, stars, 1))
    mine = narrow * n_wide + wide
    states[mine] = block

    def send_state(w, n, recvs):
        pltpu.make_async_remote_copy(
            src_ref=states.at[mine],
            dst_ref=states.at[mine],
            send_sem=send_sem,
            recv_sem=recvs.at[wide // 2],
            device_id=(w, n),
            device_id_type=MESH,
        ).start()

    def send_group(w):
        send_state(w, narrow, near_sem)
        for n in others:
            send_state(w, n, pass_sem)

    def answer_group(w):
        for n in others:
            send_state(w, n, pass_sem)
        send_state(w, narrow, near_sem)

    def send_beside(n):
        send_state(wide, n, pass_sem)

    def send_cells(w):
        pltpu.make_async_remote_copy(
            src_ref=cell_out.at[w],
            dst_ref=cell_in.at[wide],
            send_sem=send_sem,
            recv_sem=near_sem.at[wide // 2],
            device_id=(w, narrow),
            device_id_type=MESH,
        ).start()

    group = lane // GROUPS

    def meet():
        smaller = wide * n_narrow + narrow

        @pl.when(smaller > 0)
        def _():
            pl.semaphore_wait(barrier, smaller)

        def send_down(w):
            send_group(w)

            @pl.when(cells_first)
            def _():
                send_cells(w)

        one = jnp.where(lax.rem(wide, 2) == 0, 0, jnp.minimum(wide, 1))
        run(0, one, send_down)
        run(0, wide, lambda w: signal_group(enter_sem.at[wide // 2], w))
        run(0, narrow, lambda n: signal(enter_sem.at[wide // 2], wide, n))
        run(one, wide, send_down)
        run(0, narrow, send_beside)

    def make_cells():
        fetched((gal_in, 1), (masses, 2), (let_send, 3))
        if kicks != n_wide:
            fetched((star_leaf, 4))
        gpos, gmass = gal_in[0], masses[0]
        body_lane = lax.broadcasted_iota(jnp.int32, (1, bodies), 1)
        segment = group_of[...] + (body_lane // (bodies // leaves)) * GROUPS
        onehot = (
            lax.broadcasted_iota(jnp.int32, (LANES, bodies), 0)
            == jnp.broadcast_to(segment, (LANES, bodies))
        ).astype(jnp.bfloat16)
        moments = jnp.concatenate(
            [gpos * gmass, gmass, jnp.zeros((4, bodies), jnp.float32)], axis=0
        )
        sums = lax.dot_general(
            jnp.concatenate(split(moments), axis=0).astype(jnp.bfloat16),
            onehot,
            (((1,), (1,)), ((), ())),
            preferred_element_type=jnp.float32,
        )
        sums = sums[0:8] + sums[8:16] + sums[16:24]
        cells = jnp.where(row8 < 3, sums / spread(sums[3:4]), sums)
        cell_own[...] = cells

        square = (n_wide, n_wide)
        diagonal = lax.broadcasted_iota(jnp.int32, square, 0) == lax.broadcasted_iota(
            jnp.int32, square, 1
        )
        listed = jnp.broadcast_to(let_send[...].astype(jnp.float32), square)
        chosen = jnp.sum(jnp.where(diagonal, listed, 0.0), axis=1, keepdims=True)
        chosen = jnp.broadcast_to(chosen, (n_wide, LANES)).astype(jnp.int32)
        place = lax.rem(wide, slots)
        turn = jnp.bitwise_and(place - chosen, slots - 1)
        turn = jnp.where(jnp.logical_and(group == place, chosen >= 0), turn, slots)
        turned = [
            (cells if k == 0 else pltpu.roll(cells, k * GROUPS, 1))[0:4] for k in range(slots)
        ]
        for w in range(n_wide):
            taken = jnp.broadcast_to(turn[w : w + 1], (4, LANES))
            outgoing = jnp.zeros((4, LANES), jnp.float32)
            for k in range(slots):
                outgoing = jnp.where(taken == k, turned[k], outgoing)
            cell_out[w] = outgoing
        cell_in[wide] = jnp.zeros((4, LANES), jnp.float32)

    cells_first = jnp.logical_or(lax.rem(wide, 2) == 0, narrow < n_narrow // 2)

    def order(i):
        @pl.when(jnp.equal(i == 0, cells_first))
        def _():
            make_cells()

        @pl.when(jnp.not_equal(i == 0, cells_first))
        def _():
            meet()

    run(0, 2, order)

    @pl.when(jnp.logical_not(cells_first))
    def _():
        run(0, wide, send_cells)

    gpos, gmass = gal_in[0], masses[0]

    both = jnp.concatenate([pos4, vel4], axis=0)
    targets = jnp.transpose(
        jnp.concatenate([both, jnp.zeros((ROWS, LANES - stars), jnp.float32)], axis=1)
    )
    zero = jnp.zeros((ROWS, LANES), jnp.float32)

    own = [spread(cell_own[c : c + 1, :]) for c in range(4)]
    star_groups = stars // ROWS
    for t in range(star_groups):
        rows = targets[t * ROWS : (t + 1) * ROWS, :]
        place = [column(rows, c) for c in range(3)]
        for c in range(3):
            aims[t, c] = place[c]
            aims[t, 3 + c] = column(rows, 4 + c)
            star_sum[t, 3 + c] = zero
        for c, value in enumerate(pull(own[:3], own[3], place, (zero,) * 3)):
            star_sum[t, c] = value

    last4 = lax.broadcasted_iota(jnp.int32, (4, bodies), 0) == 3
    high, mid, low = split(jnp.concatenate([-2.0 * gpos, jnp.zeros_like(gmass)], axis=0))
    high = jnp.where(last4, 1.0, high)
    reach = split(norm(gpos) + soften_sq)
    blank = jnp.zeros_like(gmass)
    aimed[...] = jnp.concatenate(
        [high, mid, high, low, high, mid, *reach, blank, blank, blank, blank, blank],
        axis=0,
    ).astype(jnp.bfloat16)

    def on_bodies(rows, total):
        square = norm(rows[0:3])
        high, mid, low = split(jnp.concatenate([rows[0:3], square], axis=0))
        ones = jnp.ones(rows.shape, jnp.float32)
        turned = jnp.transpose(
            jnp.concatenate([high, high, mid, high, low, mid, ones, rows], axis=0)
        )
        reach = jnp.dot(
            turned.astype(jnp.bfloat16), aimed[...], preferred_element_type=jnp.float32
        )
        total = [list(part) for part in total]
        for g in range(rows.shape[1] // ROWS):
            some = turned[g * ROWS : (g + 1) * ROWS, :]
            place = [column(some, 28 + c) for c in range(3)]
            mass = column(some, 31)
            for t in every:
                inverse = lax.rsqrt(
                    reach[g * ROWS : (g + 1) * ROWS, t * LANES : (t + 1) * LANES]
                )
                weight = mass * inverse * (inverse * inverse)
                for c in range(3):
                    total[t][c] = total[t][c] + place[c] * weight
                total[t][3] = total[t][3] + weight
        return total

    def keep(total):
        for t in every:
            for c in range(4):
                body_sum[4 * t + c] = total[t][c]

    def kept():
        return [[body_sum[4 * t + c] for c in range(4)] for t in every]

    def cells_on_stars(rows, t):
        place = [aims[t, c] for c in range(3)]
        return pull(rows[:3], rows[3], place, [star_sum[t, c] for c in range(3)])

    total = [[zero] * 4 for _ in every]
    for t in every:
        tile = slice(t * LANES, (t + 1) * LANES)
        total = on_bodies(jnp.concatenate([gpos[:, tile], gmass[:, tile]], axis=0), total)
    keep(total)

    def larger(w):
        rest = jnp.where(w == wide, n_narrow - 1 - narrow, 0)
        return jnp.where(w > wide, n_narrow, rest)

    def answer(q):
        count = larger(2 * q) + larger(2 * q + 1)

        @pl.when(count > 0)
        def _():
            pl.semaphore_wait(enter_sem.at[q], count)

        def to_group(w):
            @pl.when(w == wide)
            def _():
                run(narrow + 1, n_narrow, send_beside)

            @pl.when(w > wide)
            def _():
                answer_group(w)
                send_cells(w)

        run(2 * q, 2 * q + 2, to_group)

    halves = n_wide // 2
    lower = wide < n_wide // 4


    def gather(n, even):
        even_block, odd_block = states[n * n_wide + even], states[n * n_wide + even + 1]
        rows = jnp.where(left, even_block, odd_block)
        speeds = pltpu.roll(jnp.where(left, odd_block, even_block), stars, 1)
        return rows, speeds

    def near_arrived(q):
        own = wide // 2 == q

        def wait(count):
            some = states.at[pl.ds(0, count)]
            pltpu.make_async_copy(some, some, near_sem.at[q]).wait()

        @pl.when(own)
        def _():
            wait(2)

        @pl.when(jnp.logical_not(own))
        def _():
            wait(4)

    def near_stars(even):
        near, _ = gather(narrow, even)
        if kicks == n_wide:
            return [near]
        padded = jnp.concatenate([near, jnp.zeros((4, LANES), jnp.float32)], axis=0)
        cols[pl.ds(pl.multiple_of(even * stars, LANES), LANES), :] = jnp.transpose(padded)
        return []

    def near_cells(e):
        cells = cell_in[e * slots]
        for k in range(1, slots):
            cells = cells + cell_in[e * slots + k]
        rows = [spread(cells[c : c + 1]) for c in range(4)]
        for t in range(star_groups):
            for c, value in enumerate(cells_on_stars(rows, t)):
                star_sum[t, c] = value
        return [cells]

    def rest_arrived(q):
        some = states.at[pl.ds(0, 2 * (n_narrow - 1))]
        pltpu.make_async_copy(some, some, pass_sem.at[q]).wait()

    def all_stars(even, take):
        for n in range(n_narrow):
            rows, speeds = gather(n, even)
            srow[n, 0:4, :] = rows
            srow[n, 4:8, :] = speeds
        sources = [
            [spread(srow[n, c : c + 1, :]) for c in range(7)] for n in range(n_narrow)
        ]
        for t in range(star_groups):
            place = [aims[t, c] for c in range(3)]
            speed = [aims[t, 3 + c] for c in range(3)]
            acc = [star_sum[t, c] for c in range(6)]
            for rows in sources:
                dx, dy, dz = (rows[c] - place[c] for c in range(3))
                ux, uy, uz = (rows[4 + c] - speed[c] for c in range(3))
                inverse = lax.rsqrt(dx * dx + dy * dy + dz * dz + soften_sq)
                square = inverse * inverse
                weight = rows[3] * inverse * square
                approach = 3.0 * (dx * ux + dy * uy + dz * uz) * square
                acc = [
                    acc[0] + dx * weight,
                    acc[1] + dy * weight,
                    acc[2] + dz * weight,
                    acc[3] + (ux - dx * approach) * weight,
                    acc[4] + (uy - dy * approach) * weight,
                    acc[5] + (uz - dz * approach) * weight,
                ]
            take(t, acc)

    def store(t, acc):
        for c in range(6):
            star_sum[t, c] = acc[c]

    pairs_per_row = slots // 2

    def nearby(q):
        near = near_stars(2 * q) + near_cells(q // pairs_per_row)
        return on_bodies(jnp.concatenate(near, axis=1), kept())

    first = wide < n_wide // 8

    def turn(p):
        run(
            jnp.where(p == 0, wide // 2, jnp.where(jnp.logical_and(first, p == 1), 2, halves)),
            jnp.where(jnp.logical_and(first, p == 0), 2, halves),
            answer,
        )
        q = jnp.where(lower, p, halves - 1 - p)
        near_arrived(q)
        second = lax.rem(p, pairs_per_row) == pairs_per_row - 1

        @pl.when(second)
        def _():
            keep(nearby(q))
            rest_arrived(q)
            all_stars(2 * q, store)

        @pl.when(jnp.logical_not(second))
        def _():
            rest_arrived(q)
            for rows in near_stars(2 * q):
                keep(on_bodies(rows, kept()))
            all_stars(2 * q, store)

    run(0, halves - 1, turn)

    last = jnp.where(lower, halves - 1, 0)
    near_arrived(last)
    total = nearby(last)
    for t in every:
        tile = slice(t * LANES, (t + 1) * LANES)
        near = [gpos[c : c + 1, tile] for c in range(3)]
        pieces = [jnp.sum(part, axis=0, keepdims=True) for part in total[t]]
        pieces = [pieces[c] - near[c] * pieces[3] for c in range(3)]
        if kicks != n_wide:
            here = [spread(row) for row in near]

            def kick(k, acc):
                listed = star_leaf[t * leaves // tiles, k]

                def some(g, acc):
                    at = pl.multiple_of(listed * stars + g * ROWS, ROWS)
                    source = cols[pl.ds(at, ROWS), :]
                    place = [column(source, c) for c in range(3)]
                    return pull(place, column(source, 3), here, acc)

                return loop(stars // ROWS, some, acc)

            kicked = lax.fori_loop(0, kicks, kick, (zero,) * 3)
            for c in range(3):
                pieces[c] = pieces[c] + jnp.sum(kicked[c], axis=0, keepdims=True)
        for c in range(3):
            out[c : c + 1, tile] = gal_in[1, c : c + 1, tile] + time_step * pieces[c]

    pieces = []

    def finish(t, acc):
        piece = jnp.zeros((ROWS, LANES), jnp.float32)
        for c in range(6):
            piece = jnp.where(lane8 == c, jnp.sum(acc[c], axis=1, keepdims=True), piece)
        pieces.append(piece)

    sent = states.at[pl.ds(0, n_wide * (n_narrow + 1) - 2)]
    pltpu.make_async_copy(sent, sent, send_sem).wait()
    rest_arrived(last)
    all_stars(2 * last, finish)
    result = jnp.transpose(jnp.concatenate(pieces, axis=0))
    new_acc, new_jerk = result[0:3], result[3:6]
    vel_new = (
        svel + time_step * 0.5 * (sacc + new_acc) + step_sq / 12.0 * (sjerk - new_jerk)
    )
    vel_at = bodies + LANES
    out[:, vel_at : vel_at + stars] = vel_new
    out[:, bodies : bodies + stars] = (
        spos + time_step * 0.5 * (svel + vel_new) + step_sq / 12.0 * (sacc - new_acc)
    )


def unpack(packed, gal_out, pos_out, vel_out):
    bodies, stars = gal_out.shape[1], pos_out.shape[1]
    gal_out[...] = packed[:, 0:bodies]
    pos_out[...] = packed[:, bodies : bodies + stars]
    vel_out[...] = packed[:, bodies + LANES : bodies + LANES + stars]


def body(
    n_wide,
    n_narrow,
    star_pos,
    star_vel,
    star_mass,
    star_acc,
    star_jerk,
    gal_pos,
    gal_vel,
    gal_mass,
    group_of,
    let_send,
    star_leaf,
):
    stars, bodies = star_pos.shape[1], gal_pos.shape[1]
    vmem = pl.BlockSpec(memory_space=pltpu.VMEM)
    f32 = jnp.float32
    i32 = jnp.int32
    hbm = pl.BlockSpec(memory_space=pltpu.HBM)
    packed = pl.pallas_call(
        functools.partial(kernel, n_wide, n_narrow),
        out_shape=jax.ShapeDtypeStruct((3, bodies + 2 * LANES), f32),
        in_specs=[hbm] * 11,
        out_specs=vmem,
        scratch_shapes=[
            pltpu.VMEM((4, 3, stars), f32),
            pltpu.VMEM((1, stars), f32),
            pltpu.VMEM((13, 1, stars), f32),
            pltpu.VMEM((2, 3, bodies), f32),
            pltpu.VMEM((2, 1, bodies), f32),
            pltpu.VMEM((1, bodies), i32),
            pltpu.VMEM((1, n_wide), i32),
            pltpu.SMEM(star_leaf.shape, i32),
            pltpu.SemaphoreType.DMA((4 + (star_leaf.shape[1] != n_wide),)),
            pltpu.VMEM(((n_narrow + 1) * n_wide, 4, LANES), f32),
            pltpu.VMEM((ROWS, LANES), f32),
            pltpu.VMEM((n_wide, 4, LANES), f32),
            pltpu.VMEM((n_wide, 4, LANES), f32),
            pltpu.VMEM((32, bodies), jnp.bfloat16),
            pltpu.VMEM((n_wide * stars, ROWS), f32),
            pltpu.VMEM((n_narrow, ROWS, LANES), f32),
            pltpu.VMEM((stars // ROWS, 6, ROWS, LANES), f32),
            pltpu.VMEM((4 * bodies // LANES, ROWS, LANES), f32),
            pltpu.VMEM((stars // ROWS, 6, ROWS, LANES), f32),
            pltpu.SemaphoreType.DMA,
            pltpu.SemaphoreType.DMA((n_wide // 2,)),
            pltpu.SemaphoreType.DMA((n_wide // 2,)),
            pltpu.SemaphoreType.REGULAR((n_wide // 2,)),
        ],
        compiler_params=pltpu.CompilerParams(
            collective_id=0, has_side_effects=True, vmem_limit_bytes=24 << 20
        ),
    )(
        *(
            pltpu.with_memory_space_constraint(array, pltpu.HBM)
            for array in (
                star_pos,
                star_vel,
                star_mass.reshape(1, stars),
                star_acc,
                star_jerk,
                gal_pos,
                gal_vel,
                gal_mass.reshape(1, bodies),
                group_of.reshape(1, bodies),
                let_send.reshape(1, n_wide),
                star_leaf,
            )
        )
    )
    return pl.pallas_call(
        unpack,
        out_shape=(
            jax.ShapeDtypeStruct(gal_vel.shape, f32),
            jax.ShapeDtypeStruct(star_pos.shape, f32),
            jax.ShapeDtypeStruct(star_vel.shape, f32),
        ),
        in_specs=[vmem],
        out_specs=(vmem,) * 3,
        compiler_params=pltpu.CompilerParams(vmem_limit_bytes=1 << 20),
    )(packed)


def solution(mesh):
    both = ("wide", "narrow")
    columns, flat = P(None, both), P(both)
    return jax.shard_map(
        functools.partial(body, mesh.shape["wide"], mesh.shape["narrow"]),
        mesh=mesh,
        in_specs=(
            columns,
            columns,
            flat,
            columns,
            columns,
            columns,
            columns,
            flat,
            flat,
            P(both, None, None),
            P(both, None),
        ),
        out_specs=(columns, columns, columns),
        check_vma=False,
    )
```
